32 devices in a mesh: dp: 4 (over z), expert: 8 (over y, x, core).
Axes of the slice: x: 2, y: 2, z: 4, core: 2. Of those that a mesh axis runs over, the one named last changes fastest.
Arguments:
- tokens: bfloat16 [8192, 768], P(('dp', 'expert')), may hold values from -6 to 6
- segment_ids: int32 [32, 256], P(('dp', 'expert')), may hold values from 0 to 2, never falling along the last dimension, each value on 1 to 204 neighbouring positions
- routes: int32 [8192, 2], P(('dp', 'expert')), may hold values from 0 to 15, all different within a row
- ln1_gain: float32 [768], P('dp'), may hold values from 0.5 to 1.5
- ln1_bias: float32 [768], P('dp'), may hold values from -0.6 to 0.6
- ln2_gain: float32 [768], P('dp'), may hold values from 0.5 to 1.5
- ln2_bias: float32 [768], P('dp'), may hold values from -0.6 to 0.6
- w_query: float32 [768, 768], P('dp'), may hold values from -0.3125 to 0.3125
- w_key: float32 [768, 768], P('dp'), may hold values from -0.3125 to 0.3125
- w_value: float32 [768, 768], P('dp'), may hold values from -0.21875 to 0.21875
- w_output: float32 [768, 768], P('dp'), may hold values from -0.875 to 0.875
- w_router: float32 [768, 16], P('dp'), may hold values from -0.15625 to 0.15625
- frozen_in: float32 [8, 768, 3072], P('expert', 'dp'), may hold values from -0.21875 to 0.21875
- frozen_out: float32 [8, 3072, 768], P('expert', 'dp'), may hold values from -0.1875 to 0.1875
- new_in: float32 [8, 768, 3072], P('expert', 'dp'), may hold values from -0.21875 to 0.21875
- new_out: float32 [8, 3072, 768], P('expert', 'dp'), may hold values from -0.1875 to 0.1875
- cotangent: bfloat16 [8192, 768], P(('dp', 'expert')), may hold values from -6 to 6
Outputs:
- block_out: bfloat16 [8192, 768], P(('dp', 'expert'))
- grad_tokens: bfloat16 [8192, 768], P(('dp', 'expert'))
- grad_w_query: float32 [768, 768], P('dp')
- grad_w_key: float32 [768, 768], P('dp')
- grad_w_value: float32 [768, 768], P('dp')
- grad_w_output: float32 [768, 768], P('dp')
- grad_w_router: float32 [768, 16], P('dp')
- grad_ln1_gain: float32 [768], P('dp')
- grad_ln1_bias: float32 [768], P('dp')
- grad_ln2_gain: float32 [768], P('dp')
- grad_ln2_bias: float32 [768], P('dp')
- grad_new_in: float32 [8, 768, 3072], P('expert', 'dp')
- grad_new_out: float32 [8, 3072, 768], P('expert', 'dp')
The draws below stay inside these ranges and needn't reach their ends.
Inputs may be any that keep to these rules, and one draw needn't show every extreme that they name: `segment_ids`: within each row ids never fall, every sequence has 1 to 204 tokens, and one has exactly 204. `routes`: the two experts of a token differ.
All inputs are finite; a program needn't handle non-finite values.
Results may differ from the reference program's by a relative error of at most 0.014.
The reference program's roundings to bfloat16 on the way count: a program that leaves them out, or rounds other values in their place, can miss the bound.
Values may be sent and summed in bfloat16 or wider, within the bound.
A program may use at most 192 MiB of HBM per device.

```python
import math
import jax
import jax.numpy as jnp
import numpy as np
from jax import lax

D = 768
HEADS = 12
HEAD = 64
FF = 3072
TOK_DEV = 256
SEQ_DEV = 3
MAXLEN = 204
TOKENS = 8192
NEW_EXPERTS = 8
EXPERTS = 16
CAP = 40
DEVICES = 32


def shard_levels(rng, shape, split, least, largest):
    level = 1.0
    for dim, shards_of in split:
        draws = jax.random.uniform(jax.random.fold_in(jax.random.fold_in(rng, 6), dim), (shards_of,), jnp.float32, least / len(split), largest / len(split))
        level = level * jnp.repeat(jnp.exp(draws), shape[dim] // shards_of).reshape((-1,) + (1,) * (len(shape) - 1 - dim))
    return level


def picks_of(key, rows, amount, top, lift):
    order = jax.random.permutation(jax.random.fold_in(key, 1), amount)
    favour = order
    for power in range(3):
        favour = favour * favour // amount
    favour = favour * lift // amount
    chance = jax.random.randint(jax.random.fold_in(key, 2), (rows, amount), 0, 4096) + favour
    fixed_rows = jax.random.permutation(jax.random.fold_in(key, 3), rows)[jnp.arange(amount) % rows]
    chance = jnp.where(jnp.arange(rows)[:, None] == fixed_rows[None, :], 1 << 14, chance)
    score = chance * amount + jnp.arange(amount)
    return lax.top_k(score.astype(jnp.int32), top)[1].astype(jnp.int32)


def length_profile(count, total, most, lean):
    loads = [(1 << 20) // math.isqrt(standing ** lean) + 1 for standing in range(2, count + 1)]
    rest, holding = total - most - (count - 1), [1] * (count - 1)
    while rest > 0:
        movable = [i for i in range(count - 1) if holding[i] < most]
        pool, remaining = sum([loads[i] for i in movable]), rest
        for i in movable:
            addition = min(most - holding[i], max(1, remaining * loads[i] // pool), rest)
            holding[i] = holding[i] + addition
            rest = rest - addition
    return np.array([most] + holding)


def uneven(rng, number_of, total, most, lean):
    if number_of == 2:
        one = jax.random.randint(rng, (), max(1, total - most), min(most, total - 1) + 1)
        return jnp.stack([one, total - one])
    tallies = jnp.asarray(length_profile(number_of, total, most, lean), jnp.int32)
    pairs = (number_of - 1) // 2
    giver, receiver = tallies[1:1 + 2 * pairs:2], tallies[2:2 + 2 * pairs:2]
    margin = jnp.minimum(giver - 1, most - receiver)
    passed = jax.random.randint(jax.random.fold_in(rng, 1), (pairs,), 0, 1 << 20) % (margin + 1)
    tallies = tallies.at[1:1 + 2 * pairs:2].set(giver - passed).at[2:2 + 2 * pairs:2].set(receiver + passed)
    return tallies[jax.random.permutation(jax.random.fold_in(rng, 2), number_of)]


def noise(key, shape, scale, bound, pieces=(), kind=jnp.bfloat16):
    entries = scale * jax.random.normal(key, shape, jnp.float32)
    if pieces:
        entries = entries * shard_levels(key, shape, pieces, -0.22, 0.18)
    return jnp.clip(entries, -bound, bound).astype(kind)


def setup_inputs(seed: int = 0) -> dict:
    seeds = jax.random.split(jax.random.key(seed), 18)
    tokens = noise(seeds[0], (TOKENS, D), 1.0, 6.0, ((0, 32),))
    segment_ids = jax.vmap(lambda own: jnp.searchsorted(jnp.cumsum(uneven(own, SEQ_DEV, TOK_DEV, MAXLEN, 2)), jnp.arange(TOK_DEV), side="right"))(jax.random.split(seeds[1], DEVICES)).reshape((DEVICES, TOK_DEV)).astype(jnp.int32)
    routes = picks_of(seeds[2], TOKENS, EXPERTS, 2, 2048)
    ln1_gain = jnp.clip(1.0 + 0.1 * jax.random.normal(seeds[3], (D,), jnp.float32), 0.5, 1.5)
    ln1_bias = noise(seeds[4], (D,), 0.1, 0.6, ((0, 4),), jnp.float32)
    ln2_gain = jnp.clip(1.0 + 0.1 * jax.random.normal(seeds[5], (D,), jnp.float32), 0.5, 1.5)
    ln2_bias = noise(seeds[6], (D,), 0.1, 0.6, ((0, 4),), jnp.float32)
    w_query = noise(seeds[7], (D, D), (D * 4 // 9) ** -0.5, 0.3125, ((0, 4),), jnp.float32)
    w_key = noise(seeds[8], (D, D), (D * 4 // 9) ** -0.5, 0.3125, ((0, 4),), jnp.float32)
    w_value = noise(seeds[9], (D, D), D ** -0.5, 0.21875, ((0, 4),), jnp.float32)
    w_output = noise(seeds[10], (D, D), (D // 16) ** -0.5, 0.875, ((0, 4),), jnp.float32)
    w_router = noise(seeds[11], (D, EXPERTS), (D * 16 // 9) ** -0.5, 0.15625, ((0, 4),), jnp.float32)
    frozen_in = noise(seeds[12], (NEW_EXPERTS, D, FF), D ** -0.5, 0.21875, ((0, 8), (1, 4)), jnp.float32)
    frozen_out = noise(seeds[13], (NEW_EXPERTS, FF, D), (FF // 3) ** -0.5, 0.1875, ((0, 8), (1, 4)), jnp.float32)
    new_in = noise(seeds[14], (NEW_EXPERTS, D, FF), D ** -0.5, 0.21875, ((0, 8), (1, 4)), jnp.float32)
    new_out = noise(seeds[15], (NEW_EXPERTS, FF, D), (FF // 3) ** -0.5, 0.1875, ((0, 8), (1, 4)), jnp.float32)
    cotangent = noise(seeds[16], (TOKENS, D), 1.0, 6.0, ((0, 32),))
    return {"tokens": tokens, "segment_ids": segment_ids, "routes": routes, "ln1_gain": ln1_gain, "ln1_bias": ln1_bias, "ln2_gain": ln2_gain, "ln2_bias": ln2_bias, "w_query": w_query, "w_key": w_key, "w_value": w_value, "w_output": w_output, "w_router": w_router, "frozen_in": frozen_in, "frozen_out": frozen_out, "new_in": new_in, "new_out": new_out, "cotangent": cotangent}


@jax.custom_vjp
def low(v):
    return lax.optimization_barrier(v.astype(jnp.bfloat16)).astype(jnp.float32)

@jax.custom_vjp
def low_back(v):
    return v

def low_keep(v):
    return (low(v), None)

def low_pass(kept, grad):
    return (grad,)

def back_keep(v):
    return (v, None)

def back_low(kept, grad):
    return (low(grad),)
low.defvjp(low_keep, low_pass)
low_back.defvjp(back_keep, back_low)
HIGHEST = lax.Precision.HIGHEST
NORM_EPS = 1e-05
MASKED = -1e+30

def layer_norm(values, norm_gain, norm_shift):
    average = lax.optimization_barrier(jnp.mean(values, axis=-1, keepdims=True))
    centred = values - average
    variance = lax.optimization_barrier(jnp.mean(centred * centred, axis=-1, keepdims=True))
    return centred * lax.rsqrt(variance + NORM_EPS) * norm_gain + norm_shift

def block_front(rows, segments, params):
    gain_one, bias_one, gain_two, bias_two, query_weight, key_weight, value_weight, output_weight, router_weight = params
    row_count = rows.shape[0]
    normed = low(layer_norm(rows, gain_one, bias_one))
    query_rows = low_back(low(jnp.dot(normed, query_weight, precision=HIGHEST))).reshape(row_count, HEADS, HEAD)
    key_rows = low_back(low(jnp.dot(normed, key_weight, precision=HIGHEST))).reshape(row_count, HEADS, HEAD)
    value_rows = low_back(low(jnp.dot(normed, value_weight, precision=HIGHEST))).reshape(row_count, HEADS, HEAD)
    scores = low_back(jnp.einsum('qhd,khd->hqk', query_rows, key_rows, precision=HIGHEST) * HEAD ** (-0.5))
    positions = jnp.arange(row_count, dtype=jnp.int32)
    allowed = (segments[:, None] == segments[None, :]) & (positions[None, :] <= positions[:, None])
    scores = jnp.where(allowed[None], scores, MASKED)
    probabilities = low(jax.nn.softmax(scores, axis=-1))
    attended = jnp.einsum('hqk,khd->qhd', probabilities, value_rows, precision=HIGHEST).reshape(row_count, HEADS * HEAD)
    attended = low_back(low(attended))
    residual = rows + low_back(jnp.dot(attended, output_weight, precision=HIGHEST))
    normed_two = low(layer_norm(residual, gain_two, bias_two))
    logits = low_back(jnp.dot(normed_two, router_weight, precision=HIGHEST))
    return (residual, normed_two, logits)

def reference(tokens, segment_ids, routes, ln1_gain, ln1_bias, ln2_gain, ln2_bias, w_query, w_key, w_value, w_output, w_router, frozen_in, frozen_out, new_in, new_out, cotangent):
    device_count = segment_ids.shape[0]
    row_count = segment_ids.shape[1]
    pair_ids = routes.reshape(device_count, 2 * row_count)
    onehot = (pair_ids[:, :, None] == jnp.arange(EXPERTS, dtype=jnp.int32)[None, None, :]).astype(jnp.int32)
    running = jnp.cumsum(onehot, axis=1)
    position = lax.optimization_barrier(jnp.sum(onehot * running, axis=2)) - 1
    is_kept = position < CAP
    slot_index = jnp.where(is_kept, pair_ids * CAP + position, EXPERTS * CAP).astype(jnp.int32)
    device_rows = jnp.broadcast_to(jnp.arange(device_count, dtype=jnp.int32)[:, None], slot_index.shape)
    token_flat = device_rows * row_count + jnp.arange(2 * row_count, dtype=jnp.int32)[None, :] // 2
    table = jnp.full((device_count, EXPERTS * CAP + 1), device_count * row_count, jnp.int32)
    table = table.at[device_rows, slot_index].set(token_flat)
    table = table[:, :EXPERTS * CAP].reshape(device_count, EXPERTS, CAP).transpose(1, 0, 2).reshape(EXPERTS, device_count * CAP)
    gather_index = jnp.where(is_kept, (pair_ids * device_count + device_rows) * CAP + position, 0).astype(jnp.int32)
    kept_float = is_kept.astype(jnp.float32)
    route_blocks = routes.reshape(device_count, row_count, 2)

    def forward(rows, gain_one, bias_one, gain_two, bias_two, query_weight, key_weight, value_weight, output_weight, router_weight, train_in, train_out):
        params = (low(gain_one), low(bias_one), low(gain_two), low(bias_two), low(query_weight), low(key_weight), low(value_weight), low(output_weight), low(router_weight))
        row_blocks = rows.reshape(device_count, row_count, D)

        def front_one(member):
            return block_front(member[0], member[1], params)
        residual, normed_two, logits = lax.map(jax.checkpoint(front_one), (row_blocks, segment_ids))
        picked = jnp.take_along_axis(logits, route_blocks, axis=2)
        gate_values = jax.nn.softmax(picked, axis=-1).reshape(device_count, 2 * row_count)
        normed_pad = jnp.concatenate([normed_two.reshape(device_count * row_count, D), jnp.zeros((1, D), jnp.float32)], axis=0)
        weights_in = jnp.concatenate([low(frozen_in), low(train_in)], axis=0)
        weights_out = jnp.concatenate([low(frozen_out), low(train_out)], axis=0)

        def expert_run(member):
            token_index, weight_in, weight_out = member
            expert_rows = low_back(normed_pad[token_index])
            pre_act = low_back(jnp.dot(expert_rows, weight_in, precision=HIGHEST))
            hidden = low(jax.nn.gelu(pre_act))
            return low_back(low(jnp.dot(hidden, weight_out, precision=HIGHEST)))
        expert_out = lax.map(jax.checkpoint(expert_run), (table, weights_in, weights_out))
        flat_out = expert_out.reshape(EXPERTS * device_count * CAP, D)
        pair_out = flat_out[gather_index]
        weighted = pair_out * (gate_values * kept_float)[:, :, None]
        mixture = lax.optimization_barrier(jnp.sum(weighted.reshape(device_count, row_count, 2, D), axis=2))
        return (residual + mixture).reshape(device_count * row_count, D)
    output, pullback = jax.vjp(forward, tokens.astype(jnp.float32), ln1_gain, ln1_bias, ln2_gain, ln2_bias, w_query, w_key, w_value, w_output, w_router, new_in, new_out)
    grads = pullback(cotangent.astype(jnp.float32))
    return (output.astype(jnp.bfloat16), grads[0].astype(jnp.bfloat16), grads[5], grads[6], grads[7], grads[8], grads[9], grads[1], grads[2], grads[3], grads[4], grads[10], grads[11])
```

```python
import functools

import jax
import jax.numpy as jnp
from jax import lax
from jax.experimental import pallas as pl
from jax.experimental.pallas import tpu as pltpu
from jax.sharding import PartitionSpec as P

HEADS = 12
HEAD = 64
NORM_EPS = 1e-05
MASKED = -1e30
MESH = pl.DeviceIdType.MESH
BF = jnp.bfloat16
F32 = jnp.float32
VMEM_LIMIT = 60 * 1024 * 1024


class Place:
    def __init__(self, planes, experts):
        self.planes, self.experts = planes, experts
        self.z = lax.axis_index("dp")
        self.i = lax.axis_index("expert")
        self.core = lax.rem(self.i, 2)
        self.chip = lax.div(self.i, 2)
        self.xb = lax.rem(self.chip, 2)
        self.yb = lax.rem(lax.div(self.i, 4), 2)
        self.sib = self.i + 1 - 2 * self.core
        self.xn = self.i + 2 - 4 * self.xb
        self.yn = self.i + 4 - 8 * self.yb
        self.chips = planes * (experts // 2)
        self.me = self.z * (experts // 2) + self.chip


def send_to(src, dst, send_sem, recv_sem, z, i):
    return pltpu.make_async_remote_copy(
        src_ref=src,
        dst_ref=dst,
        send_sem=send_sem,
        recv_sem=recv_sem,
        device_id={"dp": z, "expert": i},
        device_id_type=MESH,
    )


def greet(at):
    barrier = pltpu.get_barrier_semaphore()
    count = at.planes * at.experts
    own = at.z * at.experts + at.i

    def signal(step, carry):
        target = lax.rem(own + step, count)
        pl.semaphore_signal(
            barrier,
            inc=1,
            device_id={"dp": lax.div(target, at.experts), "expert": lax.rem(target, at.experts)},
            device_id_type=MESH,
        )
        return carry

    lax.fori_loop(1, count, signal, 0)
    return lambda: pl.semaphore_wait(barrier, count - 1)


def any_spec():
    return pl.BlockSpec(memory_space=pl.ANY)


def vmem_spec():
    return pl.BlockSpec(memory_space=pltpu.VMEM)


NN = ((1,), (0,))
NT = ((1,), (1,))
TN = ((0,), (0,))


def dot(left, right, contract, out=F32):
    return lax.dot_general(
        left, right, ((contract[0], contract[1]), ((), ())), preferred_element_type=F32
    ).astype(out)


def exact_dot(left, right, contract):
    return lax.dot_general(
        left, right, ((contract[0], contract[1]), ((), ())),
        preferred_element_type=F32, precision=lax.Precision.HIGHEST,
    )


def norm_parts(rows):
    centred = rows - jnp.mean(rows, axis=-1, keepdims=True)
    variance = jnp.mean(centred * centred, axis=-1, keepdims=True)
    scale = lax.rsqrt(variance + NORM_EPS)
    return centred * scale, scale


def norm_back(rows, gain, grad):
    unit, scale = norm_parts(rows)
    scaled = grad * gain
    inner = scaled - jnp.mean(scaled, axis=-1, keepdims=True)
    inner = inner - unit * jnp.mean(scaled * unit, axis=-1, keepdims=True)
    return scale * inner, jnp.sum(grad * unit, axis=0, keepdims=True), jnp.sum(grad, axis=0, keepdims=True)


def slot_places(slot, slots):
    lanes = lax.broadcasted_iota(jnp.int32, (slot[0].shape[0], slots), 1).astype(F32)
    return [(lanes == one).astype(F32).astype(BF) for one in slot]


def slot_values(aux, table, padded, chips):
    rows = aux.shape[0]
    low = lax.broadcasted_iota(jnp.int32, (rows, chips), 1).astype(F32) * padded
    lanes = lax.broadcasted_iota(jnp.int32, (rows, table.shape[1]), 1).astype(F32)
    found = []
    for k in range(2):
        slot = aux[:, 2 + k:3 + k]
        mine = jnp.logical_and(slot >= low, slot < low + padded).astype(F32)
        position = slot - jnp.sum(mine * low, axis=1, keepdims=True)
        picked = exact_dot(mine, table, NN)
        found.append(jnp.sum(jnp.where(lanes == position, picked, 0.0), axis=1, keepdims=True))
    return found


def front_kernel(planes, experts, capacity, padded, nrouter,
                 tokens, cot, segs, routes, router, g1, b1, g2, b2, wq, wk, wv, wo, fi, fo, ni, no,
                 wd, pk, win, wout, act_one, act_two, q, k, v, att, resid, probs, aux, ga,
                 xland, dland, gland,
                 packs, allow, xsend, esend, gsend, dstage, istage, ostage, ibf, obf,
                 ld, zs, zr, ps, pr, gs, gr, es, er, fs, fr, ts, tr, tl, sa, ra):
    at = Place(planes, experts)
    z, i, core = at.z, at.i, at.core
    rows, width = tokens.shape
    chips = at.chips
    per_plane = experts // 2
    share = dstage.shape[1]
    quarter = share // 4
    half = width // 2
    fhalf = istage.shape[2] // 2
    oshare = ostage.shape[1]
    ohalf = oshare // 2
    pairs = width // 128
    spot = lax.rem(i, 8)
    base = i - spot
    loads = [pltpu.make_async_copy(w, dstage.at[m], ld.at[m]) for m, w in enumerate((wq, wk, wv, wo))]
    loads += [
        pltpu.make_async_copy(fi.at[0], istage.at[0], ld.at[4]),
        pltpu.make_async_copy(ni.at[0], istage.at[1], ld.at[5]),
        pltpu.make_async_copy(fo.at[0], ostage.at[0], ld.at[6]),
        pltpu.make_async_copy(no.at[0], ostage.at[1], ld.at[7]),
    ]
    for load in loads:
        load.start()
    met = greet(at)
    zrow = pl.multiple_of(z * share, share)
    for m in range(4):
        loads[m].wait()
        wd[m, pl.ds(zrow, share), :] = dstage[m].astype(BF)
    packs[z, 0:nrouter, :] = router[...].astype(BF)
    norm_row = lax.broadcasted_iota(jnp.int32, (16, share), 0)
    norms = jnp.zeros((16, share), F32)
    for n, values in enumerate((g1, b1, g2, b2)):
        norms = jnp.where(norm_row == n, values[...], norms)
    packs[z, nrouter:nrouter + 16, :] = norms.astype(BF)
    met()

    def block(plane, row_quarter, column_half):
        return wd.at[
            :,
            pl.ds(pl.multiple_of(plane * share + row_quarter * quarter, 16), quarter),
            pl.ds(pl.multiple_of(column_half * half, 128), half),
        ]

    rq = 2 * at.yb + core
    rqy = 2 * (1 - at.yb) + core
    rqs = 2 * at.yb + 1 - core
    rqys = 2 * (1 - at.yb) + 1 - core
    xb, xo = at.xb, 1 - at.xb
    started = []
    for j in range(1, planes):
        zt = lax.rem(z + j, planes)
        mine = block(z, rq, xb)
        copy = send_to(mine, mine, zs.at[j - 1], zr.at[j - 1], zt, i)
        copy.start()
        started.append(copy)
        copy = send_to(packs.at[z], packs.at[z], ps.at[j - 1], pr.at[j - 1], zt, i)
        copy.start()
        started.append(copy)

    def cast(source, target, kind, chunk):
        def step(n, carry):
            part = pl.ds(pl.multiple_of(n * chunk, chunk), chunk)
            target[kind, part, :] = source[kind, part, :].astype(BF)
            return carry

        lax.fori_loop(0, source.shape[1] // chunk, step, 0)

    def in_block(plane, h):
        return win.at[
            pl.ds(pl.multiple_of(plane * share, 16), share),
            pl.ds(pl.multiple_of(h * fhalf, 128), fhalf),
        ]

    def out_block(plane, h):
        return wout.at[pl.ds(pl.multiple_of(plane * oshare + h * ohalf, 16), ohalf), :]

    remote_sends = []

    def ship(kind, h, which):
        zh = 3 * core if kind == 0 else 1 + core
        remote = jnp.logical_or(zh != z, core != h)
        src = (
            ibf.at[kind, :, pl.ds(h * fhalf, fhalf)]
            if which == 0
            else obf.at[kind, pl.ds(h * ohalf, ohalf), :]
        )
        dst = in_block(z, h) if which == 0 else out_block(z, h)
        far = send_to(src, dst, es.at[kind, h, which], er.at[z, which], zh, 2 * at.chip + h)
        near = pltpu.make_async_copy(src, dst, er.at[z, which])
        pl.when(remote)(far.start)
        pl.when(jnp.logical_not(remote))(near.start)
        remote_sends.append((remote, far))

    for n, kind in ((4, 0), (5, 1)):
        loads[n].wait()
        cast(istage, ibf, kind, 16)
        for h in range(2):
            ship(kind, h, 0)

    shift = experts.bit_length() - 1
    above = lax.broadcasted_iota(jnp.int32, (rows, rows), 0)
    across = lax.broadcasted_iota(jnp.int32, (rows, rows), 1)
    segment = segs[...].astype(F32)
    fact_row = lax.broadcasted_iota(jnp.int32, (8, rows), 0)
    facts = jnp.zeros((8, rows), F32)
    for n, values in enumerate((routes[0:1, :].astype(F32), routes[1:2, :].astype(F32), segment)):
        facts = jnp.where(fact_row == n, values, facts)
    fact_columns = dot((above == across).astype(F32).astype(BF), facts.astype(BF), NT)
    route_columns = [fact_columns[:, n:n + 1] for n in range(2)]
    route = fact_columns.astype(jnp.int32)
    expert = jnp.bitwise_and(route, experts - 1)
    kind = jnp.right_shift(route, shift)
    host_plane = jnp.where(jnp.bitwise_and(expert, 1) == 0, kind, 3 - kind)
    host = host_plane * per_plane + jnp.right_shift(expert, 1)
    chip_iota = lax.broadcasted_iota(jnp.int32, (rows, chips), 1)
    chosen = [(chip_iota == host[:, n:n + 1]).astype(F32) for n in range(2)]
    earlier = (across < above).astype(F32).astype(BF)
    before = dot(earlier, (chosen[0] + chosen[1]).astype(BF), NN)
    position = [jnp.sum(one * before, axis=1, keepdims=True) for one in chosen]
    slot = [
        jnp.where(position[n] < capacity, host[:, n:n + 1].astype(F32) * padded + position[n], -1.0)
        for n in range(2)
    ]
    place = slot_places(slot, chips * padded)
    both = place[0] + place[1]

    def fill(target, values):
        sent = dot(both, values, TN)
        for n in range(chips):
            target[n] = sent[n * padded:(n + 1) * padded].astype(BF)

    def token_copy(src, dst, which, step):
        target = lax.rem(at.me + step, chips)
        zt, it = lax.div(target, per_plane), 2 * lax.rem(target, per_plane) + core
        return send_to(src.at[target], dst.at[at.me], ts.at[which, step], tr.at[which, step], zt, it)

    def token_start(src, dst, which):
        pltpu.make_async_copy(src.at[at.me], dst.at[at.me], tl.at[which]).start()

        def step(n, carry):
            token_copy(src, dst, which, n).start()
            return carry

        lax.fori_loop(1, chips, step, 0)

    def token_finish(src, dst, which):
        def step(n, carry):
            source = lax.rem(at.me + chips - n, chips)
            send_to(
                src.at[source], dst.at[source], ts.at[which, n], tr.at[which, n], z, i
            ).wait_recv()
            token_copy(src, dst, which, n).wait_send()
            return carry

        lax.fori_loop(1, chips, step, 0)
        pltpu.make_async_copy(src.at[at.me], dst.at[at.me], tl.at[which]).wait()

    fill(esend, cot[...])
    token_start(esend, dland, 0)
    for n, kind in ((6, 0), (7, 1)):
        loads[n].wait()
        cast(ostage, obf, kind, 32)
        for h in range(2):
            ship(kind, h, 1)
    same = jnp.logical_and(fact_columns[:, 2:3] == segment, across <= above)
    allow[...] = same.astype(F32)

    def pass_on(src, j, step, target):
        copy = send_to(src, src, gs.at[j - 1, step], gr.at[j - 1, step], z, target)
        copy.start()
        started.append(copy)

    def landed(dst, j, step):
        send_to(dst, dst, gs.at[j - 1, step], gr.at[j - 1, step], z, i).wait_recv()

    for j in range(1, planes):
        zz = lax.rem(z + planes - j, planes)
        mine = block(zz, rq, xb)
        send_to(mine, mine, zs.at[j - 1], zr.at[j - 1], z, i).wait_recv()
        pass_on(mine, j, 0, at.xn)
        pass_on(mine, j, 1, at.yn)
        pass_on(mine, j, 2, at.sib)
        send_to(packs.at[zz], packs.at[zz], ps.at[j - 1], pr.at[j - 1], z, i).wait_recv()
    pk[...] = jnp.concatenate([packs[p] for p in range(planes)], axis=1)

    x = tokens[...].astype(F32)
    gain = pk[nrouter:nrouter + 1, :].astype(F32)
    bias = pk[nrouter + 1:nrouter + 2, :].astype(F32)
    act_one[...] = (norm_parts(x)[0] * gain + bias).astype(BF)

    for j in range(1, planes):
        zz = lax.rem(z + planes - j, planes)
        bx, by = block(zz, rq, xo), block(zz, rqy, xb)
        landed(bx, j, 0)
        landed(by, j, 1)
        onward = block(zz, rq + core * (rqy - rq), xo + core * (xb - xo))
        pass_on(onward, j, 3, at.yn + core * (at.xn - at.yn))
        pass_on(bx, j, 4, at.sib)
        pass_on(by, j, 5, at.sib)
    for j in range(1, planes):
        zz = lax.rem(z + planes - j, planes)
        bd = block(zz, rqy, xo)
        landed(bd, j, 3)
        pass_on(bd, j, 6, at.sib)
    for j in range(1, planes):
        zz = lax.rem(z + planes - j, planes)
        landed(block(zz, rqs, xb), j, 2)
        landed(block(zz, rqs, xo), j, 4)
        landed(block(zz, rqys, xb), j, 5)
        landed(block(zz, rqys, xo), j, 6)

    def act_copy(step, whole):
        target = lax.rem(spot + step, 8)
        src = act_one if whole else att
        return target, send_to(src, ga.at[spot], sa.at[step], ra.at[step], z, base + target)

    def act_near(whole):
        return pltpu.make_async_copy(act_one if whole else att, ga.at[spot], tl.at[3])

    for step in range(1, 8):
        target, copy = act_copy(step, True)
        pl.when(target < pairs)(copy.start)
    pl.when(spot < pairs)(act_near(True).start)

    one = act_one[...]
    q[...] = dot(one, wd[0], NN, BF)
    k[...] = dot(one, wd[1], NN, BF)
    v[...] = dot(one, wd[2], NN, BF)
    lane = lax.broadcasted_iota(jnp.int32, (rows, 128), 1)
    masks = [(lane < HEAD).astype(F32).astype(BF), (lane >= HEAD).astype(F32).astype(BF)]
    score_scale = HEAD ** (-0.5)

    def head_pair(n, carry):
        cols = pl.ds(pl.multiple_of(n * 128, 128), 128)
        q2, k2, v2 = q[:, cols], k[:, cols], v[:, cols]
        total = jnp.zeros((rows, 128), F32)
        for side in range(2):
            scores = dot(q2 * masks[side], k2, NT) * score_scale
            scores = jnp.where(allow[...] > 0.5, scores, MASKED)
            expo = jnp.exp(scores - jnp.max(scores, axis=-1, keepdims=True))
            p = expo / jnp.sum(expo, axis=-1, keepdims=True)
            probs[2 * n + side] = p
            total += dot(p.astype(BF), v2 * masks[side], NN)
        att[:, cols] = total.astype(BF)
        return carry

    lax.fori_loop(0, pairs, head_pair, 0)
    residual = x + dot(att[...], wd[3], NN)
    resid[...] = residual
    gain = pk[nrouter + 2:nrouter + 3, :].astype(F32)
    bias = pk[nrouter + 3:nrouter + 4, :].astype(F32)
    two = (norm_parts(residual)[0] * gain + bias).astype(BF)
    act_two[...] = two
    fill(xsend, two)
    token_start(xsend, xland, 1)
    for step in range(1, 8):
        target, copy = act_copy(step, False)
        pl.when(target >= pairs)(copy.start)
    pl.when(spot >= pairs)(act_near(False).start)

    logits = dot(two, pk[0:nrouter, :], NT)
    route_iota = lax.broadcasted_iota(jnp.int32, (rows, nrouter), 1)
    picked = [
        jnp.sum(jnp.where(route_iota == route[:, n:n + 1], logits, 0.0), axis=1, keepdims=True)
        for n in range(2)
    ]
    top = jnp.maximum(picked[0], picked[1])
    lifted = [jnp.exp(one_pick - top) for one_pick in picked]
    gates = [one_lift / (lifted[0] + lifted[1]) for one_lift in lifted]
    values = jnp.zeros((rows, 128), F32)
    for n, column in enumerate(gates + slot + route_columns):
        values = jnp.where(lane == n, column, values)
    aux[...] = values
    lanes = lane.astype(F32)
    table = jnp.zeros((chips, 128), F32)
    for n in range(2):
        kept = jnp.logical_and(lanes == position[n], position[n] < capacity)
        table += exact_dot(chosen[n], jnp.where(kept, gates[n], 0.0), TN)
    for n in range(chips):
        gsend[n] = table[n:n + 1]
    token_start(gsend, gland, 2)

    def hand_on(plane, which):
        blk = in_block(plane, core) if which == 0 else out_block(plane, core)
        send_to(blk, blk, es.at[0, 0, which], er.at[plane, which], z, i).wait_recv()
        copy = send_to(blk, blk, fs.at[plane, which], fr.at[plane, which], z, at.sib)
        copy.start()
        started.append(copy)

    for which in range(2):
        for plane in range(planes):
            hand_on(plane, which)
    for src, dst, which in ((esend, dland, 0), (xsend, xland, 1), (gsend, gland, 2)):
        token_finish(src, dst, which)
    for step in range(1, 8):
        source = lax.rem(spot + 8 - step, 8)
        send_to(act_one, ga.at[source], sa.at[step], ra.at[step], z, i).wait_recv()
        act_copy(step, True)[1].wait_send()
    act_near(True).wait()
    for which in range(2):
        for plane in range(planes):
            blk = in_block(plane, 1 - core) if which == 0 else out_block(plane, 1 - core)
            send_to(blk, blk, fs.at[plane, which], fr.at[plane, which], z, i).wait_recv()
    for copy in started:
        copy.wait_send()
    for remote, far in remote_sends:
        pl.when(remote)(far.wait_send)


def front(planes, experts, capacity, padded, nrouter, tokens, cot, segment_ids, routes, router, norms,
          wq, wk, wv, wo, fi, fo, ni, no):
    rows, width = tokens.shape
    share = wq.shape[0]
    ff = fi.shape[2]
    oshare = fo.shape[1]
    chips = planes * experts // 2
    dma = pltpu.SemaphoreType.DMA
    vm = pltpu.VMEM
    sds = jax.ShapeDtypeStruct
    flat = sds((rows, width), BF)
    slab = sds((chips, padded, width), BF)
    return pl.pallas_call(
        functools.partial(front_kernel, planes, experts, capacity, padded, nrouter),
        out_shape=(
            sds((4, width, width), BF),
            sds((nrouter + 16, width), BF),
            sds((width, ff), BF),
            sds((ff, width), BF),
            flat, flat, flat, flat, flat, flat,
            sds((rows, width), F32),
            sds((HEADS, rows, rows), F32),
            sds((rows, 128), F32),
            sds((8, rows, width), BF),
            slab,
            slab,
            sds((chips, 1, 128), F32),
        ),
        in_specs=[vmem_spec()] * 9 + [any_spec()] * 8,
        out_specs=(vmem_spec(), vmem_spec(), any_spec(), any_spec()) + (vmem_spec(),) * 9 + (any_spec(),) * 4,
        scratch_shapes=[
            vm((planes, nrouter + 16, share), BF),
            vm((rows, rows), F32),
            vm((chips, padded, width), BF),
            vm((chips, padded, width), BF),
            vm((chips, 1, 128), F32),
            vm((4, share, width), F32),
            vm((2, share, ff), F32),
            vm((2, oshare, width), F32),
            vm((2, share, ff), BF),
            vm((2, oshare, width), BF),
            dma((8,)),
            dma((planes - 1,)), dma((planes - 1,)), dma((planes - 1,)), dma((planes - 1,)),
            dma((planes - 1, 7)), dma((planes - 1, 7)),
            dma((2, 2, 2)), dma((planes, 2)), dma((planes, 2)), dma((planes, 2)),
            dma((3, chips)), dma((3, chips)), dma((4,)), dma((8,)), dma((8,)),
        ],
        compiler_params=pltpu.CompilerParams(
            collective_id=0, has_side_effects=True, vmem_limit_bytes=VMEM_LIMIT
        ),
        name="front",
    )(tokens, cot, segment_ids, routes.T, router.T, *[norm.reshape(1, share) for norm in norms],
      wq, wk, wv, wo, fi, fo, ni, no)


GELU_SCALE = 0.7978845608028654
GELU_CUBE = 0.044715


def mid_kernel(planes, experts, padded, blocks,
               x, do, gate, win, wout,
               ysend, gi, go, dxland, dgland,
               wi, wo, dy, hid, dpre, dxsend, dgsend,
               ls, ts, tr, tl):
    at = Place(planes, experts)
    z, i, core = at.z, at.i, at.core
    per_plane = experts // 2
    chunk = per_plane * padded
    width = x.shape[1]
    ff = wi.shape[1]
    wide = ff // blocks
    load_i = pltpu.make_async_copy(win, wi, ls.at[0])
    load_o = pltpu.make_async_copy(wout, wo, ls.at[1])
    load_i.start()
    load_o.start()
    met = greet(at)
    lane = lax.broadcasted_iota(jnp.int32, (padded, 128), 1)
    diagonal = lane == lax.broadcasted_iota(jnp.int32, (padded, 128), 0)
    load_i.wait()
    load_o.wait()
    met()

    def copies(plane, n):
        target = plane * per_plane + n
        there = 2 * n + core
        rows = dxland.at[pl.ds(pl.multiple_of(at.me * padded, 8), padded), :]
        return [
            send_to(dxsend.at[target], rows, ts.at[0, target], tr.at[0, at.me], plane, there),
            send_to(dgsend.at[target], dgland.at[at.me], ts.at[1, target], tr.at[1, at.me], plane, there),
        ]

    def own_copies():
        rows = dxland.at[pl.ds(pl.multiple_of(at.me * padded, 8), padded), :]
        return [
            pltpu.make_async_copy(dxsend.at[at.me], rows, tl.at[0]),
            pltpu.make_async_copy(dgsend.at[at.me], dgland.at[at.me], tl.at[1]),
        ]

    def work(plane):
        rows = pl.ds(pl.multiple_of(plane * chunk, 16), chunk)
        x_c = x[rows, :]
        do_c = do[rows, :].astype(F32)
        column = jnp.concatenate(
            [
                jnp.sum(jnp.where(diagonal, gate[plane * per_plane + n], 0.0), axis=1, keepdims=True)
                for n in range(per_plane)
            ],
            axis=0,
        )
        dy_c = (do_c * column).astype(BF)
        dy[rows, :] = dy_c
        y_sum = jnp.zeros((chunk, width), F32)
        dx_sum = jnp.zeros((chunk, width), F32)
        for b in range(blocks):
            cols = slice(b * wide, (b + 1) * wide)
            u = dot(x_c, wi[:, cols], NN)
            dz = dot(dy_c, wo[cols, :], NT)
            square = u * u
            bent = jnp.tanh(GELU_SCALE * (u + GELU_CUBE * (square * u)))
            cdf = 0.5 * (1.0 + bent)
            slope = cdf + (0.5 * GELU_SCALE) * u * (1.0 - bent * bent) * (1.0 + 3.0 * GELU_CUBE * square)
            hidden = (u * cdf).astype(BF)
            d_pre = (dz * slope).astype(BF)
            hid[rows, cols] = hidden
            dpre[rows, cols] = d_pre
            y_sum += dot(hidden, wo[cols, :], NN)
            dx_sum += dot(d_pre, wi[:, cols], NT)
        y_low = y_sum.astype(BF)
        d_gate = jnp.sum(y_low.astype(F32) * do_c, axis=1, keepdims=True)
        for n in range(per_plane):
            part = slice(n * padded, (n + 1) * padded)
            source = plane * per_plane + n
            ysend[source] = y_sum[part].astype(BF)
            dxsend[source] = dx_sum[part].astype(BF)
            dgsend[source] = jnp.sum(jnp.where(diagonal, d_gate[part], 0.0), axis=0, keepdims=True)

    def far_plane(turn):
        half = 1 - 2 * lax.rem(z, 2)
        other = lax.rem(z + 2, planes)
        return jnp.where(turn == 0, other, jnp.where(turn == 1, planes - 1 - z, z + half))

    def remote_turn(turn, carry):
        plane = far_plane(turn)
        work(plane)
        for n in range(per_plane):
            for copy in copies(plane, n):
                copy.start()
        return carry

    lax.fori_loop(0, planes - 1, remote_turn, 0)
    work(z)
    for copy in own_copies():
        copy.start()
    for n in range(per_plane):
        for copy in copies(z, n):
            pl.when(at.chip != n)(copy.start)

    @pl.when(jnp.logical_and(z >= 1, z <= 2))
    def _():
        turned = x[...].T
        for b in range(blocks):
            cols = slice(b * wide, (b + 1) * wide)
            gi[:, cols] = dot(turned, dpre[:, cols], NN, BF)
        for b in range(blocks):
            cols = slice(b * wide, (b + 1) * wide)
            go[cols, :] = dot(hid[:, cols], dy[...], TN, BF)

    def finish(step, carry):
        source = lax.rem(at.me + step, at.chips)
        plane, n = lax.div(source, per_plane), lax.rem(source, per_plane)
        rows = dxland.at[pl.ds(pl.multiple_of(source * padded, 8), padded), :]
        send_to(dxsend.at[source], rows, ts.at[0, source], tr.at[0, source], z, i).wait_recv()
        send_to(dgsend.at[source], dgland.at[source], ts.at[1, source], tr.at[1, source], z, i).wait_recv()
        for copy in copies(plane, n):
            copy.wait_send()
        return carry

    lax.fori_loop(1, at.chips, finish, 0)
    for copy in own_copies():
        copy.wait()


def mid(planes, experts, x, do, gate, win, wout):
    chips, padded, width = x.shape
    ff = win.shape[1]
    slots = chips * padded
    blocks = 4
    dma = pltpu.SemaphoreType.DMA
    vm = pltpu.VMEM
    sds = jax.ShapeDtypeStruct
    return pl.pallas_call(
        functools.partial(mid_kernel, planes, experts, padded, blocks),
        out_shape=(
            sds((chips, padded, width), BF),
            sds((width, ff), BF),
            sds((ff, width), BF),
            sds((slots, width), BF),
            sds((chips, 1, 128), F32),
        ),
        in_specs=[vmem_spec()] * 3 + [any_spec()] * 2,
        out_specs=(vmem_spec(),) * 3 + (any_spec(),) * 2,
        scratch_shapes=[
            vm((width, ff), BF),
            vm((ff, width), BF),
            vm((slots, width), BF),
            vm((slots, ff), BF),
            vm((slots, ff), BF),
            vm((chips, padded, width), BF),
            vm((chips, 1, 128), F32),
            dma((2,)), dma((2, chips)), dma((2, chips)), dma((2,)),
        ],
        compiler_params=pltpu.CompilerParams(
            collective_id=2, has_side_effects=True, vmem_limit_bytes=VMEM_LIMIT
        ),
        name="mid",
    )(x.reshape(slots, width), do.reshape(slots, width), gate, win, wout)
def back_kernel(planes, experts, capacity_rows, nrouter,
                tokens, cot, aux, ga, act_two, q, k, v, resid, probs, wd, pk,
                dx, dg, ysend, gi, go,
                block_out, grad_tokens, fb, osmall, wi, wo, yland,
                gd, dsend, ycol, dres, datt, dq, dk, dv, gsum, szb, rzb, sup, rup,
                sms, smr, small, xi, ri, xo, ro,
                ls, es, er, hs, hr, ys, yr, yl, sd, rd, us, ur, zs, zr, gs, gr, ms, mr):
    at = Place(planes, experts)
    z, i, core = at.z, at.i, at.core
    padded = capacity_rows
    chips = at.chips
    per_plane = experts // 2
    rows, width = tokens.shape
    pairs = width // 128
    spot = lax.rem(i, 8)
    base = i - spot
    upper = sup.shape[0] if experts > 8 else 0
    met = greet(at)
    ce = z - 1
    host = jnp.logical_and(z >= 1, z <= 2)
    load_i = pltpu.make_async_copy(gi.at[:, core], xi, ls.at[0])
    load_o = pltpu.make_async_copy(go.at[:, core], xo, ls.at[1])

    @pl.when(host)
    def _():
        load_i.start()
        load_o.start()

    met()
    pair_i = send_to(gi.at[:, 1 - core], ri, es.at[0], er.at[0], z, at.sib)
    pair_o = send_to(go.at[:, 1 - core], ro, es.at[1], er.at[1], z, at.sib)

    @pl.when(host)
    def _():
        pair_i.start()
        pair_o.start()

    def landing(source):
        return yland.at[pl.ds(pl.multiple_of(source * padded, 8), padded), :]

    def y_copy(step):
        target = lax.rem(at.me + step, chips)
        zt, it = lax.div(target, per_plane), 2 * lax.rem(target, per_plane) + core
        return send_to(ysend.at[target], landing(at.me), ys.at[step], yr.at[step], zt, it)

    def y_start(step, carry):
        y_copy(step).start()
        return carry

    y_own = pltpu.make_async_copy(ysend.at[at.me], landing(at.me), yl.at[0])
    y_own.start()
    lax.fori_loop(1, chips, y_start, 0)

    aux_v = aux[...]
    gates = [aux_v[:, 0:1], aux_v[:, 1:2]]
    place = slot_places([aux_v[:, 2:3], aux_v[:, 3:4]], chips * padded)
    d_out = cot[...].astype(F32)
    d_act = dot(place[0] + place[1], dx[...], NN)
    table = dg[:, 0, :]
    d_gate = slot_values(aux_v, table, padded, chips)
    mean_gate = gates[0] * d_gate[0] + gates[1] * d_gate[1]
    route_iota = lax.broadcasted_iota(jnp.int32, (rows, nrouter), 1).astype(F32)
    d_logits = jnp.zeros((rows, nrouter), F32)
    for n in range(2):
        chosen = route_iota == aux_v[:, 4 + n:5 + n]
        d_logits = d_logits + jnp.where(chosen, gates[n] * (d_gate[n] - mean_gate), 0.0)
    d_logits = d_logits.astype(BF)
    small[0:nrouter, :] = dot(d_logits, act_two[...], TN)
    d_act = d_act + dot(d_logits, pk[0:nrouter, :], NN)
    gain_one = pk[nrouter:nrouter + 1, :].astype(F32)
    gain_two = pk[nrouter + 2:nrouter + 3, :].astype(F32)
    d_norm, g_gain, g_bias = norm_back(resid[...], gain_two, d_act)
    small[nrouter:nrouter + 16, :] = jnp.zeros((16, width), F32)
    small[nrouter + 2:nrouter + 3, :] = g_gain
    small[nrouter + 3:nrouter + 4, :] = g_bias
    d_res = d_out + d_norm
    dres[...] = d_res
    d_branch = d_res.astype(BF)
    half = width // 2
    for n in range(2):
        dsend[pairs + n] = d_branch[:, n * half:(n + 1) * half]
    datt[...] = dot(d_branch, wd[3], NT, BF)

    def d_copy(target):
        return send_to(dsend.at[target], gd.at[spot], sd.at[target], rd.at[spot], z, base + target)

    def d_near(target):
        return pltpu.make_async_copy(dsend.at[target], gd.at[spot], rd.at[spot])

    def d_start(target):
        far = spot != target
        pl.when(far)(d_copy(target).start)
        pl.when(jnp.logical_not(far))(d_near(target).start)

    for n in range(2):
        d_start(pairs + n)

    owner = 2 * at.chip + ce
    shipments = []

    def ship(p, which):
        src, dst = (xi.at[p], wi.at[core]) if which == 0 else (xo.at[p], wo.at[core])
        near = jnp.logical_and(z == p, core == ce)
        far_copy = send_to(src, dst, hs.at[p, which], hr.at[core, which], p, owner)
        near_copy = pltpu.make_async_copy(src, dst, hr.at[core, which])
        is_far = jnp.logical_and(host, jnp.logical_not(near))
        pl.when(is_far)(far_copy.start)
        pl.when(jnp.logical_and(host, near))(near_copy.start)
        shipments.append((is_far, far_copy))

    def add_pair(load, pair, mine, theirs, chunk):
        @pl.when(host)
        def _():
            load.wait()
            pair.wait_recv()

            def add(n, carry):
                part = pl.ds(pl.multiple_of(n * chunk, chunk), chunk)
                for p in range(planes):
                    mine[p, part, :] = (
                        mine[p, part, :].astype(F32) + theirs[p, part, :].astype(F32)
                    ).astype(BF)
                return carry

            lax.fori_loop(0, mine.shape[1] // chunk, add, 0)

    add_pair(load_i, pair_i, xi, ri, 16)
    for p in range(planes):
        ship(p, 0)
    add_pair(load_o, pair_o, xo, ro, 64)
    for p in range(planes):
        ship(p, 1)

    lane = lax.broadcasted_iota(jnp.int32, (rows, 128), 1)
    masks = [(lane < HEAD).astype(F32).astype(BF), (lane >= HEAD).astype(F32).astype(BF)]
    score_scale = HEAD ** (-0.5)

    def head_pair(n, carry):
        cols = pl.ds(pl.multiple_of(n * 128, 128), 128)
        q2, k2, v2, da2 = q[:, cols], k[:, cols], v[:, cols], datt[:, cols]
        sums = [jnp.zeros((rows, 128), F32) for _ in range(3)]
        for side in range(2):
            mask = masks[side]
            da = da2 * mask
            p = probs[2 * n + side]
            dpb = dot(da, v2, NT)
            delta = jnp.sum(p * dpb, axis=-1, keepdims=True)
            ds = (p * (dpb - delta)).astype(BF)
            sums[0] += dot(ds, k2 * mask, NN)
            sums[1] += dot(ds, q2 * mask, TN)
            sums[2] += dot(p.astype(BF), da, TN)
        low = [(sums[0] * score_scale).astype(BF), (sums[1] * score_scale).astype(BF), sums[2].astype(BF)]
        for m, (value, full) in enumerate(zip(low, (dq, dk, dv))):
            dsend[n, :, m * 128:(m + 1) * 128] = value
            full[:, cols] = value
        d_start(n)
        return carry

    lax.fori_loop(0, pairs, head_pair, 0)

    d_one = dot(dq[...], wd[0], NT) + dot(dk[...], wd[1], NT) + dot(dv[...], wd[2], NT)
    d_norm, g_gain, g_bias = norm_back(tokens[...].astype(F32), gain_one, d_one)
    grad_tokens[...] = (dres[...] + d_norm).astype(BF)
    small[nrouter:nrouter + 1, :] = g_gain
    small[nrouter + 1:nrouter + 2, :] = g_bias

    hops = [at.sib, at.xn, at.yn]
    for n in range(upper):
        bit = 8 << n
        hops.append(i + bit - 2 * bit * lax.rem(lax.div(i, bit), 2))
    moves = [(z, t) for t in hops]
    for n in range(planes.bit_length() - 1):
        bit = 1 << n
        moves.append((z + bit - 2 * bit * lax.rem(lax.div(z, bit), 2), i))
    small_copies = []

    def small_start(n):
        sms[n] = small[...]
        copy = send_to(sms.at[n], smr.at[n], ms.at[n], mr.at[n], moves[n][0], moves[n][1])
        copy.start()
        small_copies.append(copy)

    def small_step(n):
        small_copies[n].wait_recv()
        small[...] = small[...] + smr[n]
        if n + 1 < len(moves):
            small_start(n + 1)

    small_start(0)

    small_step(0)

    def d_wait(source, carry):
        send_to(gd.at[source], gd.at[source], sd.at[source], rd.at[source], z, i).wait_recv()
        return carry

    lax.fori_loop(0, 8, d_wait, 0)
    columns = gd.shape[2]
    total = dot(ga[...].reshape(8 * rows, width), gd[...].reshape(8 * rows, columns), TN)
    gsum[...] = total.reshape(planes, width // planes, columns)
    small_step(1)
    tail = []
    for n in range(upper):
        sup[n] = gsum[...].astype(BF)
        copy = send_to(sup.at[n], rup.at[n], us.at[n], ur.at[n], z, hops[3 + n])
        copy.start()
        tail.append(copy)
        copy.wait_recv()
        gsum[...] = sup[n].astype(F32) + rup[n].astype(F32)
    szb[...] = gsum[...].astype(BF)
    for j in range(1, planes):
        zt = lax.rem(z + j, planes)
        copy = send_to(szb.at[zt], rzb.at[j - 1], zs.at[j - 1], zr.at[j - 1], zt, i)
        copy.start()
        tail.append(copy)
    small_step(2)

    def y_finish(step, carry):
        source = lax.rem(at.me + chips - step, chips)
        send_to(landing(source), landing(source), ys.at[step], yr.at[step], z, i).wait_recv()
        y_copy(step).wait_send()
        return carry

    y_own.wait()
    lax.fori_loop(1, chips, y_finish, 0)
    fetch = pltpu.make_async_copy(yland, ycol, yl.at[1])
    fetch.start()
    fetch.wait()
    y_all = ycol[...]
    mixed = gates[0] * dot(place[0], y_all, NN) + gates[1] * dot(place[1], y_all, NN)
    block_out[...] = (resid[...] + mixed).astype(BF)

    fin = gsum[z]
    for j in range(1, planes):
        send_to(rzb.at[j - 1], rzb.at[j - 1], zs.at[j - 1], zr.at[j - 1], z, i).wait_recv()
        fin = fin + rzb[j - 1].astype(F32)
    fb[spot] = fin.astype(BF)
    px, py = spot + 2 - 4 * at.xb, spot + 4 - 8 * at.yb
    pd = px + 4 - 8 * at.yb
    flip = 1 - 2 * core

    def pass_on(where, step, target):
        copy = send_to(fb.at[where], fb.at[where], gs.at[step], gr.at[step], z, target)
        copy.start()
        tail.append(copy)

    def landed(where, step):
        send_to(fb.at[where], fb.at[where], gs.at[step], gr.at[step], z, i).wait_recv()

    pass_on(spot, 0, at.xn)
    pass_on(spot, 1, at.yn)
    pass_on(spot, 2, at.sib)
    small_step(3)
    landed(px, 0)
    landed(py, 1)
    pass_on(px + core * (py - px), 3, at.yn + core * (at.xn - at.yn))
    pass_on(px, 4, at.sib)
    pass_on(py, 5, at.sib)
    for n in range(4, len(moves)):
        small_step(n)
    osmall[...] = small[...]
    landed(pd, 3)
    pass_on(pd, 6, at.sib)
    for h in range(2):
        send_to(wi.at[h], wi.at[h], hs.at[0, 0], hr.at[h, 0], z, i).wait_recv()
        send_to(wo.at[h], wo.at[h], hs.at[0, 1], hr.at[h, 1], z, i).wait_recv()
    landed(spot + flip, 2)
    landed(px + flip, 4)
    landed(py + flip, 5)
    landed(pd + flip, 6)
    for copy in tail + small_copies:
        copy.wait_send()
    def d_sent(target, carry):
        pl.when(spot != target)(d_copy(target).wait_send)
        return carry

    lax.fori_loop(0, 8, d_sent, 0)

    @pl.when(host)
    def _():
        pair_i.wait_send()
        pair_o.wait_send()

    for is_far, copy in shipments:
        pl.when(is_far)(copy.wait_send)


def back(planes, experts, nrouter, tokens, cot, aux, ga, act_two, q, k, v, resid,
         probs, wd, pk, dx, dg, ysend, gi, go):
    rows, width = tokens.shape
    chips, padded, _ = ysend.shape
    ff = gi.shape[1]
    share, fshare, half = width // planes, ff // planes, width // 2
    upper = max(experts.bit_length() - 4, 1)
    nbits = experts.bit_length() - 1 + planes.bit_length() - 1
    gi = gi.reshape(planes, 2, share // 2, ff)
    go = go.reshape(planes, 2, fshare // 2, width)
    dma = pltpu.SemaphoreType.DMA
    vm = pltpu.VMEM
    sds = jax.ShapeDtypeStruct
    return pl.pallas_call(
        functools.partial(back_kernel, planes, experts, padded, nrouter),
        out_shape=(
            sds((rows, width), BF),
            sds((rows, width), BF),
                    sds((8, share, half), BF),
            sds((nrouter + 16, width), F32),
            sds((2, share // 2, ff), BF),
            sds((2, fshare // 2, width), BF),
            sds((chips * padded, width), BF),
        ),
        in_specs=[vmem_spec()] * 15 + [any_spec()] * 2,
        out_specs=(vmem_spec(),) * 6 + (any_spec(),),
        scratch_shapes=[
            vm((8, rows, half), BF),
            vm((8, rows, half), BF),
            vm((chips * padded, width), BF),
            vm((rows, width), F32),
            vm((rows, width), BF),
            vm((rows, width), BF),
            vm((rows, width), BF),
            vm((rows, width), BF),
            vm((planes, share, half), F32),
            vm((planes, share, half), BF),
            vm((planes - 1, share, half), BF),
            vm((upper, planes, share, half), BF),
            vm((upper, planes, share, half), BF),
            vm((nbits, nrouter + 16, width), F32),
            vm((nbits, nrouter + 16, width), F32),
            vm((nrouter + 16, width), F32),
            vm((planes, share // 2, ff), BF),
            vm((planes, share // 2, ff), BF),
            vm((planes, fshare // 2, width), BF),
            vm((planes, fshare // 2, width), BF),
            dma((2,)), dma((2,)), dma((2,)),
            dma((planes, 2)), dma((2, 2)),
            dma((chips,)), dma((chips,)), dma((2,)),
            dma((8,)), dma((8,)),
            dma((upper,)), dma((upper,)),
            dma((planes - 1,)), dma((planes - 1,)),
            dma((7,)), dma((7,)), dma((nbits,)), dma((nbits,)),
        ],
        compiler_params=pltpu.CompilerParams(
            collective_id=3, has_side_effects=True, vmem_limit_bytes=VMEM_LIMIT
        ),
        name="back",
    )(tokens, cot, aux, ga, act_two, q, k, v, resid, probs, wd, pk, dx, dg, ysend, gi, go)


def finish_kernel(planes, nrouter, block_out, grad_tokens, fb, small, wi, wo,
                  ob, ot, o0, o1, o2, o3, og, ov, ogi, ogo,
                  s0, s1, s2, s3, sg, sv, si, so, sem):
    z = lax.axis_index("dp")
    share = s0.shape[0]
    pairs = s0.shape[1] // 128
    half = s0.shape[1] // 2
    copies = []

    def write(source, target):
        copy = pltpu.make_async_copy(source, target, sem.at[len(copies)])
        copy.start()
        copies.append(copy)

    write(block_out, ob)
    write(grad_tokens, ot)
    for wide, low, out in ((si, wi, ogi), (so, wo, ogo)):
        chunk = low.shape[1]
        for h in range(2):
            wide[h * chunk:(h + 1) * chunk, :] = low[h].astype(F32)
            write(wide.at[pl.ds(h * chunk, chunk), :], out.at[pl.ds(h * chunk, chunk), :])
    for m, (stage, out) in enumerate(((s0, o0), (s1, o1), (s2, o2))):
        for n in range(pairs):
            stage[:, n * 128:(n + 1) * 128] = fb[n, :, m * 128:(m + 1) * 128].astype(F32)
        write(stage, out)
    for n in range(2):
        s3[:, n * half:(n + 1) * half] = fb[pairs + n].astype(F32)
    write(s3, o3)
    mine = small[:, 0:share]
    for p in range(1, planes):
        mine = jnp.where(z == p, small[:, p * share:(p + 1) * share], mine)
    sg[...] = mine[0:nrouter]
    write(sg, og)
    for n in range(4):
        sv[n] = mine[nrouter + n:nrouter + n + 1]
        write(sv.at[n], ov.at[n])
    for copy in copies:
        copy.wait()


def finish(planes, nrouter, block_out, grad_tokens, fb, small, wi, wo):
    rows, width = block_out.shape
    _, share, half = fb.shape
    ff = wi.shape[2]
    fshare = 2 * wo.shape[1]
    vm = pltpu.VMEM
    sds = jax.ShapeDtypeStruct
    flat = ((share, width),) * 4 + ((nrouter, share), (4, 1, share), (share, ff), (fshare, width))
    return pl.pallas_call(
        functools.partial(finish_kernel, planes, nrouter),
        out_shape=(sds((rows, width), BF),) * 2 + tuple(sds(shape, F32) for shape in flat),
        in_specs=[vmem_spec()] * 6,
        out_specs=(any_spec(),) * 10,
        scratch_shapes=[vm(shape, F32) for shape in flat] + [pltpu.SemaphoreType.DMA((16,))],
        compiler_params=pltpu.CompilerParams(vmem_limit_bytes=VMEM_LIMIT),
        name="finish",
    )(block_out, grad_tokens, fb, small, wi, wo)


def shards(planes, experts, tokens, segment_ids, routes, ln1_gain, ln1_bias, ln2_gain, ln2_bias,
           w_query, w_key, w_value, w_output, w_router, frozen_in, frozen_out, new_in, new_out,
           cotangent):
    rows, width = tokens.shape
    expert_count = w_router.shape[1]
    capacity = 5 * rows // (2 * expert_count)
    padded = -(-capacity // 8) * 8
    (wd, pk, win, wout, _, act_two, q, k, v, _, resid, probs, aux, ga, x_recv, do_recv, g_recv) = front(
        planes, experts, capacity, padded, expert_count, tokens, cotangent, segment_ids, routes,
        w_router, (ln1_gain, ln1_bias, ln2_gain, ln2_bias),
        w_query, w_key, w_value, w_output, frozen_in, frozen_out, new_in, new_out,
    )
    y_rows, grad_in, grad_out, dx_back, dg_back = mid(
        planes, experts, x_recv, do_recv, g_recv, win, wout
    )
    block_out, grad_tokens, dense, small, low_in, low_out, _ = back(
        planes, experts, expert_count, tokens, cotangent, aux, ga, act_two, q, k, v,
        resid, probs, wd, pk, dx_back, dg_back, y_rows, grad_in, grad_out,
    )
    block_out, grad_tokens, oq, ok, ov, ow, router, norms, ogi, ogo = finish(
        planes, expert_count, block_out, grad_tokens, dense, small, low_in, low_out
    )
    norms = norms.reshape(4, width // planes)
    return (
        block_out, grad_tokens, oq, ok, ov, ow, router.T,
        norms[0], norms[1], norms[2], norms[3], ogi[None], ogo[None],
    )


def solution(mesh):
    rows = P(("dp", "expert"), None)
    in_specs = (rows, rows, rows) + (P("dp"),) * 4 + (P("dp", None),) * 5
    in_specs += (P("expert", "dp", None),) * 4 + (rows,)
    out_specs = (rows, rows) + (P("dp", None),) * 5 + (P("dp"),) * 4
    out_specs += (P("expert", "dp", None),) * 2
    body = functools.partial(shards, mesh.shape["dp"], mesh.shape["expert"])
    return jax.shard_map(body, mesh=mesh, in_specs=in_specs, out_specs=out_specs, check_vma=False)
```

```python
import functools

import jax
import jax.numpy as jnp
from jax import lax
from jax.experimental import pallas as pl
from jax.experimental.pallas import tpu as pltpu
from jax.sharding import PartitionSpec as P

HEADS = 12
HEAD = 64
NORM_EPS = 1e-05
MASKED = -1e30
MESH = pl.DeviceIdType.MESH
BF = jnp.bfloat16
F32 = jnp.float32
VMEM_LIMIT = 60 * 1024 * 1024
REAR_LIMIT = 67043328


class Place:
    def __init__(self, planes, experts):
        self.planes, self.experts = planes, experts
        self.z = lax.axis_index("dp")
        self.i = lax.axis_index("expert")
        self.core = lax.rem(self.i, 2)
        self.chip = lax.div(self.i, 2)
        self.xb = lax.rem(self.chip, 2)
        self.yb = lax.rem(lax.div(self.i, 4), 2)
        self.sib = self.i + 1 - 2 * self.core
        self.xn = self.i + 2 - 4 * self.xb
        self.yn = self.i + 4 - 8 * self.yb
        self.chips = planes * (experts // 2)
        self.me = self.z * (experts // 2) + self.chip


def send_to(src, dst, send_sem, recv_sem, z, i):
    return pltpu.make_async_remote_copy(
        src_ref=src,
        dst_ref=dst,
        send_sem=send_sem,
        recv_sem=recv_sem,
        device_id={"dp": z, "expert": i},
        device_id_type=MESH,
    )


def greet(at):
    barrier = pltpu.get_barrier_semaphore()
    count = at.planes * at.experts
    own = at.z * at.experts + at.i

    def signal(step, carry):
        target = lax.rem(own + step, count)
        pl.semaphore_signal(
            barrier,
            inc=1,
            device_id={"dp": lax.div(target, at.experts), "expert": lax.rem(target, at.experts)},
            device_id_type=MESH,
        )
        return carry

    lax.fori_loop(1, count, signal, 0)
    return lambda: pl.semaphore_wait(barrier, count - 1)


def any_spec():
    return pl.BlockSpec(memory_space=pl.ANY)


def vmem_spec():
    return pl.BlockSpec(memory_space=pltpu.VMEM)


NN = ((1,), (0,))
NT = ((1,), (1,))
TN = ((0,), (0,))


def dot(left, right, contract, out=F32):
    return lax.dot_general(
        left, right, ((contract[0], contract[1]), ((), ())), preferred_element_type=F32
    ).astype(out)


def exact_dot(left, right, contract):
    return lax.dot_general(
        left, right, ((contract[0], contract[1]), ((), ())),
        preferred_element_type=F32, precision=lax.Precision.HIGHEST,
    )


def norm_parts(rows):
    centred = rows - jnp.mean(rows, axis=-1, keepdims=True)
    variance = jnp.mean(centred * centred, axis=-1, keepdims=True)
    scale = lax.rsqrt(variance + NORM_EPS)
    return centred * scale, scale


def norm_back(rows, gain, grad):
    unit, scale = norm_parts(rows)
    scaled = grad * gain
    inner = scaled - jnp.mean(scaled, axis=-1, keepdims=True)
    inner = inner - unit * jnp.mean(scaled * unit, axis=-1, keepdims=True)
    return scale * inner, jnp.sum(grad * unit, axis=0, keepdims=True), jnp.sum(grad, axis=0, keepdims=True)


def slot_places(slot, slots):
    lanes = lax.broadcasted_iota(jnp.int32, (slot[0].shape[0], slots), 1).astype(F32)
    return [(lanes == one).astype(F32).astype(BF) for one in slot]


def slot_values(aux, table, padded, chips):
    rows = aux.shape[0]
    low = lax.broadcasted_iota(jnp.int32, (rows, chips), 1).astype(F32) * padded
    lanes = lax.broadcasted_iota(jnp.int32, (rows, table.shape[1]), 1).astype(F32)
    found = []
    for k in range(2):
        slot = aux[:, 2 + k:3 + k]
        mine = jnp.logical_and(slot >= low, slot < low + padded).astype(F32)
        position = slot - jnp.sum(mine * low, axis=1, keepdims=True)
        picked = exact_dot(mine, table, NN)
        found.append(jnp.sum(jnp.where(lanes == position, picked, 0.0), axis=1, keepdims=True))
    return found


def front_kernel(planes, experts, capacity, padded, nrouter,
                 tokens, cot, segs, routes, router, g1, b1, g2, b2, wq, wk, wv, wo, fi, fo, ni, no,
                 wd, pk, win, wout, act_one, act_two, q, k, v, att, resid, probs, aux, ga,
                 xland, dland, gland,
                 packs, allow, xsend, esend, gsend, dstage, istage, ostage, ibf, obf,
                 ld, zs, zr, ps, pr, gs, gr, es, er, fs, fr, ts, tr, tl, sa, ra):
    at = Place(planes, experts)
    z, i, core = at.z, at.i, at.core
    rows, width = tokens.shape
    chips = at.chips
    per_plane = experts // 2
    share = dstage.shape[1]
    quarter = share // 4
    half = width // 2
    fhalf = istage.shape[2] // 2
    oshare = ostage.shape[1]
    ohalf = oshare // 2
    pairs = width // 128
    spot = lax.rem(i, 8)
    base = i - spot
    loads = [pltpu.make_async_copy(w, dstage.at[m], ld.at[m]) for m, w in enumerate((wq, wk, wv, wo))]
    loads += [
        pltpu.make_async_copy(fi.at[0], istage.at[0], ld.at[4]),
        pltpu.make_async_copy(ni.at[0], istage.at[1], ld.at[5]),
        pltpu.make_async_copy(fo.at[0], ostage.at[0], ld.at[6]),
        pltpu.make_async_copy(no.at[0], ostage.at[1], ld.at[7]),
    ]
    for load in loads:
        load.start()
    met = greet(at)
    zrow = pl.multiple_of(z * share, share)
    for m in range(4):
        loads[m].wait()
        wd[m, pl.ds(zrow, share), :] = dstage[m].astype(BF)
    packs[z, 0:nrouter, :] = router[...].astype(BF)
    norm_row = lax.broadcasted_iota(jnp.int32, (16, share), 0)
    norms = jnp.zeros((16, share), F32)
    for n, values in enumerate((g1, b1, g2, b2)):
        norms = jnp.where(norm_row == n, values[...], norms)
    packs[z, nrouter:nrouter + 16, :] = norms.astype(BF)
    met()

    def block(plane, row_quarter, column_half):
        return wd.at[
            :,
            pl.ds(pl.multiple_of(plane * share + row_quarter * quarter, 16), quarter),
            pl.ds(pl.multiple_of(column_half * half, 128), half),
        ]

    rq = 2 * at.yb + core
    rqy = 2 * (1 - at.yb) + core
    rqs = 2 * at.yb + 1 - core
    rqys = 2 * (1 - at.yb) + 1 - core
    xb, xo = at.xb, 1 - at.xb
    started = []
    for j in range(1, planes):
        zt = lax.rem(z + j, planes)
        mine = block(z, rq, xb)
        copy = send_to(mine, mine, zs.at[j - 1], zr.at[j - 1], zt, i)
        copy.start()
        started.append(copy)
        copy = send_to(packs.at[z], packs.at[z], ps.at[j - 1], pr.at[j - 1], zt, i)
        copy.start()
        started.append(copy)

    def cast(source, target, kind, chunk):
        def step(n, carry):
            part = pl.ds(pl.multiple_of(n * chunk, chunk), chunk)
            target[kind, part, :] = source[kind, part, :].astype(BF)
            return carry

        lax.fori_loop(0, source.shape[1] // chunk, step, 0)

    def in_block(plane, h):
        return win.at[
            pl.ds(pl.multiple_of(plane * share, 16), share),
            pl.ds(pl.multiple_of(h * fhalf, 128), fhalf),
        ]

    def out_block(plane, h):
        return wout.at[pl.ds(pl.multiple_of(plane * oshare + h * ohalf, 16), ohalf), :]

    remote_sends = []

    def ship(kind, h, which):
        zh = 3 * core if kind == 0 else 1 + core
        remote = jnp.logical_or(zh != z, core != h)
        src = (
            ibf.at[kind, :, pl.ds(h * fhalf, fhalf)]
            if which == 0
            else obf.at[kind, pl.ds(h * ohalf, ohalf), :]
        )
        dst = in_block(z, h) if which == 0 else out_block(z, h)
        far = send_to(src, dst, es.at[kind, h, which], er.at[z, which], zh, 2 * at.chip + h)
        near = pltpu.make_async_copy(src, dst, er.at[z, which])
        pl.when(remote)(far.start)
        pl.when(jnp.logical_not(remote))(near.start)
        remote_sends.append((remote, far))

    for n, kind in ((4, 0), (5, 1)):
        loads[n].wait()
        cast(istage, ibf, kind, 16)
        for h in range(2):
            ship(kind, h, 0)

    shift = experts.bit_length() - 1
    above = lax.broadcasted_iota(jnp.int32, (rows, rows), 0)
    across = lax.broadcasted_iota(jnp.int32, (rows, rows), 1)
    segment = segs[...].astype(F32)
    fact_row = lax.broadcasted_iota(jnp.int32, (8, rows), 0)
    facts = jnp.zeros((8, rows), F32)
    for n, values in enumerate((routes[0:1, :].astype(F32), routes[1:2, :].astype(F32), segment)):
        facts = jnp.where(fact_row == n, values, facts)
    fact_columns = dot((above == across).astype(F32).astype(BF), facts.astype(BF), NT)
    route_columns = [fact_columns[:, n:n + 1] for n in range(2)]
    route = fact_columns.astype(jnp.int32)
    expert = jnp.bitwise_and(route, experts - 1)
    kind = jnp.right_shift(route, shift)
    host_plane = jnp.where(jnp.bitwise_and(expert, 1) == 0, kind, 3 - kind)
    host = host_plane * per_plane + jnp.right_shift(expert, 1)
    chip_iota = lax.broadcasted_iota(jnp.int32, (rows, chips), 1)
    chosen = [(chip_iota == host[:, n:n + 1]).astype(F32) for n in range(2)]
    earlier = (across < above).astype(F32).astype(BF)
    before = dot(earlier, (chosen[0] + chosen[1]).astype(BF), NN)
    position = [jnp.sum(one * before, axis=1, keepdims=True) for one in chosen]
    slot = [
        jnp.where(position[n] < capacity, host[:, n:n + 1].astype(F32) * padded + position[n], -1.0)
        for n in range(2)
    ]
    place = slot_places(slot, chips * padded)
    both = place[0] + place[1]

    def fill(target, values):
        sent = dot(both, values, TN)
        for n in range(chips):
            target[n] = sent[n * padded:(n + 1) * padded].astype(BF)

    def token_copy(src, dst, which, step):
        target = lax.rem(at.me + step, chips)
        zt, it = lax.div(target, per_plane), 2 * lax.rem(target, per_plane) + core
        return send_to(src.at[target], dst.at[at.me], ts.at[which, step], tr.at[which, step], zt, it)

    def token_start(src, dst, which):
        pltpu.make_async_copy(src.at[at.me], dst.at[at.me], tl.at[which]).start()

        def step(n, carry):
            token_copy(src, dst, which, n).start()
            return carry

        lax.fori_loop(1, chips, step, 0)

    def token_finish(src, dst, which):
        def step(n, carry):
            source = lax.rem(at.me + chips - n, chips)
            send_to(
                src.at[source], dst.at[source], ts.at[which, n], tr.at[which, n], z, i
            ).wait_recv()
            token_copy(src, dst, which, n).wait_send()
            return carry

        lax.fori_loop(1, chips, step, 0)
        pltpu.make_async_copy(src.at[at.me], dst.at[at.me], tl.at[which]).wait()

    fill(esend, cot[...])
    token_start(esend, dland, 0)
    for n, kind in ((6, 0), (7, 1)):
        loads[n].wait()
        cast(ostage, obf, kind, 32)
        for h in range(2):
            ship(kind, h, 1)
    same = jnp.logical_and(fact_columns[:, 2:3] == segment, across <= above)
    allow[...] = same.astype(F32)

    def pass_on(src, j, step, target):
        copy = send_to(src, src, gs.at[j - 1, step], gr.at[j - 1, step], z, target)
        copy.start()
        started.append(copy)

    def landed(dst, j, step):
        send_to(dst, dst, gs.at[j - 1, step], gr.at[j - 1, step], z, i).wait_recv()

    for j in range(1, planes):
        zz = lax.rem(z + planes - j, planes)
        mine = block(zz, rq, xb)
        send_to(mine, mine, zs.at[j - 1], zr.at[j - 1], z, i).wait_recv()
        pass_on(mine, j, 0, at.xn)
        pass_on(mine, j, 1, at.yn)
        pass_on(mine, j, 2, at.sib)
        send_to(packs.at[zz], packs.at[zz], ps.at[j - 1], pr.at[j - 1], z, i).wait_recv()
    pk[...] = jnp.concatenate([packs[p] for p in range(planes)], axis=1)

    x = tokens[...].astype(F32)
    gain = pk[nrouter:nrouter + 1, :].astype(F32)
    bias = pk[nrouter + 1:nrouter + 2, :].astype(F32)
    act_one[...] = (norm_parts(x)[0] * gain + bias).astype(BF)

    for j in range(1, planes):
        zz = lax.rem(z + planes - j, planes)
        bx, by = block(zz, rq, xo), block(zz, rqy, xb)
        landed(bx, j, 0)
        landed(by, j, 1)
        onward = block(zz, rq + core * (rqy - rq), xo + core * (xb - xo))
        pass_on(onward, j, 3, at.yn + core * (at.xn - at.yn))
        pass_on(bx, j, 4, at.sib)
        pass_on(by, j, 5, at.sib)
    for j in range(1, planes):
        zz = lax.rem(z + planes - j, planes)
        bd = block(zz, rqy, xo)
        landed(bd, j, 3)
        pass_on(bd, j, 6, at.sib)
    for j in range(1, planes):
        zz = lax.rem(z + planes - j, planes)
        landed(block(zz, rqs, xb), j, 2)
        landed(block(zz, rqs, xo), j, 4)
        landed(block(zz, rqys, xb), j, 5)
        landed(block(zz, rqys, xo), j, 6)

    def act_copy(step, whole):
        target = lax.rem(spot + step, 8)
        src = act_one if whole else att
        return target, send_to(src, ga.at[spot], sa.at[step], ra.at[step], z, base + target)

    def act_near(whole):
        return pltpu.make_async_copy(act_one if whole else att, ga.at[spot], tl.at[3])

    for step in range(1, 8):
        target, copy = act_copy(step, True)
        pl.when(target < pairs)(copy.start)
    pl.when(spot < pairs)(act_near(True).start)

    one = act_one[...]
    q[...] = dot(one, wd[0], NN, BF)
    k[...] = dot(one, wd[1], NN, BF)
    v[...] = dot(one, wd[2], NN, BF)
    lane = lax.broadcasted_iota(jnp.int32, (rows, 128), 1)
    masks = [(lane < HEAD).astype(F32).astype(BF), (lane >= HEAD).astype(F32).astype(BF)]
    score_scale = HEAD ** (-0.5)

    def head_pair(n, carry):
        cols = pl.ds(pl.multiple_of(n * 128, 128), 128)
        q2, k2, v2 = q[:, cols], k[:, cols], v[:, cols]
        total = jnp.zeros((rows, 128), F32)
        for side in range(2):
            scores = dot(q2 * masks[side], k2, NT) * score_scale
            scores = jnp.where(allow[...] > 0.5, scores, MASKED)
            expo = jnp.exp(scores - jnp.max(scores, axis=-1, keepdims=True))
            p = expo / jnp.sum(expo, axis=-1, keepdims=True)
            probs[2 * n + side] = p
            total += dot(p.astype(BF), v2 * masks[side], NN)
        att[:, cols] = total.astype(BF)
        return carry

    lax.fori_loop(0, pairs, head_pair, 0)
    residual = x + dot(att[...], wd[3], NN)
    resid[...] = residual
    gain = pk[nrouter + 2:nrouter + 3, :].astype(F32)
    bias = pk[nrouter + 3:nrouter + 4, :].astype(F32)
    two = (norm_parts(residual)[0] * gain + bias).astype(BF)
    act_two[...] = two
    fill(xsend, two)
    token_start(xsend, xland, 1)
    for step in range(1, 8):
        target, copy = act_copy(step, False)
        pl.when(target >= pairs)(copy.start)
    pl.when(spot >= pairs)(act_near(False).start)

    logits = dot(two, pk[0:nrouter, :], NT)
    route_iota = lax.broadcasted_iota(jnp.int32, (rows, nrouter), 1)
    picked = [
        jnp.sum(jnp.where(route_iota == route[:, n:n + 1], logits, 0.0), axis=1, keepdims=True)
        for n in range(2)
    ]
    top = jnp.maximum(picked[0], picked[1])
    lifted = [jnp.exp(one_pick - top) for one_pick in picked]
    gates = [one_lift / (lifted[0] + lifted[1]) for one_lift in lifted]
    values = jnp.zeros((rows, 128), F32)
    for n, column in enumerate(gates + slot + route_columns):
        values = jnp.where(lane == n, column, values)
    aux[...] = values
    lanes = lane.astype(F32)
    table = jnp.zeros((chips, 128), F32)
    for n in range(2):
        kept = jnp.logical_and(lanes == position[n], position[n] < capacity)
        table += exact_dot(chosen[n], jnp.where(kept, gates[n], 0.0), TN)
    for n in range(chips):
        gsend[n] = table[n:n + 1]
    token_start(gsend, gland, 2)

    def hand_on(plane, which):
        blk = in_block(plane, core) if which == 0 else out_block(plane, core)
        send_to(blk, blk, es.at[0, 0, which], er.at[plane, which], z, i).wait_recv()
        copy = send_to(blk, blk, fs.at[plane, which], fr.at[plane, which], z, at.sib)
        copy.start()
        started.append(copy)

    for which in range(2):
        for plane in range(planes):
            hand_on(plane, which)
    for src, dst, which in ((esend, dland, 0), (xsend, xland, 1), (gsend, gland, 2)):
        token_finish(src, dst, which)
    for step in range(1, 8):
        source = lax.rem(spot + 8 - step, 8)
        send_to(act_one, ga.at[source], sa.at[step], ra.at[step], z, i).wait_recv()
        act_copy(step, True)[1].wait_send()
    act_near(True).wait()
    for which in range(2):
        for plane in range(planes):
            blk = in_block(plane, 1 - core) if which == 0 else out_block(plane, 1 - core)
            send_to(blk, blk, fs.at[plane, which], fr.at[plane, which], z, i).wait_recv()
    for copy in started:
        copy.wait_send()
    for remote, far in remote_sends:
        pl.when(remote)(far.wait_send)


def front(planes, experts, capacity, padded, nrouter, tokens, cot, segment_ids, routes, router, norms,
          wq, wk, wv, wo, fi, fo, ni, no):
    rows, width = tokens.shape
    share = wq.shape[0]
    ff = fi.shape[2]
    oshare = fo.shape[1]
    chips = planes * experts // 2
    dma = pltpu.SemaphoreType.DMA
    vm = pltpu.VMEM
    sds = jax.ShapeDtypeStruct
    flat = sds((rows, width), BF)
    slab = sds((chips, padded, width), BF)
    return pl.pallas_call(
        functools.partial(front_kernel, planes, experts, capacity, padded, nrouter),
        out_shape=(
            sds((4, width, width), BF),
            sds((nrouter + 16, width), BF),
            sds((width, ff), BF),
            sds((ff, width), BF),
            flat, flat, flat, flat, flat, flat,
            sds((rows, width), F32),
            sds((HEADS, rows, rows), F32),
            sds((rows, 128), F32),
            sds((8, rows, width), BF),
            slab,
            slab,
            sds((chips, 1, 128), F32),
        ),
        in_specs=[vmem_spec()] * 9 + [any_spec()] * 8,
        out_specs=(vmem_spec(), vmem_spec(), any_spec(), any_spec()) + (vmem_spec(),) * 9 + (any_spec(),) * 4,
        scratch_shapes=[
            vm((planes, nrouter + 16, share), BF),
            vm((rows, rows), F32),
            vm((chips, padded, width), BF),
            vm((chips, padded, width), BF),
            vm((chips, 1, 128), F32),
            vm((4, share, width), F32),
            vm((2, share, ff), F32),
            vm((2, oshare, width), F32),
            vm((2, share, ff), BF),
            vm((2, oshare, width), BF),
            dma((8,)),
            dma((planes - 1,)), dma((planes - 1,)), dma((planes - 1,)), dma((planes - 1,)),
            dma((planes - 1, 7)), dma((planes - 1, 7)),
            dma((2, 2, 2)), dma((planes, 2)), dma((planes, 2)), dma((planes, 2)),
            dma((3, chips)), dma((3, chips)), dma((4,)), dma((8,)), dma((8,)),
        ],
        compiler_params=pltpu.CompilerParams(
            collective_id=0, has_side_effects=True, vmem_limit_bytes=VMEM_LIMIT
        ),
        name="front",
    )(tokens, cot, segment_ids, routes.T, router.T, *[norm.reshape(1, share) for norm in norms],
      wq, wk, wv, wo, fi, fo, ni, no)


GELU_SCALE = 0.7978845608028654
GELU_CUBE = 0.044715


def rear_kernel(planes, experts, padded, pieces, blocks, ga_groups, nrouter,
                x, do, gate, tokens, cot, aux, act_two, q, k, v, resid, probs, wd, pk, win, wout, ga,
                block_out, grad_tokens, fb, osmall, wi, wo, yland, dxland,
                hwi, hwo, dy, hid, dpre, dxsend, dgsend, dgland, ysend, landed_rows,
                gd, dsend, dres, gsum, szb, rzb, rup,
                sms, smr, small, ri, ro,
                ls, ts, tr, tl, gl,
                es, er, hs, hr, ys, yr, yl, sd, rd, us, ur, zs, zr, gs, gr, ms, mr):
    at = Place(planes, experts)
    z, i, core = at.z, at.i, at.core
    chips = at.chips
    per_plane = experts // 2
    rows, width = tokens.shape
    pairs = width // 128
    spot = lax.rem(i, 8)
    base = i - spot
    upper = rup.shape[0] if experts > 8 else 0
    ga_rows = 8 * rows // ga_groups
    datt, dq, dk, dv = [dpre.at[pl.ds(0, rows), pl.ds(n * width, width)] for n in range(4)]
    chunk = per_plane * padded // pieces
    batch = per_plane // pieces
    ff = hwi.shape[1]
    wide = ff // blocks
    load_i = pltpu.make_async_copy(win, hwi, ls.at[0])
    load_o = pltpu.make_async_copy(wout, hwo, ls.at[1])
    load_i.start()
    load_o.start()
    met = greet(at)
    diagonal = lax.broadcasted_iota(jnp.int32, (padded, 128), 1) == lax.broadcasted_iota(jnp.int32, (padded, 128), 0)
    load_i.wait()
    load_o.wait()
    met()

    def copies(plane, n):
        target = plane * per_plane + n
        there = 2 * n + core
        rows_in = dxland.at[pl.ds(pl.multiple_of(at.me * padded, 8), padded), :]
        return [
            send_to(dxsend.at[target], rows_in, ts.at[0, target], tr.at[0, at.me], plane, there),
            send_to(dgsend.at[target], dgland.at[at.me], ts.at[1, target], tr.at[1, at.me], plane, there),
        ]

    def own_copies():
        rows_in = dxland.at[pl.ds(pl.multiple_of(at.me * padded, 8), padded), :]
        return [
            pltpu.make_async_copy(dxsend.at[at.me], rows_in, tl.at[0]),
            pltpu.make_async_copy(dgsend.at[at.me], dgland.at[at.me], tl.at[1]),
        ]

    def work(plane, piece):
        first = plane * per_plane + piece * batch
        span = pl.ds(pl.multiple_of((plane * pieces + piece) * chunk, 16), chunk)
        x_c = x[span, :]
        do_c = do[span, :].astype(F32)
        column = jnp.concatenate(
            [
                jnp.sum(jnp.where(diagonal, gate[first + n], 0.0), axis=1, keepdims=True)
                for n in range(batch)
            ],
            axis=0,
        )
        dy_c = (do_c * column).astype(BF)
        dy[span, :] = dy_c
        y_sum = jnp.zeros((chunk, width), F32)
        dx_sum = jnp.zeros((chunk, width), F32)
        for b in range(blocks):
            cols = slice(b * wide, (b + 1) * wide)
            u = dot(x_c, hwi[:, cols], NN)
            dz = dot(dy_c, hwo[cols, :], NT)
            square = u * u
            bent = jnp.tanh(GELU_SCALE * (u + GELU_CUBE * (square * u)))
            cdf = 0.5 * (1.0 + bent)
            slope = cdf + (0.5 * GELU_SCALE) * u * (1.0 - bent * bent) * (1.0 + 3.0 * GELU_CUBE * square)
            hidden = (u * cdf).astype(BF)
            d_pre = (dz * slope).astype(BF)
            hid[span, cols] = hidden
            dpre[span, cols] = d_pre
            y_sum += dot(hidden, hwo[cols, :], NN)
            dx_sum += dot(d_pre, hwi[:, cols], NT)
        y_low = y_sum.astype(BF)
        d_gate = jnp.sum(y_low.astype(F32) * do_c, axis=1, keepdims=True)
        for n in range(batch):
            part = slice(n * padded, (n + 1) * padded)
            source = first + n
            ysend[source] = y_sum[part].astype(BF)
            dxsend[source] = dx_sum[part].astype(BF)
            dgsend[source] = jnp.sum(jnp.where(diagonal, d_gate[part], 0.0), axis=0, keepdims=True)

    def far_plane(turn):
        half = 1 - 2 * lax.rem(z, 2)
        other = lax.rem(z + 2, planes)
        return jnp.where(turn == 0, other, jnp.where(turn == 1, planes - 1 - z, z + half))

    def remote_turn(turn, carry):
        plane = far_plane(lax.div(turn, pieces))
        piece = lax.rem(turn, pieces)
        work(plane, piece)
        for n in range(batch):
            for copy in copies(plane, piece * batch + n):
                copy.start()
        return carry

    lax.fori_loop(0, (planes - 1) * pieces, remote_turn, 0)
    for piece in range(pieces):
        work(z, piece)
    for copy in own_copies():
        copy.start()
    for n in range(per_plane):
        for copy in copies(z, n):
            pl.when(at.chip != n)(copy.start)

    def landing(source):
        return yland.at[pl.ds(pl.multiple_of(source * padded, 8), padded), :]

    def y_copy(step):
        target = lax.rem(at.me + step, chips)
        zt, it = lax.div(target, per_plane), 2 * lax.rem(target, per_plane) + core
        return send_to(ysend.at[target], landing(at.me), ys.at[step], yr.at[step], zt, it)

    def y_start(step, carry):
        y_copy(step).start()
        return carry

    y_own = pltpu.make_async_copy(ysend.at[at.me], landing(at.me), yl.at[0])
    y_own.start()
    lax.fori_loop(1, chips, y_start, 0)

    ce = z - 1
    host = jnp.logical_and(z >= 1, z <= 2)
    half_i, half_o = width // planes // 2, ff // planes // 2

    def part(source, size, p, c):
        return source.at[pl.ds(pl.multiple_of((2 * p + c) * size, 16), size), :]

    pair = [
        [
            send_to(part(src, size, p, 1 - core), land.at[p], es.at[which, p], er.at[which, p], z, at.sib)
            for p in range(planes)
        ]
        for which, (src, land, size) in enumerate(((hwi, ri, half_i), (hwo, ro, half_o)))
    ]
    fetch_ga = [
        pltpu.make_async_copy(
            ga.at[pl.ds(g * ga_rows, ga_rows), :],
            hid.at[pl.ds(0, ga_rows), pl.ds(g * width, width)],
            gl.at[g],
        )
        for g in range(ga_groups)
    ]

    @pl.when(host)
    def _():
        turned = x[...].T
        for b in range(blocks):
            cols = slice(b * wide, (b + 1) * wide)
            hwi[:, cols] = dot(turned, dpre[:, cols], NN, BF)
        for copy in pair[0]:
            copy.start()
        for b in range(blocks):
            cols = slice(b * wide, (b + 1) * wide)
            hwo[cols, :] = dot(hid[:, cols], dy[...], TN, BF)
        for copy in pair[1]:
            copy.start()

    for copy in fetch_ga:
        copy.start()

    def dx_wait(step, carry):
        source = lax.rem(at.me + step, at.chips)
        rows_in = dxland.at[pl.ds(pl.multiple_of(source * padded, 8), padded), :]
        send_to(dxsend.at[source], rows_in, ts.at[0, source], tr.at[0, source], z, i).wait_recv()
        send_to(dgsend.at[source], dgland.at[source], ts.at[1, source], tr.at[1, source], z, i).wait_recv()
        return carry

    for copy in own_copies():
        copy.wait()
    lax.fori_loop(1, at.chips, dx_wait, 0)
    fetch_dx = pltpu.make_async_copy(dxland, landed_rows, yl.at[1])
    fetch_dx.start()
    fetch_dx.wait()

    aux_v = aux[...]
    gates = [aux_v[:, 0:1], aux_v[:, 1:2]]
    place = slot_places([aux_v[:, 2:3], aux_v[:, 3:4]], chips * padded)
    d_out = cot[...].astype(F32)
    d_act = dot(place[0] + place[1], landed_rows[...], NN)
    table = dgland[:, 0, :]
    d_gate = slot_values(aux_v, table, padded, chips)
    mean_gate = gates[0] * d_gate[0] + gates[1] * d_gate[1]
    route_iota = lax.broadcasted_iota(jnp.int32, (rows, nrouter), 1).astype(F32)
    d_logits = jnp.zeros((rows, nrouter), F32)
    for n in range(2):
        chosen = route_iota == aux_v[:, 4 + n:5 + n]
        d_logits = d_logits + jnp.where(chosen, gates[n] * (d_gate[n] - mean_gate), 0.0)
    d_logits = d_logits.astype(BF)
    small[0:nrouter, :] = dot(d_logits, act_two[...], TN)
    d_act = d_act + dot(d_logits, pk[0:nrouter, :], NN)
    gain_one = pk[nrouter:nrouter + 1, :].astype(F32)
    gain_two = pk[nrouter + 2:nrouter + 3, :].astype(F32)
    d_norm, g_gain, g_bias = norm_back(resid[...], gain_two, d_act)
    small[nrouter:nrouter + 16, :] = jnp.zeros((16, width), F32)
    small[nrouter + 2:nrouter + 3, :] = g_gain
    small[nrouter + 3:nrouter + 4, :] = g_bias
    d_res = d_out + d_norm
    dres[...] = d_res
    d_branch = d_res.astype(BF)
    half = width // 2
    for n in range(2):
        dsend[pairs + n] = d_branch[:, n * half:(n + 1) * half]
    datt[...] = dot(d_branch, wd[3], NT, BF)

    def d_copy(target):
        return send_to(dsend.at[target], gd.at[spot], sd.at[target], rd.at[spot], z, base + target)

    def d_near(target):
        return pltpu.make_async_copy(dsend.at[target], gd.at[spot], rd.at[spot])

    def d_start(target):
        far = spot != target
        pl.when(far)(d_copy(target).start)
        pl.when(jnp.logical_not(far))(d_near(target).start)

    for n in range(2):
        d_start(pairs + n)

    owner = 2 * at.chip + ce
    shipments = []

    def ship(p, which):
        src, dst = (part(hwi, half_i, p, core), wi.at[core]) if which == 0 else (part(hwo, half_o, p, core), wo.at[core])
        near = jnp.logical_and(z == p, core == ce)
        far_copy = send_to(src, dst, hs.at[p, which], hr.at[core, which], p, owner)
        near_copy = pltpu.make_async_copy(src, dst, hr.at[core, which])
        is_far = jnp.logical_and(host, jnp.logical_not(near))
        pl.when(is_far)(far_copy.start)
        pl.when(jnp.logical_and(host, near))(near_copy.start)
        shipments.append((is_far, far_copy))

    def add_pair(which, mine, theirs, size, chunk):
        @pl.when(host)
        def _():
            for copy in pair[which]:
                copy.wait_recv()

            def add(n, carry):
                low = pl.ds(pl.multiple_of(n * chunk, chunk), chunk)
                for p in range(planes):
                    here = pl.ds(pl.multiple_of((2 * p + core) * size + n * chunk, 16), chunk)
                    mine[here, :] = (
                        mine[here, :].astype(F32) + theirs[p, low, :].astype(F32)
                    ).astype(BF)
                return carry

            lax.fori_loop(0, size // chunk, add, 0)

    add_pair(0, hwi, ri, half_i, 16)
    for p in range(planes):
        ship(p, 0)

    lane = lax.broadcasted_iota(jnp.int32, (rows, 128), 1)
    masks = [(lane < HEAD).astype(F32).astype(BF), (lane >= HEAD).astype(F32).astype(BF)]
    score_scale = HEAD ** (-0.5)

    def head_pair(n, carry):
        cols = pl.ds(pl.multiple_of(n * 128, 128), 128)
        q2, k2, v2, da2 = q[:, cols], k[:, cols], v[:, cols], datt[:, cols]
        sums = [jnp.zeros((rows, 128), F32) for _ in range(3)]
        for side in range(2):
            mask = masks[side]
            da = da2 * mask
            p = probs[2 * n + side]
            dpb = dot(da, v2, NT)
            delta = jnp.sum(p * dpb, axis=-1, keepdims=True)
            ds = (p * (dpb - delta)).astype(BF)
            sums[0] += dot(ds, k2 * mask, NN)
            sums[1] += dot(ds, q2 * mask, TN)
            sums[2] += dot(p.astype(BF), da, TN)
        low = [(sums[0] * score_scale).astype(BF), (sums[1] * score_scale).astype(BF), sums[2].astype(BF)]
        for m, (value, full) in enumerate(zip(low, (dq, dk, dv))):
            dsend[n, :, m * 128:(m + 1) * 128] = value
            full[:, cols] = value
        d_start(n)
        return carry

    lax.fori_loop(0, pairs, head_pair, 0)

    d_one = dot(dq[...], wd[0], NT) + dot(dk[...], wd[1], NT) + dot(dv[...], wd[2], NT)
    d_norm, g_gain, g_bias = norm_back(tokens[...].astype(F32), gain_one, d_one)
    grad_tokens[...] = (dres[...] + d_norm).astype(BF)
    small[nrouter:nrouter + 1, :] = g_gain
    small[nrouter + 1:nrouter + 2, :] = g_bias

    hops = [at.sib, at.xn, at.yn]
    for n in range(upper):
        bit = 8 << n
        hops.append(i + bit - 2 * bit * lax.rem(lax.div(i, bit), 2))
    moves = [(z, t) for t in hops]
    for n in range(planes.bit_length() - 1):
        bit = 1 << n
        moves.append((z + bit - 2 * bit * lax.rem(lax.div(z, bit), 2), i))
    small_copies = []

    def small_start(n):
        if n >= 2:
            small_copies[n - 2].wait_send()
        sms[n % 2] = small[...]
        copy = send_to(sms.at[n % 2], smr.at[n], ms.at[n], mr.at[n], moves[n][0], moves[n][1])
        copy.start()
        small_copies.append(copy)

    def small_step(n):
        small_copies[n].wait_recv()
        small[...] = small[...] + smr[n]
        if n + 1 < len(moves):
            small_start(n + 1)

    small_start(0)
    add_pair(1, hwo, ro, half_o, 64)

    small_step(0)

    def d_wait(source, carry):
        send_to(gd.at[source], gd.at[source], sd.at[source], rd.at[source], z, i).wait_recv()
        return carry

    lax.fori_loop(0, 8, d_wait, 0)
    columns = gd.shape[2]
    total = jnp.zeros((width, columns), F32)
    sources = ga_rows // rows
    for g in range(ga_groups):
        fetch_ga[g].wait()
        total += dot(
            hid[0:ga_rows, g * width:(g + 1) * width],
            gd[g * sources:(g + 1) * sources].reshape(ga_rows, columns), TN,
        )
    gsum[...] = total.reshape(planes, width // planes, columns)
    small_step(1)
    tail = []
    for n in range(upper):
        szb[...] = gsum[...].astype(BF)
        copy = send_to(szb, rup.at[n], us.at[n], ur.at[n], z, hops[3 + n])
        copy.start()
        copy.wait_recv()
        gsum[...] = szb[...].astype(F32) + rup[n].astype(F32)
        copy.wait_send()
    szb[...] = gsum[...].astype(BF)
    for j in range(1, planes):
        zt = lax.rem(z + j, planes)
        copy = send_to(szb.at[zt], rzb.at[j - 1], zs.at[j - 1], zr.at[j - 1], zt, i)
        copy.start()
        tail.append(copy)
    for p in range(planes):
        ship(p, 1)
    small_step(2)

    def y_finish(step, carry):
        source = lax.rem(at.me + chips - step, chips)
        send_to(landing(source), landing(source), ys.at[step], yr.at[step], z, i).wait_recv()
        y_copy(step).wait_send()
        return carry

    y_own.wait()
    lax.fori_loop(1, chips, y_finish, 0)
    fetch = pltpu.make_async_copy(yland, landed_rows, yl.at[1])
    fetch.start()
    fetch.wait()
    y_all = landed_rows[...]
    mixed = gates[0] * dot(place[0], y_all, NN) + gates[1] * dot(place[1], y_all, NN)
    block_out[...] = (resid[...] + mixed).astype(BF)

    fin = gsum[z]
    for j in range(1, planes):
        send_to(rzb.at[j - 1], rzb.at[j - 1], zs.at[j - 1], zr.at[j - 1], z, i).wait_recv()
        fin = fin + rzb[j - 1].astype(F32)
    fb[spot] = fin.astype(BF)
    px, py = spot + 2 - 4 * at.xb, spot + 4 - 8 * at.yb
    pd = px + 4 - 8 * at.yb
    flip = 1 - 2 * core

    def pass_on(where, step, target):
        copy = send_to(fb.at[where], fb.at[where], gs.at[step], gr.at[step], z, target)
        copy.start()
        tail.append(copy)

    def landed(where, step):
        send_to(fb.at[where], fb.at[where], gs.at[step], gr.at[step], z, i).wait_recv()

    pass_on(spot, 0, at.xn)
    pass_on(spot, 1, at.yn)
    pass_on(spot, 2, at.sib)
    small_step(3)
    landed(px, 0)
    landed(py, 1)
    pass_on(px + core * (py - px), 3, at.yn + core * (at.xn - at.yn))
    pass_on(px, 4, at.sib)
    pass_on(py, 5, at.sib)
    for n in range(4, len(moves)):
        small_step(n)
    osmall[...] = small[...]
    landed(pd, 3)
    pass_on(pd, 6, at.sib)
    for h in range(2):
        send_to(wi.at[h], wi.at[h], hs.at[0, 0], hr.at[h, 0], z, i).wait_recv()
        send_to(wo.at[h], wo.at[h], hs.at[0, 1], hr.at[h, 1], z, i).wait_recv()
    landed(spot + flip, 2)
    landed(px + flip, 4)
    landed(py + flip, 5)
    landed(pd + flip, 6)
    for copy in tail + small_copies[-2:]:
        copy.wait_send()
    def d_sent(target, carry):
        pl.when(spot != target)(d_copy(target).wait_send)
        return carry

    lax.fori_loop(0, 8, d_sent, 0)

    @pl.when(host)
    def _():
        for copy in pair[0] + pair[1]:
            copy.wait_send()

    for is_far, copy in shipments:
        pl.when(is_far)(copy.wait_send)

    def dx_sent(step, carry):
        target = lax.rem(at.me + step, at.chips)
        for copy in copies(lax.div(target, per_plane), lax.rem(target, per_plane)):
            copy.wait_send()
        return carry

    lax.fori_loop(1, at.chips, dx_sent, 0)


def rear(planes, experts, nrouter, x, do, gate, tokens, cot, aux, act_two, q, k, v, resid, probs, wd, pk,
         win, wout, ga):
    rows, width = tokens.shape
    chips, padded, _ = x.shape
    slots = chips * padded
    ff = win.shape[1]
    pieces, blocks = (1, 4) if experts <= 8 else (2, 8)
    ga_groups = ff // width
    share, fshare, half = width // planes, ff // planes, width // 2
    upper = max(experts.bit_length() - 4, 1)
    nbits = experts.bit_length() - 1 + planes.bit_length() - 1
    dma = pltpu.SemaphoreType.DMA
    vm = pltpu.VMEM
    sds = jax.ShapeDtypeStruct
    return pl.pallas_call(
        functools.partial(rear_kernel, planes, experts, padded, pieces, blocks, ga_groups, nrouter),
        out_shape=(
            sds((rows, width), BF),
            sds((rows, width), BF),
            sds((8, share, half), BF),
            sds((nrouter + 16, width), F32),
            sds((2, share // 2, ff), BF),
            sds((2, fshare // 2, width), BF),
            sds((slots, width), BF),
            sds((slots, width), BF),
        ),
        in_specs=[vmem_spec()] * 14 + [any_spec()] * 3,
        out_specs=(vmem_spec(),) * 6 + (any_spec(),) * 2,
        scratch_shapes=[
            vm((width, ff), BF),
            vm((ff, width), BF),
            vm((slots, width), BF),
            vm((slots, ff), BF),
            vm((slots, ff), BF),
            vm((chips, padded, width), BF),
            vm((chips, 1, 128), F32),
            vm((chips, 1, 128), F32),
            vm((chips, padded, width), BF),
            vm((slots, width), BF),
            vm((8, rows, half), BF),
            vm((8, rows, half), BF),
            vm((rows, width), F32),
            vm((planes, share, half), F32),
            vm((planes, share, half), BF),
            vm((planes - 1, share, half), BF),
            vm((upper, planes, share, half) if experts > 8 else (1, 8, 128), BF),
            vm((2, nrouter + 16, width), F32),
            vm((nbits, nrouter + 16, width), F32),
            vm((nrouter + 16, width), F32),
            vm((planes, share // 2, ff), BF),
            vm((planes, fshare // 2, width), BF),
            dma((2,)), dma((2, chips)), dma((2, chips)), dma((2,)), dma((ga_groups,)),
            dma((2, planes)), dma((2, planes)),
            dma((planes, 2)), dma((2, 2)),
            dma((chips,)), dma((chips,)), dma((2,)),
            dma((8,)), dma((8,)),
            dma((upper,)), dma((upper,)),
            dma((planes - 1,)), dma((planes - 1,)),
            dma((7,)), dma((7,)), dma((nbits,)), dma((nbits,)),
        ],
        compiler_params=pltpu.CompilerParams(
            collective_id=2, has_side_effects=True, vmem_limit_bytes=REAR_LIMIT
        ),
        name="rear",
    )(x.reshape(slots, width), do.reshape(slots, width), gate, tokens, cot, aux, act_two, q, k, v,
      resid, probs, wd, pk, win, wout, ga.reshape(8 * rows, width))


def finish_kernel(planes, nrouter, block_out, grad_tokens, fb, small, wi, wo,
                  ob, ot, o0, o1, o2, o3, og, ov, ogi, ogo,
                  s0, s1, s2, s3, sg, sv, si, so, sem):
    z = lax.axis_index("dp")
    share = s0.shape[0]
    pairs = s0.shape[1] // 128
    half = s0.shape[1] // 2
    copies = []

    def write(source, target):
        copy = pltpu.make_async_copy(source, target, sem.at[len(copies)])
        copy.start()
        copies.append(copy)

    write(block_out, ob)
    write(grad_tokens, ot)
    for wide, low, out in ((si, wi, ogi), (so, wo, ogo)):
        chunk = low.shape[1]
        for h in range(2):
            wide[h * chunk:(h + 1) * chunk, :] = low[h].astype(F32)
            write(wide.at[pl.ds(h * chunk, chunk), :], out.at[pl.ds(h * chunk, chunk), :])
    for m, (stage, out) in enumerate(((s0, o0), (s1, o1), (s2, o2))):
        for n in range(pairs):
            stage[:, n * 128:(n + 1) * 128] = fb[n, :, m * 128:(m + 1) * 128].astype(F32)
        write(stage, out)
    for n in range(2):
        s3[:, n * half:(n + 1) * half] = fb[pairs + n].astype(F32)
    write(s3, o3)
    mine = small[:, 0:share]
    for p in range(1, planes):
        mine = jnp.where(z == p, small[:, p * share:(p + 1) * share], mine)
    sg[...] = mine[0:nrouter]
    write(sg, og)
    for n in range(4):
        sv[n] = mine[nrouter + n:nrouter + n + 1]
        write(sv.at[n], ov.at[n])
    for copy in copies:
        copy.wait()


def finish(planes, nrouter, block_out, grad_tokens, fb, small, wi, wo):
    rows, width = block_out.shape
    _, share, half = fb.shape
    ff = wi.shape[2]
    fshare = 2 * wo.shape[1]
    vm = pltpu.VMEM
    sds = jax.ShapeDtypeStruct
    flat = ((share, width),) * 4 + ((nrouter, share), (4, 1, share), (share, ff), (fshare, width))
    return pl.pallas_call(
        functools.partial(finish_kernel, planes, nrouter),
        out_shape=(sds((rows, width), BF),) * 2 + tuple(sds(shape, F32) for shape in flat),
        in_specs=[vmem_spec()] * 6,
        out_specs=(any_spec(),) * 10,
        scratch_shapes=[vm(shape, F32) for shape in flat] + [pltpu.SemaphoreType.DMA((16,))],
        compiler_params=pltpu.CompilerParams(vmem_limit_bytes=VMEM_LIMIT),
        name="finish",
    )(block_out, grad_tokens, fb, small, wi, wo)


def shards(planes, experts, tokens, segment_ids, routes, ln1_gain, ln1_bias, ln2_gain, ln2_bias,
           w_query, w_key, w_value, w_output, w_router, frozen_in, frozen_out, new_in, new_out,
           cotangent):
    rows, width = tokens.shape
    expert_count = w_router.shape[1]
    capacity = 5 * rows // (2 * expert_count)
    padded = -(-capacity // 8) * 8
    (wd, pk, win, wout, _, act_two, q, k, v, _, resid, probs, aux, ga, x_recv, do_recv, g_recv) = front(
        planes, experts, capacity, padded, expert_count, tokens, cotangent, segment_ids, routes,
        w_router, (ln1_gain, ln1_bias, ln2_gain, ln2_bias),
        w_query, w_key, w_value, w_output, frozen_in, frozen_out, new_in, new_out,
    )
    block_out, grad_tokens, dense, small, low_in, low_out, _, _ = rear(
        planes, experts, expert_count, x_recv, do_recv, g_recv, tokens, cotangent, aux, act_two, q, k, v,
        resid, probs, wd, pk, win, wout, ga,
    )
    block_out, grad_tokens, oq, ok, ov, ow, router, norms, ogi, ogo = finish(
        planes, expert_count, block_out, grad_tokens, dense, small, low_in, low_out
    )
    norms = norms.reshape(4, width // planes)
    return (
        block_out, grad_tokens, oq, ok, ov, ow, router.T,
        norms[0], norms[1], norms[2], norms[3], ogi[None], ogo[None],
    )


def solution(mesh):
    rows = P(("dp", "expert"), None)
    in_specs = (rows, rows, rows) + (P("dp"),) * 4 + (P("dp", None),) * 5
    in_specs += (P("expert", "dp", None),) * 4 + (rows,)
    out_specs = (rows, rows) + (P("dp", None),) * 5 + (P("dp"),) * 4
    out_specs += (P("expert", "dp", None),) * 2
    body = functools.partial(shards, mesh.shape["dp"], mesh.shape["expert"])
    return jax.shard_map(body, mesh=mesh, in_specs=in_specs, out_specs=out_specs, check_vma=False)
```

```python
import functools

import jax
import jax.numpy as jnp
from jax import lax
from jax.experimental import pallas as pl
from jax.experimental.pallas import tpu as pltpu
from jax.sharding import PartitionSpec as P

HEADS = 12
HEAD = 64
NORM_EPS = 1e-05
MASKED = -1e30
MESH = pl.DeviceIdType.MESH
BF = jnp.bfloat16
F32 = jnp.float32
VMEM_LIMIT = 60 * 1024 * 1024
REAR_LIMIT = 67043328


class Place:
    def __init__(self, planes, experts):
        self.planes, self.experts = planes, experts
        self.z = lax.axis_index("dp")
        self.i = lax.axis_index("expert")
        self.core = lax.rem(self.i, 2)
        self.chip = lax.div(self.i, 2)
        self.xb = lax.rem(self.chip, 2)
        self.yb = lax.rem(lax.div(self.i, 4), 2)
        self.sib = self.i + 1 - 2 * self.core
        self.xn = self.i + 2 - 4 * self.xb
        self.yn = self.i + 4 - 8 * self.yb
        self.chips = planes * (experts // 2)
        self.me = self.z * (experts // 2) + self.chip


def send_to(src, dst, send_sem, recv_sem, z, i):
    return pltpu.make_async_remote_copy(
        src_ref=src,
        dst_ref=dst,
        send_sem=send_sem,
        recv_sem=recv_sem,
        device_id={"dp": z, "expert": i},
        device_id_type=MESH,
    )


def greet(at):
    barrier = pltpu.get_barrier_semaphore()
    count = at.planes * at.experts
    own = at.z * at.experts + at.i

    def signal(step, carry):
        target = lax.rem(own + step, count)
        pl.semaphore_signal(
            barrier,
            inc=1,
            device_id={"dp": lax.div(target, at.experts), "expert": lax.rem(target, at.experts)},
            device_id_type=MESH,
        )
        return carry

    lax.fori_loop(1, count, signal, 0)
    return lambda: pl.semaphore_wait(barrier, count - 1)


def any_spec():
    return pl.BlockSpec(memory_space=pl.ANY)


def vmem_spec():
    return pl.BlockSpec(memory_space=pltpu.VMEM)


NN = ((1,), (0,))
NT = ((1,), (1,))
TN = ((0,), (0,))


def dot(left, right, contract, out=F32):
    return lax.dot_general(
        left, right, ((contract[0], contract[1]), ((), ())), preferred_element_type=F32
    ).astype(out)


def exact_dot(left, right, contract):
    return lax.dot_general(
        left, right, ((contract[0], contract[1]), ((), ())),
        preferred_element_type=F32, precision=lax.Precision.HIGHEST,
    )


def norm_parts(rows):
    centred = rows - jnp.mean(rows, axis=-1, keepdims=True)
    variance = jnp.mean(centred * centred, axis=-1, keepdims=True)
    scale = lax.rsqrt(variance + NORM_EPS)
    return centred * scale, scale


def norm_back(rows, gain, grad):
    unit, scale = norm_parts(rows)
    scaled = grad * gain
    inner = scaled - jnp.mean(scaled, axis=-1, keepdims=True)
    inner = inner - unit * jnp.mean(scaled * unit, axis=-1, keepdims=True)
    return scale * inner, jnp.sum(grad * unit, axis=0, keepdims=True), jnp.sum(grad, axis=0, keepdims=True)


def slot_places(slot, slots):
    lanes = lax.broadcasted_iota(jnp.int32, (slot[0].shape[0], slots), 1).astype(F32)
    return [(lanes == one).astype(F32).astype(BF) for one in slot]


def slot_values(aux, table, padded, chips):
    rows = aux.shape[0]
    low = lax.broadcasted_iota(jnp.int32, (rows, chips), 1).astype(F32) * padded
    lanes = lax.broadcasted_iota(jnp.int32, (rows, table.shape[1]), 1).astype(F32)
    found = []
    for k in range(2):
        slot = aux[:, 2 + k:3 + k]
        mine = jnp.logical_and(slot >= low, slot < low + padded).astype(F32)
        position = slot - jnp.sum(mine * low, axis=1, keepdims=True)
        picked = exact_dot(mine, table, NN)
        found.append(jnp.sum(jnp.where(lanes == position, picked, 0.0), axis=1, keepdims=True))
    return found


def front_kernel(planes, experts, capacity, padded, nrouter,
                 tokens, cot, segs, routes, router, g1, b1, g2, b2, wq, wk, wv, wo, fi, fo, ni, no,
                 owd, pk, win, wout, oact, oq, ok, ov, oresid, oprobs, aux, ga,
                 xland, dland, gland,
                 wd, act_one, act_two, q, k, v, att, resid, probs, packs, allow, xsend, esend, gsend, dstage, istage, ostage, ibf, obf,
                 ld, zs, zr, ps, pr, gs, gr, es, er, fs, fr, ts, tr, tl, sa, ra, sv):
    at = Place(planes, experts)
    z, i, core = at.z, at.i, at.core
    rows, width = tokens.shape
    chips = at.chips
    per_plane = experts // 2
    share = dstage.shape[1]
    quarter = share // 4
    half = width // 2
    fhalf = istage.shape[2] // 2
    oshare = ostage.shape[1]
    ohalf = oshare // 2
    pairs = width // 128
    spot = lax.rem(i, 8)
    base = i - spot
    loads = [pltpu.make_async_copy(w, dstage.at[m], ld.at[m]) for m, w in enumerate((wq, wk, wv, wo))]
    loads += [
        pltpu.make_async_copy(fi.at[0], istage.at[0], ld.at[4]),
        pltpu.make_async_copy(ni.at[0], istage.at[1], ld.at[5]),
        pltpu.make_async_copy(fo.at[0], ostage.at[0], ld.at[6]),
        pltpu.make_async_copy(no.at[0], ostage.at[1], ld.at[7]),
    ]
    for load in loads:
        load.start()
    met = greet(at)
    zrow = pl.multiple_of(z * share, share)
    for m in range(4):
        loads[m].wait()
        wd[m, pl.ds(zrow, share), :] = dstage[m].astype(BF)
    packs[z, 0:nrouter, :] = router[...].astype(BF)
    norm_row = lax.broadcasted_iota(jnp.int32, (16, share), 0)
    norms = jnp.zeros((16, share), F32)
    for n, values in enumerate((g1, b1, g2, b2)):
        norms = jnp.where(norm_row == n, values[...], norms)
    packs[z, nrouter:nrouter + 16, :] = norms.astype(BF)
    met()

    def block(plane, row_quarter, column_half):
        return wd.at[
            :,
            pl.ds(pl.multiple_of(plane * share + row_quarter * quarter, 16), quarter),
            pl.ds(pl.multiple_of(column_half * half, 128), half),
        ]

    rq = 2 * at.yb + core
    rqy = 2 * (1 - at.yb) + core
    rqs = 2 * at.yb + 1 - core
    rqys = 2 * (1 - at.yb) + 1 - core
    xb, xo = at.xb, 1 - at.xb
    started = []
    for j in range(1, planes):
        zt = lax.rem(z + j, planes)
        mine = block(z, rq, xb)
        copy = send_to(mine, mine, zs.at[j - 1], zr.at[j - 1], zt, i)
        copy.start()
        started.append(copy)
        copy = send_to(packs.at[z], packs.at[z], ps.at[j - 1], pr.at[j - 1], zt, i)
        copy.start()
        started.append(copy)

    def cast(source, target, kind, chunk):
        def step(n, carry):
            part = pl.ds(pl.multiple_of(n * chunk, chunk), chunk)
            target[kind, part, :] = source[kind, part, :].astype(BF)
            return carry

        lax.fori_loop(0, source.shape[1] // chunk, step, 0)

    def in_block(plane, h):
        return win.at[
            pl.ds(pl.multiple_of(plane * share, 16), share),
            pl.ds(pl.multiple_of(h * fhalf, 128), fhalf),
        ]

    def out_block(plane, h):
        return wout.at[pl.ds(pl.multiple_of(plane * oshare + h * ohalf, 16), ohalf), :]

    remote_sends = []

    def ship(kind, h, which):
        zh = 3 * core if kind == 0 else 1 + core
        remote = jnp.logical_or(zh != z, core != h)
        src = (
            ibf.at[kind, :, pl.ds(h * fhalf, fhalf)]
            if which == 0
            else obf.at[kind, pl.ds(h * ohalf, ohalf), :]
        )
        dst = in_block(z, h) if which == 0 else out_block(z, h)
        far = send_to(src, dst, es.at[kind, h, which], er.at[z, which], zh, 2 * at.chip + h)
        near = pltpu.make_async_copy(src, dst, er.at[z, which])
        pl.when(remote)(far.start)
        pl.when(jnp.logical_not(remote))(near.start)
        remote_sends.append((remote, far))

    for n, kind in ((4, 0), (5, 1)):
        loads[n].wait()
        cast(istage, ibf, kind, 16)
        for h in range(2):
            ship(kind, h, 0)

    shift = experts.bit_length() - 1
    above = lax.broadcasted_iota(jnp.int32, (rows, rows), 0)
    across = lax.broadcasted_iota(jnp.int32, (rows, rows), 1)
    segment = segs[...].astype(F32)
    fact_row = lax.broadcasted_iota(jnp.int32, (8, rows), 0)
    facts = jnp.zeros((8, rows), F32)
    for n, values in enumerate((routes[0:1, :].astype(F32), routes[1:2, :].astype(F32), segment)):
        facts = jnp.where(fact_row == n, values, facts)
    fact_columns = dot((above == across).astype(F32).astype(BF), facts.astype(BF), NT)
    route_columns = [fact_columns[:, n:n + 1] for n in range(2)]
    route = fact_columns.astype(jnp.int32)
    expert = jnp.bitwise_and(route, experts - 1)
    kind = jnp.right_shift(route, shift)
    host_plane = jnp.where(jnp.bitwise_and(expert, 1) == 0, kind, 3 - kind)
    host = host_plane * per_plane + jnp.right_shift(expert, 1)
    chip_iota = lax.broadcasted_iota(jnp.int32, (rows, chips), 1)
    chosen = [(chip_iota == host[:, n:n + 1]).astype(F32) for n in range(2)]
    earlier = (across < above).astype(F32).astype(BF)
    before = dot(earlier, (chosen[0] + chosen[1]).astype(BF), NN)
    position = [jnp.sum(one * before, axis=1, keepdims=True) for one in chosen]
    slot = [
        jnp.where(position[n] < capacity, host[:, n:n + 1].astype(F32) * padded + position[n], -1.0)
        for n in range(2)
    ]
    place = slot_places(slot, chips * padded)
    both = place[0] + place[1]

    def fill(target, values):
        sent = dot(both, values, TN)
        for n in range(chips):
            target[n] = sent[n * padded:(n + 1) * padded].astype(BF)

    def token_copy(src, dst, which, step):
        target = lax.rem(at.me + step, chips)
        zt, it = lax.div(target, per_plane), 2 * lax.rem(target, per_plane) + core
        return send_to(src.at[target], dst.at[at.me], ts.at[which, step], tr.at[which, step], zt, it)

    def token_start(src, dst, which):
        pltpu.make_async_copy(src.at[at.me], dst.at[at.me], tl.at[which]).start()

        def step(n, carry):
            token_copy(src, dst, which, n).start()
            return carry

        lax.fori_loop(1, chips, step, 0)

    def token_finish(src, dst, which):
        def step(n, carry):
            source = lax.rem(at.me + chips - n, chips)
            send_to(
                src.at[source], dst.at[source], ts.at[which, n], tr.at[which, n], z, i
            ).wait_recv()
            token_copy(src, dst, which, n).wait_send()
            return carry

        lax.fori_loop(1, chips, step, 0)
        pltpu.make_async_copy(src.at[at.me], dst.at[at.me], tl.at[which]).wait()

    fill(esend, cot[...])
    token_start(esend, dland, 0)
    for n, kind in ((6, 0), (7, 1)):
        loads[n].wait()
        cast(ostage, obf, kind, 32)
        for h in range(2):
            ship(kind, h, 1)
    same = jnp.logical_and(fact_columns[:, 2:3] == segment, across <= above)
    allow[...] = same.astype(F32)

    def pass_on(src, j, step, target):
        copy = send_to(src, src, gs.at[j - 1, step], gr.at[j - 1, step], z, target)
        copy.start()
        started.append(copy)

    def landed(dst, j, step):
        send_to(dst, dst, gs.at[j - 1, step], gr.at[j - 1, step], z, i).wait_recv()

    for j in range(1, planes):
        zz = lax.rem(z + planes - j, planes)
        mine = block(zz, rq, xb)
        send_to(mine, mine, zs.at[j - 1], zr.at[j - 1], z, i).wait_recv()
        pass_on(mine, j, 0, at.xn)
        pass_on(mine, j, 1, at.yn)
        pass_on(mine, j, 2, at.sib)
        send_to(packs.at[zz], packs.at[zz], ps.at[j - 1], pr.at[j - 1], z, i).wait_recv()
    pk[...] = jnp.concatenate([packs[p] for p in range(planes)], axis=1)

    x = tokens[...].astype(F32)
    gain = pk[nrouter:nrouter + 1, :].astype(F32)
    bias = pk[nrouter + 1:nrouter + 2, :].astype(F32)
    act_one[...] = (norm_parts(x)[0] * gain + bias).astype(BF)

    for j in range(1, planes):
        zz = lax.rem(z + planes - j, planes)
        bx, by = block(zz, rq, xo), block(zz, rqy, xb)
        landed(bx, j, 0)
        landed(by, j, 1)
        onward = block(zz, rq + core * (rqy - rq), xo + core * (xb - xo))
        pass_on(onward, j, 3, at.yn + core * (at.xn - at.yn))
        pass_on(bx, j, 4, at.sib)
        pass_on(by, j, 5, at.sib)
    for j in range(1, planes):
        zz = lax.rem(z + planes - j, planes)
        bd = block(zz, rqy, xo)
        landed(bd, j, 3)
        pass_on(bd, j, 6, at.sib)
    for j in range(1, planes):
        zz = lax.rem(z + planes - j, planes)
        landed(block(zz, rqs, xb), j, 2)
        landed(block(zz, rqs, xo), j, 4)
        landed(block(zz, rqys, xb), j, 5)
        landed(block(zz, rqys, xo), j, 6)

    def act_copy(step, whole):
        target = lax.rem(spot + step, 8)
        src = act_one if whole else att
        return target, send_to(src, ga.at[spot], sa.at[step], ra.at[step], z, base + target)

    def act_near(whole):
        return pltpu.make_async_copy(act_one if whole else att, ga.at[spot], tl.at[3])

    for step in range(1, 8):
        target, copy = act_copy(step, True)
        pl.when(target < pairs)(copy.start)
    pl.when(spot < pairs)(act_near(True).start)

    one = act_one[...]
    q[...] = dot(one, wd[0], NN, BF)
    k[...] = dot(one, wd[1], NN, BF)
    v[...] = dot(one, wd[2], NN, BF)
    lane = lax.broadcasted_iota(jnp.int32, (rows, 128), 1)
    masks = [(lane < HEAD).astype(F32).astype(BF), (lane >= HEAD).astype(F32).astype(BF)]
    score_scale = HEAD ** (-0.5)

    def head_pair(n, carry):
        cols = pl.ds(pl.multiple_of(n * 128, 128), 128)
        q2, k2, v2 = q[:, cols], k[:, cols], v[:, cols]
        total = jnp.zeros((rows, 128), F32)
        for side in range(2):
            scores = dot(q2 * masks[side], k2, NT) * score_scale
            scores = jnp.where(allow[...] > 0.5, scores, MASKED)
            expo = jnp.exp(scores - jnp.max(scores, axis=-1, keepdims=True))
            p = expo / jnp.sum(expo, axis=-1, keepdims=True)
            probs[2 * n + side] = p
            total += dot(p.astype(BF), v2 * masks[side], NN)
        att[:, cols] = total.astype(BF)
        return carry

    lax.fori_loop(0, pairs, head_pair, 0)
    residual = x + dot(att[...], wd[3], NN)
    resid[...] = residual
    gain = pk[nrouter + 2:nrouter + 3, :].astype(F32)
    bias = pk[nrouter + 3:nrouter + 4, :].astype(F32)
    two = (norm_parts(residual)[0] * gain + bias).astype(BF)
    act_two[...] = two
    fill(xsend, two)
    token_start(xsend, xland, 1)
    for step in range(1, 8):
        target, copy = act_copy(step, False)
        pl.when(target >= pairs)(copy.start)
    pl.when(spot >= pairs)(act_near(False).start)

    logits = dot(two, pk[0:nrouter, :], NT)
    route_iota = lax.broadcasted_iota(jnp.int32, (rows, nrouter), 1)
    picked = [
        jnp.sum(jnp.where(route_iota == route[:, n:n + 1], logits, 0.0), axis=1, keepdims=True)
        for n in range(2)
    ]
    top = jnp.maximum(picked[0], picked[1])
    lifted = [jnp.exp(one_pick - top) for one_pick in picked]
    gates = [one_lift / (lifted[0] + lifted[1]) for one_lift in lifted]
    values = jnp.zeros((rows, 128), F32)
    for n, column in enumerate(gates + slot + route_columns):
        values = jnp.where(lane == n, column, values)
    aux[...] = values
    lanes = lane.astype(F32)
    table = jnp.zeros((chips, 128), F32)
    for n in range(2):
        kept = jnp.logical_and(lanes == position[n], position[n] < capacity)
        table += exact_dot(chosen[n], jnp.where(kept, gates[n], 0.0), TN)
    for n in range(chips):
        gsend[n] = table[n:n + 1]
    token_start(gsend, gland, 2)
    kept_arrays = ((wd, owd), (act_two, oact), (q, oq), (k, ok), (v, ov), (resid, oresid), (probs, oprobs))
    saves = [pltpu.make_async_copy(src, dst, sv.at[n]) for n, (src, dst) in enumerate(kept_arrays)]
    for copy in saves:
        copy.start()

    def hand_on(plane, which):
        blk = in_block(plane, core) if which == 0 else out_block(plane, core)
        send_to(blk, blk, es.at[0, 0, which], er.at[plane, which], z, i).wait_recv()
        copy = send_to(blk, blk, fs.at[plane, which], fr.at[plane, which], z, at.sib)
        copy.start()
        started.append(copy)

    for which in range(2):
        for plane in range(planes):
            hand_on(plane, which)
    for src, dst, which in ((esend, dland, 0), (xsend, xland, 1), (gsend, gland, 2)):
        token_finish(src, dst, which)
    for step in range(1, 8):
        source = lax.rem(spot + 8 - step, 8)
        send_to(act_one, ga.at[source], sa.at[step], ra.at[step], z, i).wait_recv()
        act_copy(step, True)[1].wait_send()
    act_near(True).wait()
    for which in range(2):
        for plane in range(planes):
            blk = in_block(plane, 1 - core) if which == 0 else out_block(plane, 1 - core)
            send_to(blk, blk, fs.at[plane, which], fr.at[plane, which], z, i).wait_recv()
    for copy in started:
        copy.wait_send()
    for remote, far in remote_sends:
        pl.when(remote)(far.wait_send)
    for copy in saves:
        copy.wait()


def front(planes, experts, capacity, padded, nrouter, tokens, cot, segment_ids, routes, router, norms,
          wq, wk, wv, wo, fi, fo, ni, no):
    rows, width = tokens.shape
    share = wq.shape[0]
    ff = fi.shape[2]
    oshare = fo.shape[1]
    chips = planes * experts // 2
    dma = pltpu.SemaphoreType.DMA
    vm = pltpu.VMEM
    sds = jax.ShapeDtypeStruct
    flat = sds((rows, width), BF)
    slab = sds((chips, padded, width), BF)
    return pl.pallas_call(
        functools.partial(front_kernel, planes, experts, capacity, padded, nrouter),
        out_shape=(
            sds((4, width, width), BF),
            sds((nrouter + 16, width), BF),
            sds((width, ff), BF),
            sds((ff, width), BF),
            flat, flat, flat, flat,
            sds((rows, width), F32),
            sds((HEADS, rows, rows), F32),
            sds((rows, 128), F32),
            sds((8, rows, width), BF),
            slab,
            slab,
            sds((chips, 1, 128), F32),
        ),
        in_specs=[vmem_spec()] * 9 + [any_spec()] * 8,
        out_specs=(any_spec(), vmem_spec()) + (any_spec(),) * 8 + (vmem_spec(),) + (any_spec(),) * 4,
        scratch_shapes=[
            vm((4, width, width), BF),
        ] + [vm((rows, width), BF)] * 6 + [
            vm((rows, width), F32),
            vm((HEADS, rows, rows), F32),
            vm((planes, nrouter + 16, share), BF),
            vm((rows, rows), F32),
            vm((chips, padded, width), BF),
            vm((chips, padded, width), BF),
            vm((chips, 1, 128), F32),
            vm((4, share, width), F32),
            vm((2, share, ff), F32),
            vm((2, oshare, width), F32),
            vm((2, share, ff), BF),
            vm((2, oshare, width), BF),
            dma((8,)),
            dma((planes - 1,)), dma((planes - 1,)), dma((planes - 1,)), dma((planes - 1,)),
            dma((planes - 1, 7)), dma((planes - 1, 7)),
            dma((2, 2, 2)), dma((planes, 2)), dma((planes, 2)), dma((planes, 2)),
            dma((3, chips)), dma((3, chips)), dma((4,)), dma((8,)), dma((8,)), dma((7,)),
        ],
        compiler_params=pltpu.CompilerParams(
            collective_id=0, has_side_effects=True, vmem_limit_bytes=VMEM_LIMIT
        ),
        name="front",
    )(tokens, cot, segment_ids, routes.T, router.T, *[norm.reshape(1, share) for norm in norms],
      wq, wk, wv, wo, fi, fo, ni, no)


GELU_SCALE = 0.7978845608028654
GELU_CUBE = 0.044715


def rear_kernel(planes, experts, padded, pieces, blocks, ga_groups, nrouter,
                x, do, gate, *refs):
    back_in, refs = refs[:11], refs[11:]
    (win, wout, ga,
                block_out, grad_tokens, fb, osmall, wi, wo, yland, dxland,
                tokens, cot, aux, act_two, q, k, v, resid, probs, wd, pk,
                hwi, hwo, dy, hid, dpre, dxsend, dgsend, dgland, ysend, landed_rows,
                gd, dsend, dres, gsum, szb, rzb, rup,
                sms, smr, small, ri, ro,
                ls, ts, tr, tl, gl,
                es, er, hs, hr, ys, yr, yl, sd, rd, us, ur, zs, zr, gs, gr, ms, mr, lb) = refs
    back_held = (tokens, cot, aux, act_two, q, k, v, resid, probs, wd, pk)
    back_loads = [
        pltpu.make_async_copy(src, dst, lb.at[n]) for n, (src, dst) in enumerate(zip(back_in, back_held))
    ]
    at = Place(planes, experts)
    z, i, core = at.z, at.i, at.core
    chips = at.chips
    per_plane = experts // 2
    rows, width = tokens.shape
    pairs = width // 128
    spot = lax.rem(i, 8)
    base = i - spot
    upper = rup.shape[0] if experts > 8 else 0
    ga_rows = 8 * rows // ga_groups
    datt, dq, dk, dv = [dpre.at[pl.ds(0, rows), pl.ds(n * width, width)] for n in range(4)]
    chunk = per_plane * padded // pieces
    batch = per_plane // pieces
    ff = hwi.shape[1]
    wide = ff // blocks
    load_i = pltpu.make_async_copy(win, hwi, ls.at[0])
    load_o = pltpu.make_async_copy(wout, hwo, ls.at[1])
    load_i.start()
    load_o.start()
    met = greet(at)
    diagonal = lax.broadcasted_iota(jnp.int32, (padded, 128), 1) == lax.broadcasted_iota(jnp.int32, (padded, 128), 0)
    load_i.wait()
    load_o.wait()
    for copy in back_loads:
        copy.start()
    met()

    def copies(plane, n):
        target = plane * per_plane + n
        there = 2 * n + core
        rows_in = dxland.at[pl.ds(pl.multiple_of(at.me * padded, 8), padded), :]
        return [
            send_to(dxsend.at[target], rows_in, ts.at[0, target], tr.at[0, at.me], plane, there),
            send_to(dgsend.at[target], dgland.at[at.me], ts.at[1, target], tr.at[1, at.me], plane, there),
        ]

    def own_copies():
        rows_in = dxland.at[pl.ds(pl.multiple_of(at.me * padded, 8), padded), :]
        return [
            pltpu.make_async_copy(dxsend.at[at.me], rows_in, tl.at[0]),
            pltpu.make_async_copy(dgsend.at[at.me], dgland.at[at.me], tl.at[1]),
        ]

    def work(plane, piece):
        first = plane * per_plane + piece * batch
        span = pl.ds(pl.multiple_of((plane * pieces + piece) * chunk, 16), chunk)
        x_c = x[span, :]
        do_c = do[span, :].astype(F32)
        column = jnp.concatenate(
            [
                jnp.sum(jnp.where(diagonal, gate[first + n], 0.0), axis=1, keepdims=True)
                for n in range(batch)
            ],
            axis=0,
        )
        dy_c = (do_c * column).astype(BF)
        dy[span, :] = dy_c
        y_sum = jnp.zeros((chunk, width), F32)
        dx_sum = jnp.zeros((chunk, width), F32)
        for b in range(blocks):
            cols = slice(b * wide, (b + 1) * wide)
            u = dot(x_c, hwi[:, cols], NN)
            dz = dot(dy_c, hwo[cols, :], NT)
            square = u * u
            bent = jnp.tanh(GELU_SCALE * (u + GELU_CUBE * (square * u)))
            cdf = 0.5 * (1.0 + bent)
            slope = cdf + (0.5 * GELU_SCALE) * u * (1.0 - bent * bent) * (1.0 + 3.0 * GELU_CUBE * square)
            hidden = (u * cdf).astype(BF)
            d_pre = (dz * slope).astype(BF)
            hid[span, cols] = hidden
            dpre[span, cols] = d_pre
            y_sum += dot(hidden, hwo[cols, :], NN)
            dx_sum += dot(d_pre, hwi[:, cols], NT)
        y_low = y_sum.astype(BF)
        d_gate = jnp.sum(y_low.astype(F32) * do_c, axis=1, keepdims=True)
        for n in range(batch):
            part = slice(n * padded, (n + 1) * padded)
            source = first + n
            ysend[source] = y_sum[part].astype(BF)
            dxsend[source] = dx_sum[part].astype(BF)
            dgsend[source] = jnp.sum(jnp.where(diagonal, d_gate[part], 0.0), axis=0, keepdims=True)

    def far_plane(turn):
        half = 1 - 2 * lax.rem(z, 2)
        other = lax.rem(z + 2, planes)
        return jnp.where(turn == 0, other, jnp.where(turn == 1, planes - 1 - z, z + half))

    def remote_turn(turn, carry):
        plane = far_plane(lax.div(turn, pieces))
        piece = lax.rem(turn, pieces)
        work(plane, piece)
        for n in range(batch):
            for copy in copies(plane, piece * batch + n):
                copy.start()
        return carry

    lax.fori_loop(0, (planes - 1) * pieces, remote_turn, 0)
    for piece in range(pieces):
        work(z, piece)
    for copy in own_copies():
        copy.start()
    for n in range(per_plane):
        for copy in copies(z, n):
            pl.when(at.chip != n)(copy.start)

    def landing(source):
        return yland.at[pl.ds(pl.multiple_of(source * padded, 8), padded), :]

    def y_copy(step):
        target = lax.rem(at.me + step, chips)
        zt, it = lax.div(target, per_plane), 2 * lax.rem(target, per_plane) + core
        return send_to(ysend.at[target], landing(at.me), ys.at[step], yr.at[step], zt, it)

    def y_start(step, carry):
        y_copy(step).start()
        return carry

    y_own = pltpu.make_async_copy(ysend.at[at.me], landing(at.me), yl.at[0])
    y_own.start()
    lax.fori_loop(1, chips, y_start, 0)

    ce = z - 1
    host = jnp.logical_and(z >= 1, z <= 2)
    half_i, half_o = width // planes // 2, ff // planes // 2

    def part(source, size, p, c):
        return source.at[pl.ds(pl.multiple_of((2 * p + c) * size, 16), size), :]

    pair = [
        [
            send_to(part(src, size, p, 1 - core), land.at[p], es.at[which, p], er.at[which, p], z, at.sib)
            for p in range(planes)
        ]
        for which, (src, land, size) in enumerate(((hwi, ri, half_i), (hwo, ro, half_o)))
    ]
    fetch_ga = [
        pltpu.make_async_copy(
            ga.at[pl.ds(g * ga_rows, ga_rows), :],
            hid.at[pl.ds(0, ga_rows), pl.ds(g * width, width)],
            gl.at[g],
        )
        for g in range(ga_groups)
    ]

    @pl.when(host)
    def _():
        turned = x[...].T
        for b in range(blocks):
            cols = slice(b * wide, (b + 1) * wide)
            hwi[:, cols] = dot(turned, dpre[:, cols], NN, BF)
        for copy in pair[0]:
            copy.start()
        for b in range(blocks):
            cols = slice(b * wide, (b + 1) * wide)
            hwo[cols, :] = dot(hid[:, cols], dy[...], TN, BF)
        for copy in pair[1]:
            copy.start()

    for copy in fetch_ga:
        copy.start()

    owner = 2 * at.chip + ce
    shipments = []

    def ship(p, which):
        src, dst = (part(hwi, half_i, p, core), wi.at[core]) if which == 0 else (part(hwo, half_o, p, core), wo.at[core])
        near = jnp.logical_and(z == p, core == ce)
        far_copy = send_to(src, dst, hs.at[p, which], hr.at[core, which], p, owner)
        near_copy = pltpu.make_async_copy(src, dst, hr.at[core, which])
        is_far = jnp.logical_and(host, jnp.logical_not(near))
        pl.when(is_far)(far_copy.start)
        pl.when(jnp.logical_and(host, near))(near_copy.start)
        shipments.append((is_far, far_copy))

    def add_pair(which, mine, theirs, size, chunk):
        @pl.when(host)
        def _():
            for copy in pair[which]:
                copy.wait_recv()

            def add(n, carry):
                low = pl.ds(pl.multiple_of(n * chunk, chunk), chunk)
                for p in range(planes):
                    here = pl.ds(pl.multiple_of((2 * p + core) * size + n * chunk, 16), chunk)
                    mine[here, :] = (
                        mine[here, :].astype(F32) + theirs[p, low, :].astype(F32)
                    ).astype(BF)
                return carry

            lax.fori_loop(0, size // chunk, add, 0)

    add_pair(0, hwi, ri, half_i, 16)
    for p in range(planes):
        ship(p, 0)
    add_pair(1, hwo, ro, half_o, 64)
    for p in (0, 3):
        ship(p, 1)

    def dx_wait(step, carry):
        source = lax.rem(at.me + step, at.chips)
        rows_in = dxland.at[pl.ds(pl.multiple_of(source * padded, 8), padded), :]
        send_to(dxsend.at[source], rows_in, ts.at[0, source], tr.at[0, source], z, i).wait_recv()
        send_to(dgsend.at[source], dgland.at[source], ts.at[1, source], tr.at[1, source], z, i).wait_recv()
        return carry

    for copy in own_copies():
        copy.wait()
    lax.fori_loop(1, at.chips, dx_wait, 0)
    fetch_dx = pltpu.make_async_copy(dxland, landed_rows, yl.at[1])
    fetch_dx.start()
    fetch_dx.wait()

    for copy in back_loads:
        copy.wait()

    aux_v = aux[...]
    gates = [aux_v[:, 0:1], aux_v[:, 1:2]]
    place = slot_places([aux_v[:, 2:3], aux_v[:, 3:4]], chips * padded)
    d_out = cot[...].astype(F32)
    d_act = dot(place[0] + place[1], landed_rows[...], NN)
    table = dgland[:, 0, :]
    d_gate = slot_values(aux_v, table, padded, chips)
    mean_gate = gates[0] * d_gate[0] + gates[1] * d_gate[1]
    route_iota = lax.broadcasted_iota(jnp.int32, (rows, nrouter), 1).astype(F32)
    d_logits = jnp.zeros((rows, nrouter), F32)
    for n in range(2):
        chosen = route_iota == aux_v[:, 4 + n:5 + n]
        d_logits = d_logits + jnp.where(chosen, gates[n] * (d_gate[n] - mean_gate), 0.0)
    d_logits = d_logits.astype(BF)
    small[0:nrouter, :] = dot(d_logits, act_two[...], TN)
    d_act = d_act + dot(d_logits, pk[0:nrouter, :], NN)
    gain_one = pk[nrouter:nrouter + 1, :].astype(F32)
    gain_two = pk[nrouter + 2:nrouter + 3, :].astype(F32)
    d_norm, g_gain, g_bias = norm_back(resid[...], gain_two, d_act)
    small[nrouter:nrouter + 16, :] = jnp.zeros((16, width), F32)
    small[nrouter + 2:nrouter + 3, :] = g_gain
    small[nrouter + 3:nrouter + 4, :] = g_bias
    d_res = d_out + d_norm
    dres[...] = d_res
    d_branch = d_res.astype(BF)
    half = width // 2
    for n in range(2):
        dsend[pairs + n] = d_branch[:, n * half:(n + 1) * half]
    datt[...] = dot(d_branch, wd[3], NT, BF)

    def d_copy(target):
        return send_to(dsend.at[target], gd.at[spot], sd.at[target], rd.at[spot], z, base + target)

    def d_near(target):
        return pltpu.make_async_copy(dsend.at[target], gd.at[spot], rd.at[spot])

    def d_start(target):
        far = spot != target
        pl.when(far)(d_copy(target).start)
        pl.when(jnp.logical_not(far))(d_near(target).start)

    for n in range(2):
        d_start(pairs + n)

    lane = lax.broadcasted_iota(jnp.int32, (rows, 128), 1)
    masks = [(lane < HEAD).astype(F32).astype(BF), (lane >= HEAD).astype(F32).astype(BF)]
    score_scale = HEAD ** (-0.5)

    def head_pair(n, carry):
        cols = pl.ds(pl.multiple_of(n * 128, 128), 128)
        q2, k2, v2, da2 = q[:, cols], k[:, cols], v[:, cols], datt[:, cols]
        sums = [jnp.zeros((rows, 128), F32) for _ in range(3)]
        for side in range(2):
            mask = masks[side]
            da = da2 * mask
            p = probs[2 * n + side]
            dpb = dot(da, v2, NT)
            delta = jnp.sum(p * dpb, axis=-1, keepdims=True)
            ds = (p * (dpb - delta)).astype(BF)
            sums[0] += dot(ds, k2 * mask, NN)
            sums[1] += dot(ds, q2 * mask, TN)
            sums[2] += dot(p.astype(BF), da, TN)
        low = [(sums[0] * score_scale).astype(BF), (sums[1] * score_scale).astype(BF), sums[2].astype(BF)]
        for m, (value, full) in enumerate(zip(low, (dq, dk, dv))):
            dsend[n, :, m * 128:(m + 1) * 128] = value
            full[:, cols] = value
        d_start(n)
        return carry

    lax.fori_loop(0, pairs, head_pair, 0)

    d_one = dot(dq[...], wd[0], NT) + dot(dk[...], wd[1], NT) + dot(dv[...], wd[2], NT)
    d_norm, g_gain, g_bias = norm_back(tokens[...].astype(F32), gain_one, d_one)
    grad_tokens[...] = (dres[...] + d_norm).astype(BF)
    small[nrouter:nrouter + 1, :] = g_gain
    small[nrouter + 1:nrouter + 2, :] = g_bias

    hops = [at.sib, at.xn, at.yn]
    for n in range(upper):
        bit = 8 << n
        hops.append(i + bit - 2 * bit * lax.rem(lax.div(i, bit), 2))
    moves = [(z, t) for t in hops]
    for n in range(planes.bit_length() - 1):
        bit = 1 << n
        moves.append((z + bit - 2 * bit * lax.rem(lax.div(z, bit), 2), i))
    small_copies = []

    def small_start(n):
        if n >= 2:
            small_copies[n - 2].wait_send()
        sms[n % 2] = small[...]
        copy = send_to(sms.at[n % 2], smr.at[n], ms.at[n], mr.at[n], moves[n][0], moves[n][1])
        copy.start()
        small_copies.append(copy)

    def small_step(n):
        small_copies[n].wait_recv()
        small[...] = small[...] + smr[n]
        if n + 1 < len(moves):
            small_start(n + 1)

    small_start(0)

    small_step(0)

    def d_wait(source, carry):
        send_to(gd.at[source], gd.at[source], sd.at[source], rd.at[source], z, i).wait_recv()
        return carry

    lax.fori_loop(0, 8, d_wait, 0)
    columns = gd.shape[2]
    total = jnp.zeros((width, columns), F32)
    sources = ga_rows // rows
    for g in range(ga_groups):
        fetch_ga[g].wait()
        total += dot(
            hid[0:ga_rows, g * width:(g + 1) * width],
            gd[g * sources:(g + 1) * sources].reshape(ga_rows, columns), TN,
        )
    gsum[...] = total.reshape(planes, width // planes, columns)
    small_step(1)
    tail = []
    for n in range(upper):
        szb[...] = gsum[...].astype(BF)
        copy = send_to(szb, rup.at[n], us.at[n], ur.at[n], z, hops[3 + n])
        copy.start()
        copy.wait_recv()
        gsum[...] = szb[...].astype(F32) + rup[n].astype(F32)
        copy.wait_send()
    szb[...] = gsum[...].astype(BF)
    for j in range(1, planes):
        zt = lax.rem(z + j, planes)
        copy = send_to(szb.at[zt], rzb.at[j - 1], zs.at[j - 1], zr.at[j - 1], zt, i)
        copy.start()
        tail.append(copy)
    for p in (1, 2):
        ship(p, 1)
    small_step(2)

    def y_finish(step, carry):
        source = lax.rem(at.me + chips - step, chips)
        send_to(landing(source), landing(source), ys.at[step], yr.at[step], z, i).wait_recv()
        y_copy(step).wait_send()
        return carry

    y_own.wait()
    lax.fori_loop(1, chips, y_finish, 0)
    fetch = pltpu.make_async_copy(yland, landed_rows, yl.at[1])
    fetch.start()
    fetch.wait()
    y_all = landed_rows[...]
    mixed = gates[0] * dot(place[0], y_all, NN) + gates[1] * dot(place[1], y_all, NN)
    block_out[...] = (resid[...] + mixed).astype(BF)

    fin = gsum[z]
    for j in range(1, planes):
        send_to(rzb.at[j - 1], rzb.at[j - 1], zs.at[j - 1], zr.at[j - 1], z, i).wait_recv()
        fin = fin + rzb[j - 1].astype(F32)
    fb[spot] = fin.astype(BF)
    px, py = spot + 2 - 4 * at.xb, spot + 4 - 8 * at.yb
    pd = px + 4 - 8 * at.yb
    flip = 1 - 2 * core

    def pass_on(where, step, target):
        copy = send_to(fb.at[where], fb.at[where], gs.at[step], gr.at[step], z, target)
        copy.start()
        tail.append(copy)

    def landed(where, step):
        send_to(fb.at[where], fb.at[where], gs.at[step], gr.at[step], z, i).wait_recv()

    pass_on(spot, 0, at.xn)
    pass_on(spot, 1, at.yn)
    pass_on(spot, 2, at.sib)
    small_step(3)
    landed(px, 0)
    landed(py, 1)
    pass_on(px + core * (py - px), 3, at.yn + core * (at.xn - at.yn))
    pass_on(px, 4, at.sib)
    pass_on(py, 5, at.sib)
    for n in range(4, len(moves)):
        small_step(n)
    osmall[...] = small[...]
    landed(pd, 3)
    pass_on(pd, 6, at.sib)
    for h in range(2):
        send_to(wi.at[h], wi.at[h], hs.at[0, 0], hr.at[h, 0], z, i).wait_recv()
        send_to(wo.at[h], wo.at[h], hs.at[0, 1], hr.at[h, 1], z, i).wait_recv()
    landed(spot + flip, 2)
    landed(px + flip, 4)
    landed(py + flip, 5)
    landed(pd + flip, 6)
    for copy in tail + small_copies[-2:]:
        copy.wait_send()
    def d_sent(target, carry):
        pl.when(spot != target)(d_copy(target).wait_send)
        return carry

    lax.fori_loop(0, 8, d_sent, 0)

    @pl.when(host)
    def _():
        for copy in pair[0] + pair[1]:
            copy.wait_send()

    for is_far, copy in shipments:
        pl.when(is_far)(copy.wait_send)

    def dx_sent(step, carry):
        target = lax.rem(at.me + step, at.chips)
        for copy in copies(lax.div(target, per_plane), lax.rem(target, per_plane)):
            copy.wait_send()
        return carry

    lax.fori_loop(1, at.chips, dx_sent, 0)


def rear(planes, experts, nrouter, x, do, gate, back_in, win, wout, ga):
    rows, width = back_in[0].shape
    chips, padded, _ = x.shape
    slots = chips * padded
    ff = win.shape[1]
    pieces, blocks = (1, 4) if experts <= 8 else (2, 8)
    ga_groups = ff // width
    share, fshare, half = width // planes, ff // planes, width // 2
    upper = max(experts.bit_length() - 4, 1)
    nbits = experts.bit_length() - 1 + planes.bit_length() - 1
    dma = pltpu.SemaphoreType.DMA
    vm = pltpu.VMEM
    sds = jax.ShapeDtypeStruct
    return pl.pallas_call(
        functools.partial(rear_kernel, planes, experts, padded, pieces, blocks, ga_groups, nrouter),
        out_shape=(
            sds((rows, width), BF),
            sds((rows, width), BF),
            sds((8, share, half), BF),
            sds((nrouter + 16, width), F32),
            sds((2, share // 2, ff), BF),
            sds((2, fshare // 2, width), BF),
            sds((slots, width), BF),
            sds((slots, width), BF),
        ),
        in_specs=[vmem_spec()] * 3 + [any_spec()] * 14,
        out_specs=(vmem_spec(),) * 4 + (any_spec(),) * 4,
        scratch_shapes=[vm(a.shape, a.dtype) for a in back_in] + [
            vm((width, ff), BF),
            vm((ff, width), BF),
            vm((slots, width), BF),
            vm((slots, ff), BF),
            vm((slots, ff), BF),
            vm((chips, padded, width), BF),
            vm((chips, 1, 128), F32),
            vm((chips, 1, 128), F32),
            vm((chips, padded, width), BF),
            vm((slots, width), BF),
            vm((8, rows, half), BF),
            vm((8, rows, half), BF),
            vm((rows, width), F32),
            vm((planes, share, half), F32),
            vm((planes, share, half), BF),
            vm((planes - 1, share, half), BF),
            vm((upper, planes, share, half) if experts > 8 else (1, 8, 128), BF),
            vm((2, nrouter + 16, width), F32),
            vm((nbits, nrouter + 16, width), F32),
            vm((nrouter + 16, width), F32),
            vm((planes, share // 2, ff), BF),
            vm((planes, fshare // 2, width), BF),
            dma((2,)), dma((2, chips)), dma((2, chips)), dma((2,)), dma((ga_groups,)),
            dma((2, planes)), dma((2, planes)),
            dma((planes, 2)), dma((2, 2)),
            dma((chips,)), dma((chips,)), dma((2,)),
            dma((8,)), dma((8,)),
            dma((upper,)), dma((upper,)),
            dma((planes - 1,)), dma((planes - 1,)),
            dma((7,)), dma((7,)), dma((nbits,)), dma((nbits,)), dma((11,)),
        ],
        compiler_params=pltpu.CompilerParams(
            collective_id=2, has_side_effects=True, vmem_limit_bytes=REAR_LIMIT
        ),
        name="rear",
    )(x.reshape(slots, width), do.reshape(slots, width), gate, *back_in, win, wout, ga.reshape(8 * rows, width))


def finish_kernel(planes, nrouter, block_out, grad_tokens, fb, small, wi, wo,
                  ob, ot, o0, o1, o2, o3, og, v0, v1, v2, v3, ogi, ogo,
                  s0, s1, s2, s3, sg, sv, si, so, sem):
    z = lax.axis_index("dp")
    share = s0.shape[0]
    pairs = s0.shape[1] // 128
    half = s0.shape[1] // 2
    copies = []

    def write(source, target):
        copy = pltpu.make_async_copy(source, target, sem.at[len(copies)])
        copy.start()
        copies.append(copy)

    write(block_out, ob)
    write(grad_tokens, ot)
    for wide, low, out in ((si, wi, ogi), (so, wo, ogo)):
        chunk = low.shape[1]
        for h in range(2):
            wide[h * chunk:(h + 1) * chunk, :] = low[h].astype(F32)
            write(wide.at[pl.ds(h * chunk, chunk), :], out.at[pl.ds(h * chunk, chunk), :])
    for m, (stage, out) in enumerate(((s0, o0), (s1, o1), (s2, o2))):
        for n in range(pairs):
            stage[:, n * 128:(n + 1) * 128] = fb[n, :, m * 128:(m + 1) * 128].astype(F32)
        write(stage, out)
    for n in range(2):
        s3[:, n * half:(n + 1) * half] = fb[pairs + n].astype(F32)
    write(s3, o3)
    mine = small[:, 0:share]
    for p in range(1, planes):
        mine = jnp.where(z == p, small[:, p * share:(p + 1) * share], mine)
    sg[...] = mine[0:nrouter]
    write(sg, og)
    for n, out in enumerate((v0, v1, v2, v3)):
        sv[n] = mine[nrouter + n:nrouter + n + 1]
        write(sv.at[n], out)
    for copy in copies:
        copy.wait()


def finish(planes, nrouter, block_out, grad_tokens, fb, small, wi, wo):
    rows, width = block_out.shape
    _, share, half = fb.shape
    ff = wi.shape[2]
    fshare = 2 * wo.shape[1]
    vm = pltpu.VMEM
    sds = jax.ShapeDtypeStruct
    dense = ((share, width),) * 4 + ((nrouter, share),)
    wide = ((share, ff), (fshare, width))
    results = dense + ((1, share),) * 4 + wide
    stages = dense + ((4, 1, share),) + wide
    return pl.pallas_call(
        functools.partial(finish_kernel, planes, nrouter),
        out_shape=(sds((rows, width), BF),) * 2 + tuple(sds(shape, F32) for shape in results),
        in_specs=[vmem_spec()] * 6,
        out_specs=(any_spec(),) * 13,
        scratch_shapes=[vm(shape, F32) for shape in stages] + [pltpu.SemaphoreType.DMA((16,))],
        compiler_params=pltpu.CompilerParams(vmem_limit_bytes=VMEM_LIMIT),
        name="finish",
    )(block_out, grad_tokens, fb, small, wi, wo)


def shards(planes, experts, tokens, segment_ids, routes, ln1_gain, ln1_bias, ln2_gain, ln2_bias,
           w_query, w_key, w_value, w_output, w_router, frozen_in, frozen_out, new_in, new_out,
           cotangent):
    rows, width = tokens.shape
    expert_count = w_router.shape[1]
    capacity = 5 * rows // (2 * expert_count)
    padded = -(-capacity // 8) * 8
    (wd, pk, win, wout, act_two, q, k, v, resid, probs, aux, ga, x_recv, do_recv, g_recv) = front(
        planes, experts, capacity, padded, expert_count, tokens, cotangent, segment_ids, routes,
        w_router, (ln1_gain, ln1_bias, ln2_gain, ln2_bias),
        w_query, w_key, w_value, w_output, frozen_in, frozen_out, new_in, new_out,
    )
    block_out, grad_tokens, dense, small, low_in, low_out, _, _ = rear(
        planes, experts, expert_count, x_recv, do_recv, g_recv,
        (tokens, cotangent, aux, act_two, q, k, v, resid, probs, wd, pk), win, wout, ga,
    )
    block_out, grad_tokens, oq, ok, ov, ow, router, *norms, ogi, ogo = finish(
        planes, expert_count, block_out, grad_tokens, dense, small, low_in, low_out
    )
    norms = [norm.reshape(width // planes) for norm in norms]
    return (
        block_out, grad_tokens, oq, ok, ov, ow, router.T,
        norms[0], norms[1], norms[2], norms[3], ogi[None], ogo[None],
    )


def solution(mesh):
    rows = P(("dp", "expert"), None)
    in_specs = (rows, rows, rows) + (P("dp"),) * 4 + (P("dp", None),) * 5
    in_specs += (P("expert", "dp", None),) * 4 + (rows,)
    out_specs = (rows, rows) + (P("dp", None),) * 5 + (P("dp"),) * 4
    out_specs += (P("expert", "dp", None),) * 2
    body = functools.partial(shards, mesh.shape["dp"], mesh.shape["expert"])
    return jax.shard_map(body, mesh=mesh, in_specs=in_specs, out_specs=out_specs, check_vma=False)
```

```python
import functools

import jax
import jax.numpy as jnp
from jax import lax
from jax.experimental import pallas as pl
from jax.experimental.pallas import tpu as pltpu
from jax.sharding import PartitionSpec as P

HEADS = 12
HEAD = 64
NORM_EPS = 1e-05
MASKED = -1e30
MESH = pl.DeviceIdType.MESH
BF = jnp.bfloat16
F32 = jnp.float32
VMEM_LIMIT = 60 * 1024 * 1024
REAR_LIMIT = 67043328


class Place:
    def __init__(self, planes, experts):
        self.planes, self.experts = planes, experts
        self.z = lax.axis_index("dp")
        self.i = lax.axis_index("expert")
        self.core = lax.rem(self.i, 2)
        self.chip = lax.div(self.i, 2)
        self.xb = lax.rem(self.chip, 2)
        self.yb = lax.rem(lax.div(self.i, 4), 2)
        self.sib = self.i + 1 - 2 * self.core
        self.xn = self.i + 2 - 4 * self.xb
        self.yn = self.i + 4 - 8 * self.yb
        self.chips = planes * (experts // 2)
        self.me = self.z * (experts // 2) + self.chip


def send_to(src, dst, send_sem, recv_sem, z, i):
    return pltpu.make_async_remote_copy(
        src_ref=src,
        dst_ref=dst,
        send_sem=send_sem,
        recv_sem=recv_sem,
        device_id={"dp": z, "expert": i},
        device_id_type=MESH,
    )


def greet(at):
    barrier = pltpu.get_barrier_semaphore()
    count = at.planes * at.experts
    own = at.z * at.experts + at.i

    def signal(step, carry):
        target = lax.rem(own + step, count)
        pl.semaphore_signal(
            barrier,
            inc=1,
            device_id={"dp": lax.div(target, at.experts), "expert": lax.rem(target, at.experts)},
            device_id_type=MESH,
        )
        return carry

    lax.fori_loop(1, count, signal, 0)
    return lambda: pl.semaphore_wait(barrier, count - 1)


def any_spec():
    return pl.BlockSpec(memory_space=pl.ANY)


def vmem_spec():
    return pl.BlockSpec(memory_space=pltpu.VMEM)


NN = ((1,), (0,))
NT = ((1,), (1,))
TN = ((0,), (0,))


def dot(left, right, contract, out=F32):
    return lax.dot_general(
        left, right, ((contract[0], contract[1]), ((), ())), preferred_element_type=F32
    ).astype(out)


def exact_dot(left, right, contract):
    return lax.dot_general(
        left, right, ((contract[0], contract[1]), ((), ())),
        preferred_element_type=F32, precision=lax.Precision.HIGHEST,
    )


def norm_parts(rows):
    centred = rows - jnp.mean(rows, axis=-1, keepdims=True)
    variance = jnp.mean(centred * centred, axis=-1, keepdims=True)
    scale = lax.rsqrt(variance + NORM_EPS)
    return centred * scale, scale


def norm_back(rows, gain, grad):
    unit, scale = norm_parts(rows)
    scaled = grad * gain
    inner = scaled - jnp.mean(scaled, axis=-1, keepdims=True)
    inner = inner - unit * jnp.mean(scaled * unit, axis=-1, keepdims=True)
    return scale * inner, jnp.sum(grad * unit, axis=0, keepdims=True), jnp.sum(grad, axis=0, keepdims=True)


def slot_places(slot, slots):
    lanes = lax.broadcasted_iota(jnp.int32, (slot[0].shape[0], slots), 1).astype(F32)
    return [(lanes == one).astype(F32).astype(BF) for one in slot]


def slot_values(aux, table, padded, chips):
    rows = aux.shape[0]
    low = lax.broadcasted_iota(jnp.int32, (rows, chips), 1).astype(F32) * padded
    lanes = lax.broadcasted_iota(jnp.int32, (rows, table.shape[1]), 1).astype(F32)
    found = []
    for k in range(2):
        slot = aux[:, 2 + k:3 + k]
        mine = jnp.logical_and(slot >= low, slot < low + padded).astype(F32)
        position = slot - jnp.sum(mine * low, axis=1, keepdims=True)
        picked = exact_dot(mine, table, NN)
        found.append(jnp.sum(jnp.where(lanes == position, picked, 0.0), axis=1, keepdims=True))
    return found


def front_kernel(planes, experts, capacity, padded, nrouter,
                 tokens, cot, segs, routes, router, g1, b1, g2, b2, wq, wk, wv, wo, fi, fo, ni, no,
                 owd, pk, win, wout, oact, oq, ok, ov, oresid, oprobs, aux, ga,
                 xland, dland, gland,
                 wd, act_one, act_two, q, k, v, att, resid, probs, packs, allow, xsend, esend, gsend, dstage, istage, ostage, ibf, obf,
                 ld, zs, zr, ps, pr, gs, gr, es, er, fs, fr, ts, tr, tl, sa, ra, sv, zf):
    at = Place(planes, experts)
    z, i, core = at.z, at.i, at.core
    rows, width = tokens.shape
    chips = at.chips
    per_plane = experts // 2
    share = dstage.shape[1]
    quarter = share // 4
    half = width // 2
    fhalf = istage.shape[2] // 2
    oshare = ostage.shape[1]
    ohalf = oshare // 2
    pairs = width // 128
    spot = lax.rem(i, 8)
    base = i - spot
    loads = [pltpu.make_async_copy(w, dstage.at[m], ld.at[m]) for m, w in enumerate((wq, wk, wv, wo))]
    loads += [
        pltpu.make_async_copy(fi.at[0], istage.at[0], ld.at[4]),
        pltpu.make_async_copy(ni.at[0], istage.at[1], ld.at[5]),
        pltpu.make_async_copy(fo.at[0], ostage.at[0], ld.at[6]),
        pltpu.make_async_copy(no.at[0], ostage.at[1], ld.at[7]),
    ]
    for load in loads:
        load.start()
    met = greet(at)
    zrow = pl.multiple_of(z * share, share)
    for m in range(4):
        loads[m].wait()
        wd[m, pl.ds(zrow, share), :] = dstage[m].astype(BF)
    packs[z, 0:nrouter, :] = router[...].astype(BF)
    norm_row = lax.broadcasted_iota(jnp.int32, (16, share), 0)
    norms = jnp.zeros((16, share), F32)
    for n, values in enumerate((g1, b1, g2, b2)):
        norms = jnp.where(norm_row == n, values[...], norms)
    packs[z, nrouter:nrouter + 16, :] = norms.astype(BF)
    met()

    def block(plane, row_quarter, column_half):
        return wd.at[
            :,
            pl.ds(pl.multiple_of(plane * share + row_quarter * quarter, 16), quarter),
            pl.ds(pl.multiple_of(column_half * half, 128), half),
        ]

    rq = 2 * at.yb + core
    rqy = 2 * (1 - at.yb) + core
    rqs = 2 * at.yb + 1 - core
    rqys = 2 * (1 - at.yb) + 1 - core
    xb, xo = at.xb, 1 - at.xb
    started, remote_sends = [], []
    for j in range(1, planes):
        zt = lax.rem(z + j, planes)
        mine = block(z, rq, xb)
        copy = send_to(mine, mine, zs.at[j - 1], zr.at[j - 1], zt, i)
        direct = jnp.logical_or(lax.div(zt, 2) == lax.div(z, 2), jnp.logical_and(zt >= 1, zt <= 2))
        pl.when(direct)(copy.start)
        remote_sends.append((direct, copy))
        copy = send_to(packs.at[z], packs.at[z], ps.at[j - 1], pr.at[j - 1], zt, i)
        copy.start()
        started.append(copy)

    def cast(source, target, kind, chunk):
        def step(n, carry):
            part = pl.ds(pl.multiple_of(n * chunk, chunk), chunk)
            target[kind, part, :] = source[kind, part, :].astype(BF)
            return carry

        lax.fori_loop(0, source.shape[1] // chunk, step, 0)

    def in_block(plane, h):
        return win.at[
            pl.ds(pl.multiple_of(plane * share, 16), share),
            pl.ds(pl.multiple_of(h * fhalf, 128), fhalf),
        ]

    def out_block(plane, h):
        return wout.at[pl.ds(pl.multiple_of(plane * oshare + h * ohalf, 16), ohalf), :]


    def ship(kind, h, which):
        zh = 3 * core if kind == 0 else 1 + core
        remote = jnp.logical_or(zh != z, core != h)
        src = (
            ibf.at[kind, :, pl.ds(h * fhalf, fhalf)]
            if which == 0
            else obf.at[kind, pl.ds(h * ohalf, ohalf), :]
        )
        dst = in_block(z, h) if which == 0 else out_block(z, h)
        far = send_to(src, dst, es.at[kind, h, which], er.at[z, which], zh, 2 * at.chip + h)
        near = pltpu.make_async_copy(src, dst, er.at[z, which])
        pl.when(remote)(far.start)
        pl.when(jnp.logical_not(remote))(near.start)
        remote_sends.append((remote, far))

    def ship_in(kind):
        loads[4 + kind].wait()
        cast(istage, ibf, kind, 16)
        for h in range(2):
            ship(kind, h, 0)

    ship_in(1)
    end = 3 * (z - 1)
    handed = []
    for j in range(1, planes):
        zz = lax.rem(z + planes - j, planes)
        hand = jnp.logical_and(lax.div(zz, 2) != lax.div(z, 2), jnp.logical_and(z >= 1, z <= 2))
        mine = block(zz, rq, xb)
        there = lax.rem(end + planes - zz, planes)
        copy = send_to(mine, mine, zf.at[j - 1], zr.at[jnp.maximum(there, 1) - 1], jnp.clip(end, 0, planes - 1), i)

        @pl.when(hand)
        def _():
            send_to(mine, mine, zs.at[j - 1], zr.at[j - 1], z, i).wait_recv()
            copy.start()

        handed.append(hand)
        remote_sends.append((hand, copy))
    ship_in(0)

    shift = experts.bit_length() - 1
    above = lax.broadcasted_iota(jnp.int32, (rows, rows), 0)
    across = lax.broadcasted_iota(jnp.int32, (rows, rows), 1)
    segment = segs[...].astype(F32)
    fact_row = lax.broadcasted_iota(jnp.int32, (8, rows), 0)
    facts = jnp.zeros((8, rows), F32)
    for n, values in enumerate((routes[0:1, :].astype(F32), routes[1:2, :].astype(F32), segment)):
        facts = jnp.where(fact_row == n, values, facts)
    fact_columns = dot((above == across).astype(F32).astype(BF), facts.astype(BF), NT)
    route_columns = [fact_columns[:, n:n + 1] for n in range(2)]
    route = fact_columns.astype(jnp.int32)
    expert = jnp.bitwise_and(route, experts - 1)
    kind = jnp.right_shift(route, shift)
    host_plane = jnp.where(jnp.bitwise_and(expert, 1) == 0, kind, 3 - kind)
    host = host_plane * per_plane + jnp.right_shift(expert, 1)
    chip_iota = lax.broadcasted_iota(jnp.int32, (rows, chips), 1)
    chosen = [(chip_iota == host[:, n:n + 1]).astype(F32) for n in range(2)]
    earlier = (across < above).astype(F32).astype(BF)
    before = dot(earlier, (chosen[0] + chosen[1]).astype(BF), NN)
    position = [jnp.sum(one * before, axis=1, keepdims=True) for one in chosen]
    slot = [
        jnp.where(position[n] < capacity, host[:, n:n + 1].astype(F32) * padded + position[n], -1.0)
        for n in range(2)
    ]
    place = slot_places(slot, chips * padded)
    both = place[0] + place[1]

    def fill(target, values):
        sent = dot(both, values, TN)
        for n in range(chips):
            target[n] = sent[n * padded:(n + 1) * padded].astype(BF)

    def token_copy(src, dst, which, step):
        target = lax.rem(at.me + step, chips)
        zt, it = lax.div(target, per_plane), 2 * lax.rem(target, per_plane) + core
        return send_to(src.at[target], dst.at[at.me], ts.at[which, step], tr.at[which, step], zt, it)

    def token_start(src, dst, which):
        pltpu.make_async_copy(src.at[at.me], dst.at[at.me], tl.at[which]).start()

        def step(n, carry):
            token_copy(src, dst, which, n).start()
            return carry

        lax.fori_loop(1, chips, step, 0)

    def token_finish(src, dst, which):
        def step(n, carry):
            source = lax.rem(at.me + chips - n, chips)
            send_to(
                src.at[source], dst.at[source], ts.at[which, n], tr.at[which, n], z, i
            ).wait_recv()
            token_copy(src, dst, which, n).wait_send()
            return carry

        lax.fori_loop(1, chips, step, 0)
        pltpu.make_async_copy(src.at[at.me], dst.at[at.me], tl.at[which]).wait()

    fill(esend, cot[...])
    token_start(esend, dland, 0)
    for n, kind in ((6, 0), (7, 1)):
        loads[n].wait()
        cast(ostage, obf, kind, 32)
        for h in range(2):
            ship(kind, h, 1)
    same = jnp.logical_and(fact_columns[:, 2:3] == segment, across <= above)
    allow[...] = same.astype(F32)

    def pass_on(src, j, step, target):
        copy = send_to(src, src, gs.at[j - 1, step], gr.at[j - 1, step], z, target)
        copy.start()
        started.append(copy)

    def landed(dst, j, step):
        send_to(dst, dst, gs.at[j - 1, step], gr.at[j - 1, step], z, i).wait_recv()

    for j in range(1, planes):
        zz = lax.rem(z + planes - j, planes)
        mine = block(zz, rq, xb)
        arrival = send_to(mine, mine, zs.at[j - 1], zr.at[j - 1], z, i)
        pl.when(jnp.logical_not(handed[j - 1]))(arrival.wait_recv)
        pass_on(mine, j, 0, at.xn)
        pass_on(mine, j, 1, at.yn)
        pass_on(mine, j, 2, at.sib)
        send_to(packs.at[zz], packs.at[zz], ps.at[j - 1], pr.at[j - 1], z, i).wait_recv()
    pk[...] = jnp.concatenate([packs[p] for p in range(planes)], axis=1)

    x = tokens[...].astype(F32)
    gain = pk[nrouter:nrouter + 1, :].astype(F32)
    bias = pk[nrouter + 1:nrouter + 2, :].astype(F32)
    act_one[...] = (norm_parts(x)[0] * gain + bias).astype(BF)

    for j in range(1, planes):
        zz = lax.rem(z + planes - j, planes)
        bx, by = block(zz, rq, xo), block(zz, rqy, xb)
        landed(bx, j, 0)
        landed(by, j, 1)
        onward = block(zz, rq + core * (rqy - rq), xo + core * (xb - xo))
        pass_on(onward, j, 3, at.yn + core * (at.xn - at.yn))
        pass_on(bx, j, 4, at.sib)
        pass_on(by, j, 5, at.sib)
    for j in range(1, planes):
        zz = lax.rem(z + planes - j, planes)
        bd = block(zz, rqy, xo)
        landed(bd, j, 3)
        pass_on(bd, j, 6, at.sib)
    for j in range(1, planes):
        zz = lax.rem(z + planes - j, planes)
        landed(block(zz, rqs, xb), j, 2)
        landed(block(zz, rqs, xo), j, 4)
        landed(block(zz, rqys, xb), j, 5)
        landed(block(zz, rqys, xo), j, 6)

    def act_copy(step, whole):
        target = lax.rem(spot + step, 8)
        src = act_one if whole else att
        return target, send_to(src, ga.at[spot], sa.at[step], ra.at[step], z, base + target)

    def act_near(whole):
        return pltpu.make_async_copy(act_one if whole else att, ga.at[spot], tl.at[3])

    for step in range(1, 8):
        target, copy = act_copy(step, True)
        pl.when(target < pairs)(copy.start)
    pl.when(spot < pairs)(act_near(True).start)

    one = act_one[...]
    q[...] = dot(one, wd[0], NN, BF)
    k[...] = dot(one, wd[1], NN, BF)
    v[...] = dot(one, wd[2], NN, BF)
    lane = lax.broadcasted_iota(jnp.int32, (rows, 128), 1)
    masks = [(lane < HEAD).astype(F32).astype(BF), (lane >= HEAD).astype(F32).astype(BF)]
    score_scale = HEAD ** (-0.5)

    def head_pair(n, carry):
        cols = pl.ds(pl.multiple_of(n * 128, 128), 128)
        q2, k2, v2 = q[:, cols], k[:, cols], v[:, cols]
        total = jnp.zeros((rows, 128), F32)
        for side in range(2):
            scores = dot(q2 * masks[side], k2, NT) * score_scale
            scores = jnp.where(allow[...] > 0.5, scores, MASKED)
            expo = jnp.exp(scores - jnp.max(scores, axis=-1, keepdims=True))
            p = expo / jnp.sum(expo, axis=-1, keepdims=True)
            probs[2 * n + side] = p
            total += dot(p.astype(BF), v2 * masks[side], NN)
        att[:, cols] = total.astype(BF)
        return carry

    lax.fori_loop(0, pairs, head_pair, 0)
    residual = x + dot(att[...], wd[3], NN)
    resid[...] = residual
    gain = pk[nrouter + 2:nrouter + 3, :].astype(F32)
    bias = pk[nrouter + 3:nrouter + 4, :].astype(F32)
    two = (norm_parts(residual)[0] * gain + bias).astype(BF)
    act_two[...] = two
    fill(xsend, two)
    token_start(xsend, xland, 1)
    for step in range(1, 8):
        target, copy = act_copy(step, False)
        pl.when(target >= pairs)(copy.start)
    pl.when(spot >= pairs)(act_near(False).start)

    logits = dot(two, pk[0:nrouter, :], NT)
    route_iota = lax.broadcasted_iota(jnp.int32, (rows, nrouter), 1)
    picked = [
        jnp.sum(jnp.where(route_iota == route[:, n:n + 1], logits, 0.0), axis=1, keepdims=True)
        for n in range(2)
    ]
    top = jnp.maximum(picked[0], picked[1])
    lifted = [jnp.exp(one_pick - top) for one_pick in picked]
    gates = [one_lift / (lifted[0] + lifted[1]) for one_lift in lifted]
    values = jnp.zeros((rows, 128), F32)
    for n, column in enumerate(gates + slot + route_columns):
        values = jnp.where(lane == n, column, values)
    aux[...] = values
    lanes = lane.astype(F32)
    table = jnp.zeros((chips, 128), F32)
    for n in range(2):
        kept = jnp.logical_and(lanes == position[n], position[n] < capacity)
        table += exact_dot(chosen[n], jnp.where(kept, gates[n], 0.0), TN)
    for n in range(chips):
        gsend[n] = table[n:n + 1]
    token_start(gsend, gland, 2)
    kept_arrays = ((wd, owd), (act_two, oact), (q, oq), (k, ok), (v, ov), (resid, oresid), (probs, oprobs))
    saves = [pltpu.make_async_copy(src, dst, sv.at[n]) for n, (src, dst) in enumerate(kept_arrays)]
    for copy in saves:
        copy.start()

    def hand_on(plane, which):
        blk = in_block(plane, core) if which == 0 else out_block(plane, core)
        send_to(blk, blk, es.at[0, 0, which], er.at[plane, which], z, i).wait_recv()
        copy = send_to(blk, blk, fs.at[plane, which], fr.at[plane, which], z, at.sib)
        copy.start()
        started.append(copy)

    for which in range(2):
        for plane in range(planes):
            hand_on(plane, which)
    for src, dst, which in ((esend, dland, 0), (xsend, xland, 1), (gsend, gland, 2)):
        token_finish(src, dst, which)
    for step in range(1, 8):
        source = lax.rem(spot + 8 - step, 8)
        send_to(act_one, ga.at[source], sa.at[step], ra.at[step], z, i).wait_recv()
        act_copy(step, True)[1].wait_send()
    act_near(True).wait()
    for which in range(2):
        for plane in range(planes):
            blk = in_block(plane, 1 - core) if which == 0 else out_block(plane, 1 - core)
            send_to(blk, blk, fs.at[plane, which], fr.at[plane, which], z, i).wait_recv()
    for copy in started:
        copy.wait_send()
    for remote, far in remote_sends:
        pl.when(remote)(far.wait_send)
    for copy in saves:
        copy.wait()


def front(planes, experts, capacity, padded, nrouter, tokens, cot, segment_ids, routes, router, norms,
          wq, wk, wv, wo, fi, fo, ni, no):
    rows, width = tokens.shape
    share = wq.shape[0]
    ff = fi.shape[2]
    oshare = fo.shape[1]
    chips = planes * experts // 2
    dma = pltpu.SemaphoreType.DMA
    vm = pltpu.VMEM
    sds = jax.ShapeDtypeStruct
    flat = sds((rows, width), BF)
    slab = sds((chips, padded, width), BF)
    return pl.pallas_call(
        functools.partial(front_kernel, planes, experts, capacity, padded, nrouter),
        out_shape=(
            sds((4, width, width), BF),
            sds((nrouter + 16, width), BF),
            sds((width, ff), BF),
            sds((ff, width), BF),
            flat, flat, flat, flat,
            sds((rows, width), F32),
            sds((HEADS, rows, rows), F32),
            sds((rows, 128), F32),
            sds((8, rows, width), BF),
            slab,
            slab,
            sds((chips, 1, 128), F32),
        ),
        in_specs=[vmem_spec()] * 9 + [any_spec()] * 8,
        out_specs=(any_spec(), vmem_spec()) + (any_spec(),) * 8 + (vmem_spec(),) + (any_spec(),) * 4,
        scratch_shapes=[
            vm((4, width, width), BF),
        ] + [vm((rows, width), BF)] * 6 + [
            vm((rows, width), F32),
            vm((HEADS, rows, rows), F32),
            vm((planes, nrouter + 16, share), BF),
            vm((rows, rows), F32),
            vm((chips, padded, width), BF),
            vm((chips, padded, width), BF),
            vm((chips, 1, 128), F32),
            vm((4, share, width), F32),
            vm((2, share, ff), F32),
            vm((2, oshare, width), F32),
            vm((2, share, ff), BF),
            vm((2, oshare, width), BF),
            dma((8,)),
            dma((planes - 1,)), dma((planes - 1,)), dma((planes - 1,)), dma((planes - 1,)),
            dma((planes - 1, 7)), dma((planes - 1, 7)),
            dma((2, 2, 2)), dma((planes, 2)), dma((planes, 2)), dma((planes, 2)),
            dma((3, chips)), dma((3, chips)), dma((4,)), dma((8,)), dma((8,)), dma((7,)), dma((planes - 1,)),
        ],
        compiler_params=pltpu.CompilerParams(
            collective_id=0, has_side_effects=True, vmem_limit_bytes=VMEM_LIMIT
        ),
        name="front",
    )(tokens, cot, segment_ids, routes.T, router.T, *[norm.reshape(1, share) for norm in norms],
      wq, wk, wv, wo, fi, fo, ni, no)


GELU_SCALE = 0.7978845608028654
GELU_CUBE = 0.044715


def rear_kernel(planes, experts, padded, pieces, blocks, ga_groups, nrouter,
                x, do, gate, *refs):
    back_in, refs = refs[:11], refs[11:]
    (win, wout, ga,
                block_out, grad_tokens, fb, osmall, wi, wo, yland, dxland,
                tokens, cot, aux, act_two, q, k, v, resid, probs, wd, pk,
                hwi, hwo, dy, hid, dpre, dxsend, dgsend, dgland, ysend, landed_rows,
                gd, dsend, dres, gsum, szb, rzb, rup,
                sms, smr, small, ri, ro,
                ls, ts, tr, tl, gl,
                es, er, hs, hr, ys, yr, yl, sd, rd, us, ur, zs, zr, gs, gr, ms, mr, lb) = refs
    back_held = (tokens, cot, aux, act_two, q, k, v, resid, probs, wd, pk)
    back_loads = [
        pltpu.make_async_copy(src, dst, lb.at[n]) for n, (src, dst) in enumerate(zip(back_in, back_held))
    ]
    at = Place(planes, experts)
    z, i, core = at.z, at.i, at.core
    chips = at.chips
    per_plane = experts // 2
    rows, width = tokens.shape
    pairs = width // 128
    spot = lax.rem(i, 8)
    base = i - spot
    upper = rup.shape[0] if experts > 8 else 0
    ga_rows = 8 * rows // ga_groups
    datt, dq, dk, dv = [dpre.at[pl.ds(0, rows), pl.ds(n * width, width)] for n in range(4)]
    chunk = per_plane * padded // pieces
    batch = per_plane // pieces
    ff = hwi.shape[1]
    wide = ff // blocks
    load_i = pltpu.make_async_copy(win, hwi, ls.at[0])
    load_o = pltpu.make_async_copy(wout, hwo, ls.at[1])
    load_i.start()
    load_o.start()
    met = greet(at)
    diagonal = lax.broadcasted_iota(jnp.int32, (padded, 128), 1) == lax.broadcasted_iota(jnp.int32, (padded, 128), 0)
    load_i.wait()
    load_o.wait()
    for copy in back_loads:
        copy.start()
    met()

    def copies(plane, n):
        target = plane * per_plane + n
        there = 2 * n + core
        rows_in = dxland.at[pl.ds(pl.multiple_of(at.me * padded, 8), padded), :]
        return [
            send_to(dxsend.at[target], rows_in, ts.at[0, target], tr.at[0, at.me], plane, there),
            send_to(dgsend.at[target], dgland.at[at.me], ts.at[1, target], tr.at[1, at.me], plane, there),
        ]

    def own_copies():
        rows_in = dxland.at[pl.ds(pl.multiple_of(at.me * padded, 8), padded), :]
        return [
            pltpu.make_async_copy(dxsend.at[at.me], rows_in, tl.at[0]),
            pltpu.make_async_copy(dgsend.at[at.me], dgland.at[at.me], tl.at[1]),
        ]

    def work(plane, piece):
        first = plane * per_plane + piece * batch
        span = pl.ds(pl.multiple_of((plane * pieces + piece) * chunk, 16), chunk)
        x_c = x[span, :]
        do_c = do[span, :].astype(F32)
        column = jnp.concatenate(
            [
                jnp.sum(jnp.where(diagonal, gate[first + n], 0.0), axis=1, keepdims=True)
                for n in range(batch)
            ],
            axis=0,
        )
        dy_c = (do_c * column).astype(BF)
        dy[span, :] = dy_c
        y_sum = jnp.zeros((chunk, width), F32)
        dx_sum = jnp.zeros((chunk, width), F32)
        for b in range(blocks):
            cols = slice(b * wide, (b + 1) * wide)
            u = dot(x_c, hwi[:, cols], NN)
            dz = dot(dy_c, hwo[cols, :], NT)
            square = u * u
            bent = jnp.tanh(GELU_SCALE * (u + GELU_CUBE * (square * u)))
            cdf = 0.5 * (1.0 + bent)
            slope = cdf + (0.5 * GELU_SCALE) * u * (1.0 - bent * bent) * (1.0 + 3.0 * GELU_CUBE * square)
            hidden = (u * cdf).astype(BF)
            d_pre = (dz * slope).astype(BF)
            hid[span, cols] = hidden
            dpre[span, cols] = d_pre
            y_sum += dot(hidden, hwo[cols, :], NN)
            dx_sum += dot(d_pre, hwi[:, cols], NT)
        y_low = y_sum.astype(BF)
        d_gate = jnp.sum(y_low.astype(F32) * do_c, axis=1, keepdims=True)
        for n in range(batch):
            part = slice(n * padded, (n + 1) * padded)
            source = first + n
            ysend[source] = y_sum[part].astype(BF)
            dxsend[source] = dx_sum[part].astype(BF)
            dgsend[source] = jnp.sum(jnp.where(diagonal, d_gate[part], 0.0), axis=0, keepdims=True)

    def far_plane(turn):
        half = 1 - 2 * lax.rem(z, 2)
        other = lax.rem(z + 2, planes)
        return jnp.where(turn == 0, other, jnp.where(turn == 1, planes - 1 - z, z + half))

    def remote_turn(turn, carry):
        plane = far_plane(lax.div(turn, pieces))
        piece = lax.rem(turn, pieces)
        work(plane, piece)
        for n in range(batch):
            for copy in copies(plane, piece * batch + n):
                copy.start()
        return carry

    lax.fori_loop(0, (planes - 1) * pieces, remote_turn, 0)
    for piece in range(pieces):
        work(z, piece)
    for copy in own_copies():
        copy.start()
    for n in range(per_plane):
        for copy in copies(z, n):
            pl.when(at.chip != n)(copy.start)

    def landing(source):
        return yland.at[pl.ds(pl.multiple_of(source * padded, 8), padded), :]

    def y_copy(step):
        target = lax.rem(at.me + step, chips)
        zt, it = lax.div(target, per_plane), 2 * lax.rem(target, per_plane) + core
        return send_to(ysend.at[target], landing(at.me), ys.at[step], yr.at[step], zt, it)

    def y_start(step, carry):
        y_copy(step).start()
        return carry

    y_own = pltpu.make_async_copy(ysend.at[at.me], landing(at.me), yl.at[0])
    y_own.start()
    lax.fori_loop(1, chips, y_start, 0)

    ce = z - 1
    host = jnp.logical_and(z >= 1, z <= 2)
    half_i, half_o = width // planes // 2, ff // planes // 2

    def part(source, size, p, c):
        return source.at[pl.ds(pl.multiple_of((2 * p + c) * size, 16), size), :]

    pair = [
        [
            send_to(part(src, size, p, 1 - core), land.at[p], es.at[which, p], er.at[which, p], z, at.sib)
            for p in range(planes)
        ]
        for which, (src, land, size) in enumerate(((hwi, ri, half_i), (hwo, ro, half_o)))
    ]
    fetch_ga = [
        pltpu.make_async_copy(
            ga.at[pl.ds(g * ga_rows, ga_rows), :],
            hid.at[pl.ds(0, ga_rows), pl.ds(g * width, width)],
            gl.at[g],
        )
        for g in range(ga_groups)
    ]

    @pl.when(host)
    def _():
        turned = x[...].T
        for b in range(blocks):
            cols = slice(b * wide, (b + 1) * wide)
            hwi[:, cols] = dot(turned, dpre[:, cols], NN, BF)
        for copy in pair[0]:
            copy.start()
        for b in range(blocks):
            cols = slice(b * wide, (b + 1) * wide)
            hwo[cols, :] = dot(hid[:, cols], dy[...], TN, BF)
        for copy in pair[1]:
            copy.start()

    for copy in fetch_ga:
        copy.start()

    owner = 2 * at.chip + ce
    shipments = []

    def ship(p, which):
        src, dst = (part(hwi, half_i, p, core), wi.at[core]) if which == 0 else (part(hwo, half_o, p, core), wo.at[core])
        near = jnp.logical_and(z == p, core == ce)
        far_copy = send_to(src, dst, hs.at[p, which], hr.at[core, which], p, owner)
        near_copy = pltpu.make_async_copy(src, dst, hr.at[core, which])
        is_far = jnp.logical_and(host, jnp.logical_not(near))
        pl.when(is_far)(far_copy.start)
        pl.when(jnp.logical_and(host, near))(near_copy.start)
        shipments.append((is_far, far_copy))

    def add_pair(which, mine, theirs, size, chunk):
        @pl.when(host)
        def _():
            for copy in pair[which]:
                copy.wait_recv()

            def add(n, carry):
                low = pl.ds(pl.multiple_of(n * chunk, chunk), chunk)
                for p in range(planes):
                    here = pl.ds(pl.multiple_of((2 * p + core) * size + n * chunk, 16), chunk)
                    mine[here, :] = (
                        mine[here, :].astype(F32) + theirs[p, low, :].astype(F32)
                    ).astype(BF)
                return carry

            lax.fori_loop(0, size // chunk, add, 0)

    add_pair(0, hwi, ri, half_i, 16)
    for p in range(planes):
        ship(p, 0)
    add_pair(1, hwo, ro, half_o, 64)
    for p in (0, 3):
        ship(p, 1)

    def dx_wait(step, carry):
        source = lax.rem(at.me + step, at.chips)
        rows_in = dxland.at[pl.ds(pl.multiple_of(source * padded, 8), padded), :]
        send_to(dxsend.at[source], rows_in, ts.at[0, source], tr.at[0, source], z, i).wait_recv()
        send_to(dgsend.at[source], dgland.at[source], ts.at[1, source], tr.at[1, source], z, i).wait_recv()
        return carry

    for copy in own_copies():
        copy.wait()
    lax.fori_loop(1, at.chips, dx_wait, 0)
    fetch_dx = pltpu.make_async_copy(dxland, landed_rows, yl.at[1])
    fetch_dx.start()
    fetch_dx.wait()

    for copy in back_loads:
        copy.wait()

    aux_v = aux[...]
    gates = [aux_v[:, 0:1], aux_v[:, 1:2]]
    place = slot_places([aux_v[:, 2:3], aux_v[:, 3:4]], chips * padded)
    d_out = cot[...].astype(F32)
    d_act = dot(place[0] + place[1], landed_rows[...], NN)
    table = dgland[:, 0, :]
    d_gate = slot_values(aux_v, table, padded, chips)
    mean_gate = gates[0] * d_gate[0] + gates[1] * d_gate[1]
    route_iota = lax.broadcasted_iota(jnp.int32, (rows, nrouter), 1).astype(F32)
    d_logits = jnp.zeros((rows, nrouter), F32)
    for n in range(2):
        chosen = route_iota == aux_v[:, 4 + n:5 + n]
        d_logits = d_logits + jnp.where(chosen, gates[n] * (d_gate[n] - mean_gate), 0.0)
    d_logits = d_logits.astype(BF)
    small[0:nrouter, :] = dot(d_logits, act_two[...], TN)
    d_act = d_act + dot(d_logits, pk[0:nrouter, :], NN)
    gain_one = pk[nrouter:nrouter + 1, :].astype(F32)
    gain_two = pk[nrouter + 2:nrouter + 3, :].astype(F32)
    d_norm, g_gain, g_bias = norm_back(resid[...], gain_two, d_act)
    small[nrouter:nrouter + 16, :] = jnp.zeros((16, width), F32)
    small[nrouter + 2:nrouter + 3, :] = g_gain
    small[nrouter + 3:nrouter + 4, :] = g_bias
    d_res = d_out + d_norm
    dres[...] = d_res
    d_branch = d_res.astype(BF)
    half = width // 2
    for n in range(2):
        dsend[pairs + n] = d_branch[:, n * half:(n + 1) * half]
    datt[...] = dot(d_branch, wd[3], NT, BF)

    def d_copy(target):
        return send_to(dsend.at[target], gd.at[spot], sd.at[target], rd.at[spot], z, base + target)

    def d_near(target):
        return pltpu.make_async_copy(dsend.at[target], gd.at[spot], rd.at[spot])

    def d_start(target):
        far = spot != target
        pl.when(far)(d_copy(target).start)
        pl.when(jnp.logical_not(far))(d_near(target).start)

    for n in range(2):
        d_start(pairs + n)

    lane = lax.broadcasted_iota(jnp.int32, (rows, 128), 1)
    masks = [(lane < HEAD).astype(F32).astype(BF), (lane >= HEAD).astype(F32).astype(BF)]
    score_scale = HEAD ** (-0.5)

    def head_pair(n, carry):
        cols = pl.ds(pl.multiple_of(n * 128, 128), 128)
        q2, k2, v2, da2 = q[:, cols], k[:, cols], v[:, cols], datt[:, cols]
        sums = [jnp.zeros((rows, 128), F32) for _ in range(3)]
        for side in range(2):
            mask = masks[side]
            da = da2 * mask
            p = probs[2 * n + side]
            dpb = dot(da, v2, NT)
            delta = jnp.sum(p * dpb, axis=-1, keepdims=True)
            ds = (p * (dpb - delta)).astype(BF)
            sums[0] += dot(ds, k2 * mask, NN)
            sums[1] += dot(ds, q2 * mask, TN)
            sums[2] += dot(p.astype(BF), da, TN)
        low = [(sums[0] * score_scale).astype(BF), (sums[1] * score_scale).astype(BF), sums[2].astype(BF)]
        for m, (value, full) in enumerate(zip(low, (dq, dk, dv))):
            dsend[n, :, m * 128:(m + 1) * 128] = value
            full[:, cols] = value
        d_start(n)
        return carry

    lax.fori_loop(0, pairs, head_pair, 0)

    d_one = dot(dq[...], wd[0], NT) + dot(dk[...], wd[1], NT) + dot(dv[...], wd[2], NT)
    d_norm, g_gain, g_bias = norm_back(tokens[...].astype(F32), gain_one, d_one)
    grad_tokens[...] = (dres[...] + d_norm).astype(BF)
    small[nrouter:nrouter + 1, :] = g_gain
    small[nrouter + 1:nrouter + 2, :] = g_bias

    hops = [at.sib, at.xn, at.yn]
    for n in range(upper):
        bit = 8 << n
        hops.append(i + bit - 2 * bit * lax.rem(lax.div(i, bit), 2))
    moves = [(z, t) for t in hops]
    for n in range(planes.bit_length() - 1):
        bit = 1 << n
        moves.append((z + bit - 2 * bit * lax.rem(lax.div(z, bit), 2), i))
    small_copies = []

    def small_start(n):
        if n >= 2:
            small_copies[n - 2].wait_send()
        sms[n % 2] = small[...]
        copy = send_to(sms.at[n % 2], smr.at[n], ms.at[n], mr.at[n], moves[n][0], moves[n][1])
        copy.start()
        small_copies.append(copy)

    def small_step(n):
        small_copies[n].wait_recv()
        small[...] = small[...] + smr[n]
        if n + 1 < len(moves):
            small_start(n + 1)

    small_start(0)

    small_step(0)

    def d_wait(source, carry):
        send_to(gd.at[source], gd.at[source], sd.at[source], rd.at[source], z, i).wait_recv()
        return carry

    lax.fori_loop(0, 8, d_wait, 0)
    columns = gd.shape[2]
    total = jnp.zeros((width, columns), F32)
    sources = ga_rows // rows
    for g in range(ga_groups):
        fetch_ga[g].wait()
        total += dot(
            hid[0:ga_rows, g * width:(g + 1) * width],
            gd[g * sources:(g + 1) * sources].reshape(ga_rows, columns), TN,
        )
    gsum[...] = total.reshape(planes, width // planes, columns)
    small_step(1)
    tail = []
    for n in range(upper):
        szb[...] = gsum[...].astype(BF)
        copy = send_to(szb, rup.at[n], us.at[n], ur.at[n], z, hops[3 + n])
        copy.start()
        copy.wait_recv()
        gsum[...] = szb[...].astype(F32) + rup[n].astype(F32)
        copy.wait_send()
    szb[...] = gsum[...].astype(BF)
    partner = z + 1 - 2 * lax.rem(z, 2)
    others = 2 - 2 * lax.div(z, 2)
    outer = jnp.logical_not(host)
    copy = send_to(szb.at[partner], rzb.at[0], zs.at[0], zr.at[0], partner, i)
    copy.start()
    tail.append(copy)
    inward = [
        send_to(szb.at[others + n], rzb.at[2 + n], zs.at[1 + n], zr.at[2 + n], partner, i) for n in range(2)
    ]
    across = [
        send_to(szb.at[others + n], rzb.at[1], zs.at[1 + n], zr.at[1], others + n, i) for n in range(2)
    ]

    @pl.when(outer)
    def _():
        for copy in inward:
            copy.start()

    @pl.when(host)
    def _():
        for n in range(2):
            inward[n].wait_recv()
            szb[others + n] = (gsum[others + n] + rzb[2 + n].astype(F32)).astype(BF)
            across[n].start()

    shipments += [(outer, copy) for copy in inward] + [(host, copy) for copy in across]
    for p in (1, 2):
        ship(p, 1)
    small_step(2)

    def y_finish(step, carry):
        source = lax.rem(at.me + chips - step, chips)
        send_to(landing(source), landing(source), ys.at[step], yr.at[step], z, i).wait_recv()
        y_copy(step).wait_send()
        return carry

    y_own.wait()
    lax.fori_loop(1, chips, y_finish, 0)
    fetch = pltpu.make_async_copy(yland, landed_rows, yl.at[1])
    fetch.start()
    fetch.wait()
    y_all = landed_rows[...]
    mixed = gates[0] * dot(place[0], y_all, NN) + gates[1] * dot(place[1], y_all, NN)
    block_out[...] = (resid[...] + mixed).astype(BF)

    fin = gsum[z]
    for n in range(2):
        send_to(rzb.at[n], rzb.at[n], zs.at[n], zr.at[n], z, i).wait_recv()
        fin = fin + rzb[n].astype(F32)
    fb[spot] = fin.astype(BF)
    px, py = spot + 2 - 4 * at.xb, spot + 4 - 8 * at.yb
    pd = px + 4 - 8 * at.yb
    flip = 1 - 2 * core

    def pass_on(where, step, target):
        copy = send_to(fb.at[where], fb.at[where], gs.at[step], gr.at[step], z, target)
        copy.start()
        tail.append(copy)

    def landed(where, step):
        send_to(fb.at[where], fb.at[where], gs.at[step], gr.at[step], z, i).wait_recv()

    pass_on(spot, 0, at.xn)
    pass_on(spot, 1, at.yn)
    pass_on(spot, 2, at.sib)
    small_step(3)
    landed(px, 0)
    landed(py, 1)
    pass_on(px + core * (py - px), 3, at.yn + core * (at.xn - at.yn))
    pass_on(px, 4, at.sib)
    pass_on(py, 5, at.sib)
    for n in range(4, len(moves)):
        small_step(n)
    osmall[...] = small[...]
    landed(pd, 3)
    pass_on(pd, 6, at.sib)
    for h in range(2):
        send_to(wi.at[h], wi.at[h], hs.at[0, 0], hr.at[h, 0], z, i).wait_recv()
        send_to(wo.at[h], wo.at[h], hs.at[0, 1], hr.at[h, 1], z, i).wait_recv()
    landed(spot + flip, 2)
    landed(px + flip, 4)
    landed(py + flip, 5)
    landed(pd + flip, 6)
    for copy in tail + small_copies[-2:]:
        copy.wait_send()
    def d_sent(target, carry):
        pl.when(spot != target)(d_copy(target).wait_send)
        return carry

    lax.fori_loop(0, 8, d_sent, 0)

    @pl.when(host)
    def _():
        for copy in pair[0] + pair[1]:
            copy.wait_send()

    for is_far, copy in shipments:
        pl.when(is_far)(copy.wait_send)

    def dx_sent(step, carry):
        target = lax.rem(at.me + step, at.chips)
        for copy in copies(lax.div(target, per_plane), lax.rem(target, per_plane)):
            copy.wait_send()
        return carry

    lax.fori_loop(1, at.chips, dx_sent, 0)


def rear(planes, experts, nrouter, x, do, gate, back_in, win, wout, ga):
    rows, width = back_in[0].shape
    chips, padded, _ = x.shape
    slots = chips * padded
    ff = win.shape[1]
    pieces, blocks = (1, 4) if experts <= 8 else (2, 8)
    ga_groups = ff // width
    share, fshare, half = width // planes, ff // planes, width // 2
    upper = max(experts.bit_length() - 4, 1)
    nbits = experts.bit_length() - 1 + planes.bit_length() - 1
    dma = pltpu.SemaphoreType.DMA
    vm = pltpu.VMEM
    sds = jax.ShapeDtypeStruct
    return pl.pallas_call(
        functools.partial(rear_kernel, planes, experts, padded, pieces, blocks, ga_groups, nrouter),
        out_shape=(
            sds((rows, width), BF),
            sds((rows, width), BF),
            sds((8, share, half), BF),
            sds((nrouter + 16, width), F32),
            sds((2, share // 2, ff), BF),
            sds((2, fshare // 2, width), BF),
            sds((slots, width), BF),
            sds((slots, width), BF),
        ),
        in_specs=[vmem_spec()] * 3 + [any_spec()] * 14,
        out_specs=(vmem_spec(),) * 4 + (any_spec(),) * 4,
        scratch_shapes=[vm(a.shape, a.dtype) for a in back_in] + [
            vm((width, ff), BF),
            vm((ff, width), BF),
            vm((slots, width), BF),
            vm((slots, ff), BF),
            vm((slots, ff), BF),
            vm((chips, padded, width), BF),
            vm((chips, 1, 128), F32),
            vm((chips, 1, 128), F32),
            vm((chips, padded, width), BF),
            vm((slots, width), BF),
            vm((8, rows, half), BF),
            vm((8, rows, half), BF),
            vm((rows, width), F32),
            vm((planes, share, half), F32),
            vm((planes, share, half), BF),
            vm((4, share, half), BF),
            vm((upper, planes, share, half) if experts > 8 else (1, 8, 128), BF),
            vm((2, nrouter + 16, width), F32),
            vm((nbits, nrouter + 16, width), F32),
            vm((nrouter + 16, width), F32),
            vm((planes, share // 2, ff), BF),
            vm((planes, fshare // 2, width), BF),
            dma((2,)), dma((2, chips)), dma((2, chips)), dma((2,)), dma((ga_groups,)),
            dma((2, planes)), dma((2, planes)),
            dma((planes, 2)), dma((2, 2)),
            dma((chips,)), dma((chips,)), dma((2,)),
            dma((8,)), dma((8,)),
            dma((upper,)), dma((upper,)),
            dma((3,)), dma((4,)),
            dma((7,)), dma((7,)), dma((nbits,)), dma((nbits,)), dma((11,)),
        ],
        compiler_params=pltpu.CompilerParams(
            collective_id=2, has_side_effects=True, vmem_limit_bytes=REAR_LIMIT
        ),
        name="rear",
    )(x.reshape(slots, width), do.reshape(slots, width), gate, *back_in, win, wout, ga.reshape(8 * rows, width))


def finish_kernel(planes, nrouter, block_out, grad_tokens, fb, small, wi, wo,
                  ob, ot, o0, o1, o2, o3, og, v0, v1, v2, v3, ogi, ogo,
                  s0, s1, s2, s3, sg, sv, si, so, sem):
    z = lax.axis_index("dp")
    share = s0.shape[0]
    pairs = s0.shape[1] // 128
    half = s0.shape[1] // 2
    copies = []

    def write(source, target):
        copy = pltpu.make_async_copy(source, target, sem.at[len(copies)])
        copy.start()
        copies.append(copy)

    write(block_out, ob)
    write(grad_tokens, ot)
    for wide, low, out in ((si, wi, ogi), (so, wo, ogo)):
        chunk = low.shape[1]
        for h in range(2):
            wide[h * chunk:(h + 1) * chunk, :] = low[h].astype(F32)
            write(wide.at[pl.ds(h * chunk, chunk), :], out.at[pl.ds(h * chunk, chunk), :])
    for m, (stage, out) in enumerate(((s0, o0), (s1, o1), (s2, o2))):
        for n in range(pairs):
            stage[:, n * 128:(n + 1) * 128] = fb[n, :, m * 128:(m + 1) * 128].astype(F32)
        write(stage, out)
    for n in range(2):
        s3[:, n * half:(n + 1) * half] = fb[pairs + n].astype(F32)
    write(s3, o3)
    mine = small[:, 0:share]
    for p in range(1, planes):
        mine = jnp.where(z == p, small[:, p * share:(p + 1) * share], mine)
    sg[...] = mine[0:nrouter]
    write(sg, og)
    for n, out in enumerate((v0, v1, v2, v3)):
        sv[n] = mine[nrouter + n:nrouter + n + 1]
        write(sv.at[n], out)
    for copy in copies:
        copy.wait()


def finish(planes, nrouter, block_out, grad_tokens, fb, small, wi, wo):
    rows, width = block_out.shape
    _, share, half = fb.shape
    ff = wi.shape[2]
    fshare = 2 * wo.shape[1]
    vm = pltpu.VMEM
    sds = jax.ShapeDtypeStruct
    dense = ((share, width),) * 4 + ((nrouter, share),)
    wide = ((share, ff), (fshare, width))
    results = dense + ((1, share),) * 4 + wide
    stages = dense + ((4, 1, share),) + wide
    return pl.pallas_call(
        functools.partial(finish_kernel, planes, nrouter),
        out_shape=(sds((rows, width), BF),) * 2 + tuple(sds(shape, F32) for shape in results),
        in_specs=[vmem_spec()] * 6,
        out_specs=(any_spec(),) * 13,
        scratch_shapes=[vm(shape, F32) for shape in stages] + [pltpu.SemaphoreType.DMA((16,))],
        compiler_params=pltpu.CompilerParams(vmem_limit_bytes=VMEM_LIMIT),
        name="finish",
    )(block_out, grad_tokens, fb, small, wi, wo)


def shards(planes, experts, tokens, segment_ids, routes, ln1_gain, ln1_bias, ln2_gain, ln2_bias,
           w_query, w_key, w_value, w_output, w_router, frozen_in, frozen_out, new_in, new_out,
           cotangent):
    rows, width = tokens.shape
    expert_count = w_router.shape[1]
    capacity = 5 * rows // (2 * expert_count)
    padded = -(-capacity // 8) * 8
    (wd, pk, win, wout, act_two, q, k, v, resid, probs, aux, ga, x_recv, do_recv, g_recv) = front(
        planes, experts, capacity, padded, expert_count, tokens, cotangent, segment_ids, routes,
        w_router, (ln1_gain, ln1_bias, ln2_gain, ln2_bias),
        w_query, w_key, w_value, w_output, frozen_in, frozen_out, new_in, new_out,
    )
    block_out, grad_tokens, dense, small, low_in, low_out, _, _ = rear(
        planes, experts, expert_count, x_recv, do_recv, g_recv,
        (tokens, cotangent, aux, act_two, q, k, v, resid, probs, wd, pk), win, wout, ga,
    )
    block_out, grad_tokens, oq, ok, ov, ow, router, *norms, ogi, ogo = finish(
        planes, expert_count, block_out, grad_tokens, dense, small, low_in, low_out
    )
    norms = [norm.reshape(width // planes) for norm in norms]
    return (
        block_out, grad_tokens, oq, ok, ov, ow, router.T,
        norms[0], norms[1], norms[2], norms[3], ogi[None], ogo[None],
    )


def solution(mesh):
    rows = P(("dp", "expert"), None)
    in_specs = (rows, rows, rows) + (P("dp"),) * 4 + (P("dp", None),) * 5
    in_specs += (P("expert", "dp", None),) * 4 + (rows,)
    out_specs = (rows, rows) + (P("dp", None),) * 5 + (P("dp"),) * 4
    out_specs += (P("expert", "dp", None),) * 2
    body = functools.partial(shards, mesh.shape["dp"], mesh.shape["expert"])
    return jax.shard_map(body, mesh=mesh, in_specs=in_specs, out_specs=out_specs, check_vma=False)
```

```python
import functools

import jax
import jax.numpy as jnp
from jax import lax
from jax.experimental import pallas as pl
from jax.experimental.pallas import tpu as pltpu
from jax.sharding import PartitionSpec as P

HEADS = 12
HEAD = 64
NORM_EPS = 1e-05
MASKED = -1e30
MESH = pl.DeviceIdType.MESH
BF = jnp.bfloat16
F32 = jnp.float32
VMEM_LIMIT = 60 * 1024 * 1024
REAR_LIMIT = 67043328


class Place:
    def __init__(self, planes, experts):
        self.planes, self.experts = planes, experts
        self.z = lax.axis_index("dp")
        self.i = lax.axis_index("expert")
        self.core = lax.rem(self.i, 2)
        self.chip = lax.div(self.i, 2)
        self.xb = lax.rem(self.chip, 2)
        self.yb = lax.rem(lax.div(self.i, 4), 2)
        self.sib = self.i + 1 - 2 * self.core
        self.xn = self.i + 2 - 4 * self.xb
        self.yn = self.i + 4 - 8 * self.yb
        self.chips = planes * (experts // 2)
        self.me = self.z * (experts // 2) + self.chip


def send_to(src, dst, send_sem, recv_sem, z, i):
    return pltpu.make_async_remote_copy(
        src_ref=src,
        dst_ref=dst,
        send_sem=send_sem,
        recv_sem=recv_sem,
        device_id={"dp": z, "expert": i},
        device_id_type=MESH,
    )


def greet(at):
    barrier = pltpu.get_barrier_semaphore()
    count = at.planes * at.experts
    own = at.z * at.experts + at.i

    def signal(step, carry):
        target = lax.rem(own + step, count)
        pl.semaphore_signal(
            barrier,
            inc=1,
            device_id={"dp": lax.div(target, at.experts), "expert": lax.rem(target, at.experts)},
            device_id_type=MESH,
        )
        return carry

    lax.fori_loop(1, count, signal, 0)
    return lambda: pl.semaphore_wait(barrier, count - 1)


def any_spec():
    return pl.BlockSpec(memory_space=pl.ANY)


def vmem_spec():
    return pl.BlockSpec(memory_space=pltpu.VMEM)


NN = ((1,), (0,))
NT = ((1,), (1,))
TN = ((0,), (0,))


def dot(left, right, contract, out=F32):
    return lax.dot_general(
        left, right, ((contract[0], contract[1]), ((), ())), preferred_element_type=F32
    ).astype(out)


def exact_dot(left, right, contract):
    return lax.dot_general(
        left, right, ((contract[0], contract[1]), ((), ())),
        preferred_element_type=F32, precision=lax.Precision.HIGHEST,
    )


def norm_parts(rows):
    centred = rows - jnp.mean(rows, axis=-1, keepdims=True)
    variance = jnp.mean(centred * centred, axis=-1, keepdims=True)
    scale = lax.rsqrt(variance + NORM_EPS)
    return centred * scale, scale


def norm_back(rows, gain, grad):
    unit, scale = norm_parts(rows)
    scaled = grad * gain
    inner = scaled - jnp.mean(scaled, axis=-1, keepdims=True)
    inner = inner - unit * jnp.mean(scaled * unit, axis=-1, keepdims=True)
    return scale * inner, jnp.sum(grad * unit, axis=0, keepdims=True), jnp.sum(grad, axis=0, keepdims=True)


def slot_places(slot, slots):
    lanes = lax.broadcasted_iota(jnp.int32, (slot[0].shape[0], slots), 1).astype(F32)
    return [(lanes == one).astype(F32).astype(BF) for one in slot]


def slot_values(aux, table, padded, chips):
    rows = aux.shape[0]
    low = lax.broadcasted_iota(jnp.int32, (rows, chips), 1).astype(F32) * padded
    lanes = lax.broadcasted_iota(jnp.int32, (rows, table.shape[1]), 1).astype(F32)
    found = []
    for k in range(2):
        slot = aux[:, 2 + k:3 + k]
        mine = jnp.logical_and(slot >= low, slot < low + padded).astype(F32)
        position = slot - jnp.sum(mine * low, axis=1, keepdims=True)
        picked = exact_dot(mine, table, NN)
        found.append(jnp.sum(jnp.where(lanes == position, picked, 0.0), axis=1, keepdims=True))
    return found


def front_kernel(planes, experts, capacity, padded, nrouter,
                 tokens, cot, segs, routes, router, g1, b1, g2, b2, wq, wk, wv, wo, fi, fo, ni, no,
                 owd, pk, win, wout, oact, oq, ok, ov, oresid, oprobs, aux, ga,
                 xland, dland, gland,
                 wd, act_one, act_two, q, k, v, att, resid, probs, packs, allow, xsend, esend, gsend, dstage, istage, ostage, ibf, obf,
                 ld, zs, zr, ps, pr, gs, gr, es, er, fs, fr, ts, tr, tl, sa, ra, sv, zf):
    at = Place(planes, experts)
    z, i, core = at.z, at.i, at.core
    rows, width = tokens.shape
    chips = at.chips
    per_plane = experts // 2
    share = dstage.shape[1]
    quarter = share // 4
    half = width // 2
    fhalf = istage.shape[2] // 2
    oshare = ostage.shape[1]
    ohalf = oshare // 2
    pairs = width // 128
    spot = lax.rem(i, 8)
    base = i - spot
    loads = [pltpu.make_async_copy(w, dstage.at[m], ld.at[m]) for m, w in enumerate((wq, wk, wv, wo))]
    loads += [
        pltpu.make_async_copy(fi.at[0], istage.at[0], ld.at[4]),
        pltpu.make_async_copy(ni.at[0], istage.at[1], ld.at[5]),
        pltpu.make_async_copy(fo.at[0], ostage.at[0], ld.at[6]),
        pltpu.make_async_copy(no.at[0], ostage.at[1], ld.at[7]),
    ]
    for load in loads:
        load.start()
    met = greet(at)
    zrow = pl.multiple_of(z * share, share)
    for m in range(4):
        loads[m].wait()
        wd[m, pl.ds(zrow, share), :] = dstage[m].astype(BF)
    packs[z, 0:nrouter, :] = router[...].astype(BF)
    norm_row = lax.broadcasted_iota(jnp.int32, (16, share), 0)
    norms = jnp.zeros((16, share), F32)
    for n, values in enumerate((g1, b1, g2, b2)):
        norms = jnp.where(norm_row == n, values[...], norms)
    packs[z, nrouter:nrouter + 16, :] = norms.astype(BF)
    met()

    def block(plane, row_quarter, column_half):
        return wd.at[
            :,
            pl.ds(pl.multiple_of(plane * share + row_quarter * quarter, 16), quarter),
            pl.ds(pl.multiple_of(column_half * half, 128), half),
        ]

    rq = 2 * at.yb + core
    rqy = 2 * (1 - at.yb) + core
    rqs = 2 * at.yb + 1 - core
    rqys = 2 * (1 - at.yb) + 1 - core
    xb, xo = at.xb, 1 - at.xb
    started, remote_sends = [], []
    for j in range(1, planes):
        zt = lax.rem(z + j, planes)
        mine = block(z, rq, xb)
        copy = send_to(mine, mine, zs.at[j - 1], zr.at[j - 1], zt, i)
        direct = jnp.logical_or(lax.div(zt, 2) == lax.div(z, 2), jnp.logical_and(zt >= 1, zt <= 2))
        pl.when(direct)(copy.start)
        remote_sends.append((direct, copy))
        copy = send_to(packs.at[z], packs.at[z], ps.at[j - 1], pr.at[j - 1], zt, i)
        copy.start()
        started.append(copy)

    def cast(source, target, kind, chunk):
        def step(n, carry):
            part = pl.ds(pl.multiple_of(n * chunk, chunk), chunk)
            target[kind, part, :] = source[kind, part, :].astype(BF)
            return carry

        lax.fori_loop(0, source.shape[1] // chunk, step, 0)

    def in_block(plane, h):
        return win.at[
            pl.ds(pl.multiple_of(plane * share, 16), share),
            pl.ds(pl.multiple_of(h * fhalf, 128), fhalf),
        ]

    def out_block(plane, h):
        return wout.at[pl.ds(pl.multiple_of(plane * oshare + h * ohalf, 16), ohalf), :]


    def ship(kind, h, which):
        zh = 3 * core if kind == 0 else 1 + core
        remote = jnp.logical_or(zh != z, core != h)
        src = (
            ibf.at[kind, :, pl.ds(h * fhalf, fhalf)]
            if which == 0
            else obf.at[kind, pl.ds(h * ohalf, ohalf), :]
        )
        dst = in_block(z, h) if which == 0 else out_block(z, h)
        far = send_to(src, dst, es.at[kind, h, which], er.at[z, which], zh, 2 * at.chip + h)
        near = pltpu.make_async_copy(src, dst, er.at[z, which])
        pl.when(remote)(far.start)
        pl.when(jnp.logical_not(remote))(near.start)
        remote_sends.append((remote, far))

    def ship_in(kind):
        loads[4 + kind].wait()
        cast(istage, ibf, kind, 16)
        for h in range(2):
            ship(kind, h, 0)

    ship_in(1)
    end = 3 * (z - 1)
    handed = []
    for j in range(1, planes):
        zz = lax.rem(z + planes - j, planes)
        hand = jnp.logical_and(lax.div(zz, 2) != lax.div(z, 2), jnp.logical_and(z >= 1, z <= 2))
        mine = block(zz, rq, xb)
        there = lax.rem(end + planes - zz, planes)
        copy = send_to(mine, mine, zf.at[j - 1], zr.at[jnp.maximum(there, 1) - 1], jnp.clip(end, 0, planes - 1), i)

        @pl.when(hand)
        def _():
            send_to(mine, mine, zs.at[j - 1], zr.at[j - 1], z, i).wait_recv()
            copy.start()

        handed.append(hand)
        remote_sends.append((hand, copy))
    ship_in(0)

    shift = experts.bit_length() - 1
    above = lax.broadcasted_iota(jnp.int32, (rows, rows), 0)
    across = lax.broadcasted_iota(jnp.int32, (rows, rows), 1)
    segment = segs[...].astype(F32)
    fact_row = lax.broadcasted_iota(jnp.int32, (8, rows), 0)
    facts = jnp.zeros((8, rows), F32)
    for n, values in enumerate((routes[0:1, :].astype(F32), routes[1:2, :].astype(F32), segment)):
        facts = jnp.where(fact_row == n, values, facts)
    fact_columns = dot((above == across).astype(F32).astype(BF), facts.astype(BF), NT)
    route_columns = [fact_columns[:, n:n + 1] for n in range(2)]
    route = fact_columns.astype(jnp.int32)
    expert = jnp.bitwise_and(route, experts - 1)
    kind = jnp.right_shift(route, shift)
    host_plane = jnp.where(jnp.bitwise_and(expert, 1) == 0, kind, 3 - kind)
    host = host_plane * per_plane + jnp.right_shift(expert, 1)
    chip_iota = lax.broadcasted_iota(jnp.int32, (rows, chips), 1)
    chosen = [(chip_iota == host[:, n:n + 1]).astype(F32) for n in range(2)]
    earlier = (across < above).astype(F32).astype(BF)
    before = dot(earlier, (chosen[0] + chosen[1]).astype(BF), NN)
    position = [jnp.sum(one * before, axis=1, keepdims=True) for one in chosen]
    slot = [
        jnp.where(position[n] < capacity, host[:, n:n + 1].astype(F32) * padded + position[n], -1.0)
        for n in range(2)
    ]
    place = slot_places(slot, chips * padded)
    both = place[0] + place[1]

    def fill(target, values):
        sent = dot(both, values, TN)
        for n in range(chips):
            target[n] = sent[n * padded:(n + 1) * padded].astype(BF)

    def token_copy(src, dst, which, step):
        target = lax.rem(at.me + step, chips)
        zt, it = lax.div(target, per_plane), 2 * lax.rem(target, per_plane) + core
        return send_to(src.at[target], dst.at[at.me], ts.at[which, step], tr.at[which, step], zt, it)

    def token_start(src, dst, which):
        pltpu.make_async_copy(src.at[at.me], dst.at[at.me], tl.at[which]).start()

        def step(n, carry):
            token_copy(src, dst, which, n).start()
            return carry

        lax.fori_loop(1, chips, step, 0)

    def token_finish(src, dst, which):
        def step(n, carry):
            source = lax.rem(at.me + chips - n, chips)
            send_to(
                src.at[source], dst.at[source], ts.at[which, n], tr.at[which, n], z, i
            ).wait_recv()
            token_copy(src, dst, which, n).wait_send()
            return carry

        lax.fori_loop(1, chips, step, 0)
        pltpu.make_async_copy(src.at[at.me], dst.at[at.me], tl.at[which]).wait()

    fill(esend, cot[...])
    token_start(esend, dland, 0)
    for n, kind in ((6, 0), (7, 1)):
        loads[n].wait()
        cast(ostage, obf, kind, 32)
        for h in range(2):
            ship(kind, h, 1)
    same = jnp.logical_and(fact_columns[:, 2:3] == segment, across <= above)
    allow[...] = same.astype(F32)

    def pass_on(src, j, step, target):
        copy = send_to(src, src, gs.at[j - 1, step], gr.at[j - 1, step], z, target)
        copy.start()
        started.append(copy)

    def landed(dst, j, step):
        send_to(dst, dst, gs.at[j - 1, step], gr.at[j - 1, step], z, i).wait_recv()

    for j in range(1, planes):
        zz = lax.rem(z + planes - j, planes)
        mine = block(zz, rq, xb)
        arrival = send_to(mine, mine, zs.at[j - 1], zr.at[j - 1], z, i)
        pl.when(jnp.logical_not(handed[j - 1]))(arrival.wait_recv)
        pass_on(mine, j, 0, at.xn)
        pass_on(mine, j, 1, at.yn)
        pass_on(mine, j, 2, at.sib)
        send_to(packs.at[zz], packs.at[zz], ps.at[j - 1], pr.at[j - 1], z, i).wait_recv()
    pk[...] = jnp.concatenate([packs[p] for p in range(planes)], axis=1)

    x = tokens[...].astype(F32)
    gain = pk[nrouter:nrouter + 1, :].astype(F32)
    bias = pk[nrouter + 1:nrouter + 2, :].astype(F32)
    act_one[...] = (norm_parts(x)[0] * gain + bias).astype(BF)

    for j in range(1, planes):
        zz = lax.rem(z + planes - j, planes)
        bx, by = block(zz, rq, xo), block(zz, rqy, xb)
        landed(bx, j, 0)
        landed(by, j, 1)
        onward = block(zz, rq + core * (rqy - rq), xo + core * (xb - xo))
        pass_on(onward, j, 3, at.yn + core * (at.xn - at.yn))
        pass_on(bx, j, 4, at.sib)
        pass_on(by, j, 5, at.sib)
    for j in range(1, planes):
        zz = lax.rem(z + planes - j, planes)
        bd = block(zz, rqy, xo)
        landed(bd, j, 3)
        pass_on(bd, j, 6, at.sib)
    for j in range(1, planes):
        zz = lax.rem(z + planes - j, planes)
        landed(block(zz, rqs, xb), j, 2)
        landed(block(zz, rqs, xo), j, 4)
        landed(block(zz, rqys, xb), j, 5)
        landed(block(zz, rqys, xo), j, 6)

    def act_copy(step, whole):
        target = lax.rem(spot + step, 8)
        src = act_one if whole else att
        return target, send_to(src, ga.at[spot], sa.at[step], ra.at[step], z, base + target)

    def act_near(whole):
        return pltpu.make_async_copy(act_one if whole else att, ga.at[spot], tl.at[3])

    for step in range(1, 8):
        target, copy = act_copy(step, True)
        pl.when(target < pairs)(copy.start)
    pl.when(spot < pairs)(act_near(True).start)

    one = act_one[...]
    q[...] = dot(one, wd[0], NN, BF)
    k[...] = dot(one, wd[1], NN, BF)
    v[...] = dot(one, wd[2], NN, BF)
    lane = lax.broadcasted_iota(jnp.int32, (rows, 128), 1)
    masks = [(lane < HEAD).astype(F32).astype(BF), (lane >= HEAD).astype(F32).astype(BF)]
    score_scale = HEAD ** (-0.5)

    def head_pair(n, carry):
        cols = pl.ds(pl.multiple_of(n * 128, 128), 128)
        q2, k2, v2 = q[:, cols], k[:, cols], v[:, cols]
        total = jnp.zeros((rows, 128), F32)
        for side in range(2):
            scores = dot(q2 * masks[side], k2, NT) * score_scale
            scores = jnp.where(allow[...] > 0.5, scores, MASKED)
            expo = jnp.exp(scores - jnp.max(scores, axis=-1, keepdims=True))
            p = expo / jnp.sum(expo, axis=-1, keepdims=True)
            probs[2 * n + side] = p
            total += dot(p.astype(BF), v2 * masks[side], NN)
        att[:, cols] = total.astype(BF)
        return carry

    lax.fori_loop(0, pairs, head_pair, 0)
    residual = x + dot(att[...], wd[3], NN)
    resid[...] = residual
    gain = pk[nrouter + 2:nrouter + 3, :].astype(F32)
    bias = pk[nrouter + 3:nrouter + 4, :].astype(F32)
    two = (norm_parts(residual)[0] * gain + bias).astype(BF)
    act_two[...] = two
    fill(xsend, two)
    token_start(xsend, xland, 1)
    for step in range(1, 8):
        target, copy = act_copy(step, False)
        pl.when(target >= pairs)(copy.start)
    pl.when(spot >= pairs)(act_near(False).start)

    logits = dot(two, pk[0:nrouter, :], NT)
    route_iota = lax.broadcasted_iota(jnp.int32, (rows, nrouter), 1)
    picked = [
        jnp.sum(jnp.where(route_iota == route[:, n:n + 1], logits, 0.0), axis=1, keepdims=True)
        for n in range(2)
    ]
    top = jnp.maximum(picked[0], picked[1])
    lifted = [jnp.exp(one_pick - top) for one_pick in picked]
    gates = [one_lift / (lifted[0] + lifted[1]) for one_lift in lifted]
    values = jnp.zeros((rows, 128), F32)
    for n, column in enumerate(gates + slot + route_columns):
        values = jnp.where(lane == n, column, values)
    aux[...] = values
    lanes = lane.astype(F32)
    table = jnp.zeros((chips, 128), F32)
    for n in range(2):
        kept = jnp.logical_and(lanes == position[n], position[n] < capacity)
        table += exact_dot(chosen[n], jnp.where(kept, gates[n], 0.0), TN)
    for n in range(chips):
        gsend[n] = table[n:n + 1]
    token_start(gsend, gland, 2)
    kept_arrays = ((wd, owd), (act_two, oact), (q, oq), (k, ok), (v, ov), (resid, oresid), (probs, oprobs))
    saves = [pltpu.make_async_copy(src, dst, sv.at[n]) for n, (src, dst) in enumerate(kept_arrays)]
    for copy in saves:
        copy.start()

    def hand_on(plane, which):
        blk = in_block(plane, core) if which == 0 else out_block(plane, core)
        send_to(blk, blk, es.at[0, 0, which], er.at[plane, which], z, i).wait_recv()
        copy = send_to(blk, blk, fs.at[plane, which], fr.at[plane, which], z, at.sib)
        copy.start()
        started.append(copy)

    for which in range(2):
        for plane in range(planes):
            hand_on(plane, which)
    for src, dst, which in ((esend, dland, 0), (xsend, xland, 1), (gsend, gland, 2)):
        token_finish(src, dst, which)
    for step in range(1, 8):
        source = lax.rem(spot + 8 - step, 8)
        send_to(act_one, ga.at[source], sa.at[step], ra.at[step], z, i).wait_recv()
        act_copy(step, True)[1].wait_send()
    act_near(True).wait()
    for which in range(2):
        for plane in range(planes):
            blk = in_block(plane, 1 - core) if which == 0 else out_block(plane, 1 - core)
            send_to(blk, blk, fs.at[plane, which], fr.at[plane, which], z, i).wait_recv()
    for copy in started:
        copy.wait_send()
    for remote, far in remote_sends:
        pl.when(remote)(far.wait_send)
    for copy in saves:
        copy.wait()


def front(planes, experts, capacity, padded, nrouter, tokens, cot, segment_ids, routes, router, norms,
          wq, wk, wv, wo, fi, fo, ni, no):
    rows, width = tokens.shape
    share = wq.shape[0]
    ff = fi.shape[2]
    oshare = fo.shape[1]
    chips = planes * experts // 2
    dma = pltpu.SemaphoreType.DMA
    vm = pltpu.VMEM
    sds = jax.ShapeDtypeStruct
    flat = sds((rows, width), BF)
    slab = sds((chips, padded, width), BF)
    return pl.pallas_call(
        functools.partial(front_kernel, planes, experts, capacity, padded, nrouter),
        out_shape=(
            sds((4, width, width), BF),
            sds((nrouter + 16, width), BF),
            sds((width, ff), BF),
            sds((ff, width), BF),
            flat, flat, flat, flat,
            sds((rows, width), F32),
            sds((HEADS, rows, rows), F32),
            sds((rows, 128), F32),
            sds((8, rows, width), BF),
            slab,
            slab,
            sds((chips, 1, 128), F32),
        ),
        in_specs=[vmem_spec()] * 9 + [any_spec()] * 8,
        out_specs=(any_spec(), vmem_spec()) + (any_spec(),) * 8 + (vmem_spec(),) + (any_spec(),) * 4,
        scratch_shapes=[
            vm((4, width, width), BF),
        ] + [vm((rows, width), BF)] * 6 + [
            vm((rows, width), F32),
            vm((HEADS, rows, rows), F32),
            vm((planes, nrouter + 16, share), BF),
            vm((rows, rows), F32),
            vm((chips, padded, width), BF),
            vm((chips, padded, width), BF),
            vm((chips, 1, 128), F32),
            vm((4, share, width), F32),
            vm((2, share, ff), F32),
            vm((2, oshare, width), F32),
            vm((2, share, ff), BF),
            vm((2, oshare, width), BF),
            dma((8,)),
            dma((planes - 1,)), dma((planes - 1,)), dma((planes - 1,)), dma((planes - 1,)),
            dma((planes - 1, 7)), dma((planes - 1, 7)),
            dma((2, 2, 2)), dma((planes, 2)), dma((planes, 2)), dma((planes, 2)),
            dma((3, chips)), dma((3, chips)), dma((4,)), dma((8,)), dma((8,)), dma((7,)), dma((planes - 1,)),
        ],
        compiler_params=pltpu.CompilerParams(
            collective_id=0, has_side_effects=True, vmem_limit_bytes=VMEM_LIMIT
        ),
        name="front",
    )(tokens, cot, segment_ids, routes.T, router.T, *[norm.reshape(1, share) for norm in norms],
      wq, wk, wv, wo, fi, fo, ni, no)


GELU_SCALE = 0.7978845608028654
GELU_CUBE = 0.044715


def rear_kernel(planes, experts, padded, pieces, blocks, ga_groups, nrouter,
                x, do, gate, *refs):
    back_in, refs = refs[:11], refs[11:]
    (win, wout, ga,
                block_out, grad_tokens, fb, osmall, wi, wo, yland, dxland,
                tokens, cot, aux, act_two, q, k, v, resid, probs, wd, pk,
                hwi, hwo, dy, hid, dpre, dxsend, dgsend, dgland, ysend, landed_rows,
                gd, dsend, dres, gsum, szb, rzb, rup,
                sms, smr, small, ri, ro,
                ls, ts, tr, tl, gl,
                es, er, hs, hr, ys, yr, yl, sd, rd, us, ur, zs, zr, gs, gr, ms, mr, lb) = refs
    back_held = (tokens, cot, aux, act_two, q, k, v, resid, probs, wd, pk)
    back_loads = [
        pltpu.make_async_copy(src, dst, lb.at[n]) for n, (src, dst) in enumerate(zip(back_in, back_held))
    ]
    at = Place(planes, experts)
    z, i, core = at.z, at.i, at.core
    chips = at.chips
    per_plane = experts // 2
    rows, width = tokens.shape
    pairs = width // 128
    spot = lax.rem(i, 8)
    base = i - spot
    upper = rup.shape[0] if experts > 8 else 0
    ga_rows = 8 * rows // ga_groups
    datt, dq, dk, dv = [dpre.at[pl.ds(0, rows), pl.ds(n * width, width)] for n in range(4)]
    chunk = per_plane * padded // pieces
    batch = per_plane // pieces
    ff = hwi.shape[1]
    wide = ff // blocks
    load_i = pltpu.make_async_copy(win, hwi, ls.at[0])
    load_o = pltpu.make_async_copy(wout, hwo, ls.at[1])
    load_i.start()
    load_o.start()
    met = greet(at)
    diagonal = lax.broadcasted_iota(jnp.int32, (padded, 128), 1) == lax.broadcasted_iota(jnp.int32, (padded, 128), 0)
    load_i.wait()

    def copies(plane, n):
        target = plane * per_plane + n
        there = 2 * n + core
        rows_in = dxland.at[pl.ds(pl.multiple_of(at.me * padded, 8), padded), :]
        return [
            send_to(dxsend.at[target], rows_in, ts.at[0, target], tr.at[0, at.me], plane, there),
            send_to(dgsend.at[target], dgland.at[at.me], ts.at[1, target], tr.at[1, at.me], plane, there),
        ]

    def own_copies():
        rows_in = dxland.at[pl.ds(pl.multiple_of(at.me * padded, 8), padded), :]
        return [
            pltpu.make_async_copy(dxsend.at[at.me], rows_in, tl.at[0]),
            pltpu.make_async_copy(dgsend.at[at.me], dgland.at[at.me], tl.at[1]),
        ]

    def work(plane, piece, opening=None):
        first = plane * per_plane + piece * batch
        span = pl.ds(pl.multiple_of((plane * pieces + piece) * chunk, 16), chunk)
        x_c = x[span, :]
        do_c = do[span, :].astype(F32)
        column = jnp.concatenate(
            [
                jnp.sum(jnp.where(diagonal, gate[first + n], 0.0), axis=1, keepdims=True)
                for n in range(batch)
            ],
            axis=0,
        )
        dy_c = (do_c * column).astype(BF)
        dy[span, :] = dy_c
        y_sum = jnp.zeros((chunk, width), F32)
        dx_sum = jnp.zeros((chunk, width), F32)
        for b in range(blocks):
            cols = slice(b * wide, (b + 1) * wide)
            u = dot(x_c, hwi[:, cols], NN)
            if b == 0 and opening is not None:
                @pl.when(opening)
                def _():
                    load_o.wait()
                    for copy in back_loads:
                        copy.start()
            dz = dot(dy_c, hwo[cols, :], NT)
            square = u * u
            bent = jnp.tanh(GELU_SCALE * (u + GELU_CUBE * (square * u)))
            cdf = 0.5 * (1.0 + bent)
            slope = cdf + (0.5 * GELU_SCALE) * u * (1.0 - bent * bent) * (1.0 + 3.0 * GELU_CUBE * square)
            hidden = (u * cdf).astype(BF)
            d_pre = (dz * slope).astype(BF)
            hid[span, cols] = hidden
            dpre[span, cols] = d_pre
            y_sum += dot(hidden, hwo[cols, :], NN)
            dx_sum += dot(d_pre, hwi[:, cols], NT)
        y_low = y_sum.astype(BF)
        d_gate = jnp.sum(y_low.astype(F32) * do_c, axis=1, keepdims=True)
        for n in range(batch):
            part = slice(n * padded, (n + 1) * padded)
            source = first + n
            ysend[source] = y_sum[part].astype(BF)
            dxsend[source] = dx_sum[part].astype(BF)
            dgsend[source] = jnp.sum(jnp.where(diagonal, d_gate[part], 0.0), axis=0, keepdims=True)

    def far_plane(turn):
        half = 1 - 2 * lax.rem(z, 2)
        other = lax.rem(z + 2, planes)
        return jnp.where(turn == 0, other, jnp.where(turn == 1, planes - 1 - z, z + half))

    def remote_turn(turn, carry):
        plane = far_plane(lax.div(turn, pieces))
        piece = lax.rem(turn, pieces)
        work(plane, piece, turn == 0)
        pl.when(turn == 0)(met)
        for n in range(batch):
            for copy in copies(plane, piece * batch + n):
                copy.start()
        return carry

    lax.fori_loop(0, (planes - 1) * pieces, remote_turn, 0)
    for piece in range(pieces):
        work(z, piece)
    for copy in own_copies():
        copy.start()
    for n in range(per_plane):
        for copy in copies(z, n):
            pl.when(at.chip != n)(copy.start)

    def landing(source):
        return yland.at[pl.ds(pl.multiple_of(source * padded, 8), padded), :]

    def y_copy(step):
        target = lax.rem(at.me + step, chips)
        zt, it = lax.div(target, per_plane), 2 * lax.rem(target, per_plane) + core
        return send_to(ysend.at[target], landing(at.me), ys.at[step], yr.at[step], zt, it)

    def y_start(step, carry):
        y_copy(step).start()
        return carry

    y_own = pltpu.make_async_copy(ysend.at[at.me], landing(at.me), yl.at[0])
    y_own.start()
    lax.fori_loop(1, chips, y_start, 0)

    ce = z - 1
    host = jnp.logical_and(z >= 1, z <= 2)
    half_i, half_o = width // planes // 2, ff // planes // 2

    def part(source, size, p, c):
        return source.at[pl.ds(pl.multiple_of((2 * p + c) * size, 16), size), :]

    pair = [
        [
            send_to(part(src, size, p, 1 - core), land.at[p], es.at[which, p], er.at[which, p], z, at.sib)
            for p in range(planes)
        ]
        for which, (src, land, size) in enumerate(((hwi, ri, half_i), (hwo, ro, half_o)))
    ]
    fetch_ga = [
        pltpu.make_async_copy(
            ga.at[pl.ds(g * ga_rows, ga_rows), :],
            hid.at[pl.ds(0, ga_rows), pl.ds(g * width, width)],
            gl.at[g],
        )
        for g in range(ga_groups)
    ]

    @pl.when(host)
    def _():
        turned = x[...].T
        for b in range(blocks):
            cols = slice(b * wide, (b + 1) * wide)
            hwi[:, cols] = dot(turned, dpre[:, cols], NN, BF)
        for copy in pair[0]:
            copy.start()
        for b in range(blocks):
            cols = slice(b * wide, (b + 1) * wide)
            hwo[cols, :] = dot(hid[:, cols], dy[...], TN, BF)
        for copy in pair[1]:
            copy.start()

    for copy in fetch_ga:
        copy.start()

    owner = 2 * at.chip + ce
    shipments = []

    def ship(p, which):
        src, dst = (part(hwi, half_i, p, core), wi.at[core]) if which == 0 else (part(hwo, half_o, p, core), wo.at[core])
        near = jnp.logical_and(z == p, core == ce)
        far_copy = send_to(src, dst, hs.at[p, which], hr.at[core, which], p, owner)
        near_copy = pltpu.make_async_copy(src, dst, hr.at[core, which])
        is_far = jnp.logical_and(host, jnp.logical_not(near))
        pl.when(is_far)(far_copy.start)
        pl.when(jnp.logical_and(host, near))(near_copy.start)
        shipments.append((is_far, far_copy))

    def add_pair(which, mine, theirs, size, chunk):
        @pl.when(host)
        def _():
            for copy in pair[which]:
                copy.wait_recv()

            def add(n, carry):
                low = pl.ds(pl.multiple_of(n * chunk, chunk), chunk)
                for p in range(planes):
                    here = pl.ds(pl.multiple_of((2 * p + core) * size + n * chunk, 16), chunk)
                    mine[here, :] = (
                        mine[here, :].astype(F32) + theirs[p, low, :].astype(F32)
                    ).astype(BF)
                return carry

            lax.fori_loop(0, size // chunk, add, 0)

    add_pair(0, hwi, ri, half_i, 16)
    for p in range(planes):
        ship(p, 0)
    add_pair(1, hwo, ro, half_o, 64)
    for p in (0, 3):
        ship(p, 1)

    def dx_wait(step, carry):
        source = lax.rem(at.me + step, at.chips)
        rows_in = dxland.at[pl.ds(pl.multiple_of(source * padded, 8), padded), :]
        send_to(dxsend.at[source], rows_in, ts.at[0, source], tr.at[0, source], z, i).wait_recv()
        send_to(dgsend.at[source], dgland.at[source], ts.at[1, source], tr.at[1, source], z, i).wait_recv()
        return carry

    for copy in own_copies():
        copy.wait()
    lax.fori_loop(1, at.chips, dx_wait, 0)
    fetch_dx = pltpu.make_async_copy(dxland, landed_rows, yl.at[1])
    fetch_dx.start()
    fetch_dx.wait()

    for copy in back_loads:
        copy.wait()

    aux_v = aux[...]
    gates = [aux_v[:, 0:1], aux_v[:, 1:2]]
    place = slot_places([aux_v[:, 2:3], aux_v[:, 3:4]], chips * padded)
    d_out = cot[...].astype(F32)
    d_act = dot(place[0] + place[1], landed_rows[...], NN)
    table = dgland[:, 0, :]
    d_gate = slot_values(aux_v, table, padded, chips)
    mean_gate = gates[0] * d_gate[0] + gates[1] * d_gate[1]
    route_iota = lax.broadcasted_iota(jnp.int32, (rows, nrouter), 1).astype(F32)
    d_logits = jnp.zeros((rows, nrouter), F32)
    for n in range(2):
        chosen = route_iota == aux_v[:, 4 + n:5 + n]
        d_logits = d_logits + jnp.where(chosen, gates[n] * (d_gate[n] - mean_gate), 0.0)
    d_logits = d_logits.astype(BF)
    small[0:nrouter, :] = dot(d_logits, act_two[...], TN)
    d_act = d_act + dot(d_logits, pk[0:nrouter, :], NN)
    gain_one = pk[nrouter:nrouter + 1, :].astype(F32)
    gain_two = pk[nrouter + 2:nrouter + 3, :].astype(F32)
    d_norm, g_gain, g_bias = norm_back(resid[...], gain_two, d_act)
    small[nrouter:nrouter + 16, :] = jnp.zeros((16, width), F32)
    small[nrouter + 2:nrouter + 3, :] = g_gain
    small[nrouter + 3:nrouter + 4, :] = g_bias
    d_res = d_out + d_norm
    dres[...] = d_res
    d_branch = d_res.astype(BF)
    half = width // 2
    for n in range(2):
        dsend[pairs + n] = d_branch[:, n * half:(n + 1) * half]
    datt[...] = dot(d_branch, wd[3], NT, BF)

    def d_copy(target):
        return send_to(dsend.at[target], gd.at[spot], sd.at[target], rd.at[spot], z, base + target)

    def d_near(target):
        return pltpu.make_async_copy(dsend.at[target], gd.at[spot], rd.at[spot])

    def d_start(target):
        far = spot != target
        pl.when(far)(d_copy(target).start)
        pl.when(jnp.logical_not(far))(d_near(target).start)

    for n in range(2):
        d_start(pairs + n)

    lane = lax.broadcasted_iota(jnp.int32, (rows, 128), 1)
    masks = [(lane < HEAD).astype(F32).astype(BF), (lane >= HEAD).astype(F32).astype(BF)]
    score_scale = HEAD ** (-0.5)

    def head_pair(n, carry):
        cols = pl.ds(pl.multiple_of(n * 128, 128), 128)
        q2, k2, v2, da2 = q[:, cols], k[:, cols], v[:, cols], datt[:, cols]
        sums = [jnp.zeros((rows, 128), F32) for _ in range(3)]
        for side in range(2):
            mask = masks[side]
            da = da2 * mask
            p = probs[2 * n + side]
            dpb = dot(da, v2, NT)
            delta = jnp.sum(p * dpb, axis=-1, keepdims=True)
            ds = (p * (dpb - delta)).astype(BF)
            sums[0] += dot(ds, k2 * mask, NN)
            sums[1] += dot(ds, q2 * mask, TN)
            sums[2] += dot(p.astype(BF), da, TN)
        low = [(sums[0] * score_scale).astype(BF), (sums[1] * score_scale).astype(BF), sums[2].astype(BF)]
        for m, (value, full) in enumerate(zip(low, (dq, dk, dv))):
            dsend[n, :, m * 128:(m + 1) * 128] = value
            full[:, cols] = value
        d_start(n)
        return carry

    lax.fori_loop(0, pairs, head_pair, 0)

    d_one = dot(dq[...], wd[0], NT) + dot(dk[...], wd[1], NT) + dot(dv[...], wd[2], NT)
    d_norm, g_gain, g_bias = norm_back(tokens[...].astype(F32), gain_one, d_one)
    grad_tokens[...] = (dres[...] + d_norm).astype(BF)
    small[nrouter:nrouter + 1, :] = g_gain
    small[nrouter + 1:nrouter + 2, :] = g_bias

    hops = [at.sib, at.xn, at.yn]
    for n in range(upper):
        bit = 8 << n
        hops.append(i + bit - 2 * bit * lax.rem(lax.div(i, bit), 2))
    moves = [(z, t) for t in hops]
    for n in range(planes.bit_length() - 1):
        bit = 1 << n
        moves.append((z + bit - 2 * bit * lax.rem(lax.div(z, bit), 2), i))
    small_copies = []

    def small_start(n):
        if n >= 2:
            small_copies[n - 2].wait_send()
        sms[n % 2] = small[...]
        copy = send_to(sms.at[n % 2], smr.at[n], ms.at[n], mr.at[n], moves[n][0], moves[n][1])
        copy.start()
        small_copies.append(copy)

    def small_step(n):
        small_copies[n].wait_recv()
        small[...] = small[...] + smr[n]
        if n + 1 < len(moves):
            small_start(n + 1)

    small_start(0)

    small_step(0)

    def d_wait(source, carry):
        send_to(gd.at[source], gd.at[source], sd.at[source], rd.at[source], z, i).wait_recv()
        return carry

    lax.fori_loop(0, 8, d_wait, 0)
    columns = gd.shape[2]
    total = jnp.zeros((width, columns), F32)
    sources = ga_rows // rows
    for g in range(ga_groups):
        fetch_ga[g].wait()
        total += dot(
            hid[0:ga_rows, g * width:(g + 1) * width],
            gd[g * sources:(g + 1) * sources].reshape(ga_rows, columns), TN,
        )
    gsum[...] = total.reshape(planes, width // planes, columns)
    small_step(1)
    tail = []
    for n in range(upper):
        szb[...] = gsum[...].astype(BF)
        copy = send_to(szb, rup.at[n], us.at[n], ur.at[n], z, hops[3 + n])
        copy.start()
        copy.wait_recv()
        gsum[...] = szb[...].astype(F32) + rup[n].astype(F32)
        copy.wait_send()
    szb[...] = gsum[...].astype(BF)
    partner = z + 1 - 2 * lax.rem(z, 2)
    others = 2 - 2 * lax.div(z, 2)
    outer = jnp.logical_not(host)
    copy = send_to(szb.at[partner], rzb.at[0], zs.at[0], zr.at[0], partner, i)
    copy.start()
    tail.append(copy)
    inward = [
        send_to(szb.at[others + n], rzb.at[2 + n], zs.at[1 + n], zr.at[2 + n], partner, i) for n in range(2)
    ]
    across = [
        send_to(szb.at[others + n], rzb.at[1], zs.at[1 + n], zr.at[1], others + n, i) for n in range(2)
    ]

    @pl.when(outer)
    def _():
        for copy in inward:
            copy.start()

    @pl.when(host)
    def _():
        for n in range(2):
            inward[n].wait_recv()
            szb[others + n] = (gsum[others + n] + rzb[2 + n].astype(F32)).astype(BF)
            across[n].start()

    shipments += [(outer, copy) for copy in inward] + [(host, copy) for copy in across]
    for p in (1, 2):
        ship(p, 1)
    small_step(2)

    def y_finish(step, carry):
        source = lax.rem(at.me + chips - step, chips)
        send_to(landing(source), landing(source), ys.at[step], yr.at[step], z, i).wait_recv()
        y_copy(step).wait_send()
        return carry

    y_own.wait()
    lax.fori_loop(1, chips, y_finish, 0)
    fetch = pltpu.make_async_copy(yland, landed_rows, yl.at[1])
    fetch.start()
    fetch.wait()
    y_all = landed_rows[...]
    mixed = gates[0] * dot(place[0], y_all, NN) + gates[1] * dot(place[1], y_all, NN)
    block_out[...] = (resid[...] + mixed).astype(BF)

    fin = gsum[z]
    for n in range(2):
        send_to(rzb.at[n], rzb.at[n], zs.at[n], zr.at[n], z, i).wait_recv()
        fin = fin + rzb[n].astype(F32)
    fb[spot] = fin.astype(BF)
    px, py = spot + 2 - 4 * at.xb, spot + 4 - 8 * at.yb
    pd = px + 4 - 8 * at.yb
    flip = 1 - 2 * core

    def pass_on(where, step, target):
        copy = send_to(fb.at[where], fb.at[where], gs.at[step], gr.at[step], z, target)
        copy.start()
        tail.append(copy)

    def landed(where, step):
        send_to(fb.at[where], fb.at[where], gs.at[step], gr.at[step], z, i).wait_recv()

    pass_on(spot, 0, at.xn)
    pass_on(spot, 1, at.yn)
    pass_on(spot, 2, at.sib)
    small_step(3)
    landed(px, 0)
    landed(py, 1)
    pass_on(px + core * (py - px), 3, at.yn + core * (at.xn - at.yn))
    pass_on(px, 4, at.sib)
    pass_on(py, 5, at.sib)
    for n in range(4, len(moves)):
        small_step(n)
    osmall[...] = small[...]
    landed(pd, 3)
    pass_on(pd, 6, at.sib)
    for h in range(2):
        send_to(wi.at[h], wi.at[h], hs.at[0, 0], hr.at[h, 0], z, i).wait_recv()
        send_to(wo.at[h], wo.at[h], hs.at[0, 1], hr.at[h, 1], z, i).wait_recv()
    landed(spot + flip, 2)
    landed(px + flip, 4)
    landed(py + flip, 5)
    landed(pd + flip, 6)
    for copy in tail + small_copies[-2:]:
        copy.wait_send()
    def d_sent(target, carry):
        pl.when(spot != target)(d_copy(target).wait_send)
        return carry

    lax.fori_loop(0, 8, d_sent, 0)

    @pl.when(host)
    def _():
        for copy in pair[0] + pair[1]:
            copy.wait_send()

    for is_far, copy in shipments:
        pl.when(is_far)(copy.wait_send)

    def dx_sent(step, carry):
        target = lax.rem(at.me + step, at.chips)
        for copy in copies(lax.div(target, per_plane), lax.rem(target, per_plane)):
            copy.wait_send()
        return carry

    lax.fori_loop(1, at.chips, dx_sent, 0)


def rear(planes, experts, nrouter, x, do, gate, back_in, win, wout, ga):
    rows, width = back_in[0].shape
    chips, padded, _ = x.shape
    slots = chips * padded
    ff = win.shape[1]
    pieces, blocks = (1, 4) if experts <= 8 else (2, 8)
    ga_groups = ff // width
    share, fshare, half = width // planes, ff // planes, width // 2
    upper = max(experts.bit_length() - 4, 1)
    nbits = experts.bit_length() - 1 + planes.bit_length() - 1
    dma = pltpu.SemaphoreType.DMA
    vm = pltpu.VMEM
    sds = jax.ShapeDtypeStruct
    return pl.pallas_call(
        functools.partial(rear_kernel, planes, experts, padded, pieces, blocks, ga_groups, nrouter),
        out_shape=(
            sds((rows, width), BF),
            sds((rows, width), BF),
            sds((8, share, half), BF),
            sds((nrouter + 16, width), F32),
            sds((2, share // 2, ff), BF),
            sds((2, fshare // 2, width), BF),
            sds((slots, width), BF),
            sds((slots, width), BF),
        ),
        in_specs=[vmem_spec()] * 3 + [any_spec()] * 14,
        out_specs=(vmem_spec(),) * 4 + (any_spec(),) * 4,
        scratch_shapes=[vm(a.shape, a.dtype) for a in back_in] + [
            vm((width, ff), BF),
            vm((ff, width), BF),
            vm((slots, width), BF),
            vm((slots, ff), BF),
            vm((slots, ff), BF),
            vm((chips, padded, width), BF),
            vm((chips, 1, 128), F32),
            vm((chips, 1, 128), F32),
            vm((chips, padded, width), BF),
            vm((slots, width), BF),
            vm((8, rows, half), BF),
            vm((8, rows, half), BF),
            vm((rows, width), F32),
            vm((planes, share, half), F32),
            vm((planes, share, half), BF),
            vm((4, share, half), BF),
            vm((upper, planes, share, half) if experts > 8 else (1, 8, 128), BF),
            vm((2, nrouter + 16, width), F32),
            vm((nbits, nrouter + 16, width), F32),
            vm((nrouter + 16, width), F32),
            vm((planes, share // 2, ff), BF),
            vm((planes, fshare // 2, width), BF),
            dma((2,)), dma((2, chips)), dma((2, chips)), dma((2,)), dma((ga_groups,)),
            dma((2, planes)), dma((2, planes)),
            dma((planes, 2)), dma((2, 2)),
            dma((chips,)), dma((chips,)), dma((2,)),
            dma((8,)), dma((8,)),
            dma((upper,)), dma((upper,)),
            dma((3,)), dma((4,)),
            dma((7,)), dma((7,)), dma((nbits,)), dma((nbits,)), dma((11,)),
        ],
        compiler_params=pltpu.CompilerParams(
            collective_id=2, has_side_effects=True, vmem_limit_bytes=REAR_LIMIT
        ),
        name="rear",
    )(x.reshape(slots, width), do.reshape(slots, width), gate, *back_in, win, wout, ga.reshape(8 * rows, width))


def finish_kernel(planes, nrouter, block_out, grad_tokens, fb, small, wi, wo,
                  ob, ot, o0, o1, o2, o3, og, v0, v1, v2, v3, ogi, ogo,
                  s0, s1, s2, s3, sg, sv, si, so, sem):
    z = lax.axis_index("dp")
    share = s0.shape[0]
    pairs = s0.shape[1] // 128
    half = s0.shape[1] // 2
    copies = []

    def write(source, target):
        copy = pltpu.make_async_copy(source, target, sem.at[len(copies)])
        copy.start()
        copies.append(copy)

    write(block_out, ob)
    write(grad_tokens, ot)
    for wide, low, out in ((si, wi, ogi), (so, wo, ogo)):
        chunk = low.shape[1]
        for h in range(2):
            wide[h * chunk:(h + 1) * chunk, :] = low[h].astype(F32)
            write(wide.at[pl.ds(h * chunk, chunk), :], out.at[pl.ds(h * chunk, chunk), :])
    for m, (stage, out) in enumerate(((s0, o0), (s1, o1), (s2, o2))):
        for n in range(pairs):
            stage[:, n * 128:(n + 1) * 128] = fb[n, :, m * 128:(m + 1) * 128].astype(F32)
        write(stage, out)
    for n in range(2):
        s3[:, n * half:(n + 1) * half] = fb[pairs + n].astype(F32)
    write(s3, o3)
    mine = small[:, 0:share]
    for p in range(1, planes):
        mine = jnp.where(z == p, small[:, p * share:(p + 1) * share], mine)
    sg[...] = mine[0:nrouter]
    write(sg, og)
    for n, out in enumerate((v0, v1, v2, v3)):
        sv[n] = mine[nrouter + n:nrouter + n + 1]
        write(sv.at[n], out)
    for copy in copies:
        copy.wait()


def finish(planes, nrouter, block_out, grad_tokens, fb, small, wi, wo):
    rows, width = block_out.shape
    _, share, half = fb.shape
    ff = wi.shape[2]
    fshare = 2 * wo.shape[1]
    vm = pltpu.VMEM
    sds = jax.ShapeDtypeStruct
    dense = ((share, width),) * 4 + ((nrouter, share),)
    wide = ((share, ff), (fshare, width))
    results = dense + ((1, share),) * 4 + wide
    stages = dense + ((4, 1, share),) + wide
    return pl.pallas_call(
        functools.partial(finish_kernel, planes, nrouter),
        out_shape=(sds((rows, width), BF),) * 2 + tuple(sds(shape, F32) for shape in results),
        in_specs=[vmem_spec()] * 6,
        out_specs=(any_spec(),) * 13,
        scratch_shapes=[vm(shape, F32) for shape in stages] + [pltpu.SemaphoreType.DMA((16,))],
        compiler_params=pltpu.CompilerParams(vmem_limit_bytes=VMEM_LIMIT),
        name="finish",
    )(block_out, grad_tokens, fb, small, wi, wo)


def shards(planes, experts, tokens, segment_ids, routes, ln1_gain, ln1_bias, ln2_gain, ln2_bias,
           w_query, w_key, w_value, w_output, w_router, frozen_in, frozen_out, new_in, new_out,
           cotangent):
    rows, width = tokens.shape
    expert_count = w_router.shape[1]
    capacity = 5 * rows // (2 * expert_count)
    padded = -(-capacity // 8) * 8
    (wd, pk, win, wout, act_two, q, k, v, resid, probs, aux, ga, x_recv, do_recv, g_recv) = front(
        planes, experts, capacity, padded, expert_count, tokens, cotangent, segment_ids, routes,
        w_router, (ln1_gain, ln1_bias, ln2_gain, ln2_bias),
        w_query, w_key, w_value, w_output, frozen_in, frozen_out, new_in, new_out,
    )
    block_out, grad_tokens, dense, small, low_in, low_out, _, _ = rear(
        planes, experts, expert_count, x_recv, do_recv, g_recv,
        (tokens, cotangent, aux, act_two, q, k, v, resid, probs, wd, pk), win, wout, ga,
    )
    block_out, grad_tokens, oq, ok, ov, ow, router, *norms, ogi, ogo = finish(
        planes, expert_count, block_out, grad_tokens, dense, small, low_in, low_out
    )
    norms = [norm.reshape(width // planes) for norm in norms]
    return (
        block_out, grad_tokens, oq, ok, ov, ow, router.T,
        norms[0], norms[1], norms[2], norms[3], ogi[None], ogo[None],
    )


def solution(mesh):
    rows = P(("dp", "expert"), None)
    in_specs = (rows, rows, rows) + (P("dp"),) * 4 + (P("dp", None),) * 5
    in_specs += (P("expert", "dp", None),) * 4 + (rows,)
    out_specs = (rows, rows) + (P("dp", None),) * 5 + (P("dp"),) * 4
    out_specs += (P("expert", "dp", None),) * 2
    body = functools.partial(shards, mesh.shape["dp"], mesh.shape["expert"])
    return jax.shard_map(body, mesh=mesh, in_specs=in_specs, out_specs=out_specs, check_vma=False)
```

```python
import functools

import jax
import jax.numpy as jnp
from jax import lax
from jax.experimental import pallas as pl
from jax.experimental.pallas import tpu as pltpu
from jax.sharding import PartitionSpec as P

HEADS = 12
HEAD = 64
NORM_EPS = 1e-05
MASKED = -1e30
MESH = pl.DeviceIdType.MESH
BF = jnp.bfloat16
F32 = jnp.float32
VMEM_LIMIT = 60 * 1024 * 1024
REAR_LIMIT = 67043328


class Place:
    def __init__(self, planes, experts):
        self.planes, self.experts = planes, experts
        self.z = lax.axis_index("dp")
        self.i = lax.axis_index("expert")
        self.core = lax.rem(self.i, 2)
        self.chip = lax.div(self.i, 2)
        self.xb = lax.rem(self.chip, 2)
        self.yb = lax.rem(lax.div(self.i, 4), 2)
        self.sib = self.i + 1 - 2 * self.core
        self.xn = self.i + 2 - 4 * self.xb
        self.yn = self.i + 4 - 8 * self.yb
        self.chips = planes * (experts // 2)
        self.me = self.z * (experts // 2) + self.chip


def send_to(src, dst, send_sem, recv_sem, z, i):
    return pltpu.make_async_remote_copy(
        src_ref=src,
        dst_ref=dst,
        send_sem=send_sem,
        recv_sem=recv_sem,
        device_id={"dp": z, "expert": i},
        device_id_type=MESH,
    )


def greet(at):
    barrier = pltpu.get_barrier_semaphore()
    count = at.planes * at.experts
    own = at.z * at.experts + at.i

    def signal(step, carry):
        target = lax.rem(own + step, count)
        pl.semaphore_signal(
            barrier,
            inc=1,
            device_id={"dp": lax.div(target, at.experts), "expert": lax.rem(target, at.experts)},
            device_id_type=MESH,
        )
        return carry

    lax.fori_loop(1, count, signal, 0)
    return lambda: pl.semaphore_wait(barrier, count - 1)


def any_spec():
    return pl.BlockSpec(memory_space=pl.ANY)


def vmem_spec():
    return pl.BlockSpec(memory_space=pltpu.VMEM)


NN = ((1,), (0,))
NT = ((1,), (1,))
TN = ((0,), (0,))


def dot(left, right, contract, out=F32):
    return lax.dot_general(
        left, right, ((contract[0], contract[1]), ((), ())), preferred_element_type=F32
    ).astype(out)


def exact_dot(left, right, contract):
    return lax.dot_general(
        left, right, ((contract[0], contract[1]), ((), ())),
        preferred_element_type=F32, precision=lax.Precision.HIGHEST,
    )


def norm_parts(rows):
    centred = rows - jnp.mean(rows, axis=-1, keepdims=True)
    variance = jnp.mean(centred * centred, axis=-1, keepdims=True)
    scale = lax.rsqrt(variance + NORM_EPS)
    return centred * scale, scale


def norm_back(rows, gain, grad):
    unit, scale = norm_parts(rows)
    scaled = grad * gain
    inner = scaled - jnp.mean(scaled, axis=-1, keepdims=True)
    inner = inner - unit * jnp.mean(scaled * unit, axis=-1, keepdims=True)
    return scale * inner, jnp.sum(grad * unit, axis=0, keepdims=True), jnp.sum(grad, axis=0, keepdims=True)


def slot_places(slot, slots):
    lanes = lax.broadcasted_iota(jnp.int32, (slot[0].shape[0], slots), 1).astype(F32)
    return [(lanes == one).astype(F32).astype(BF) for one in slot]


def slot_values(aux, table, padded, chips):
    rows = aux.shape[0]
    low = lax.broadcasted_iota(jnp.int32, (rows, chips), 1).astype(F32) * padded
    lanes = lax.broadcasted_iota(jnp.int32, (rows, table.shape[1]), 1).astype(F32)
    found = []
    for k in range(2):
        slot = aux[:, 2 + k:3 + k]
        mine = jnp.logical_and(slot >= low, slot < low + padded).astype(F32)
        position = slot - jnp.sum(mine * low, axis=1, keepdims=True)
        picked = exact_dot(mine, table, NN)
        found.append(jnp.sum(jnp.where(lanes == position, picked, 0.0), axis=1, keepdims=True))
    return found


def front_kernel(planes, experts, capacity, padded, nrouter,
                 tokens, cot, segs, routes, router, g1, b1, g2, b2, wq, wk, wv, wo, fi, fo, ni, no,
                 owd, pk, win, wout, oact, oq, ok, ov, oresid, oprobs, aux, ga,
                 xland, dland, gland,
                 wd, act_one, act_two, q, k, v, att, resid, probs, packs, allow, xsend, esend, gsend, dstage, istage, ostage, ibf, obf,
                 ld, zs, zr, ps, pr, gs, gr, es, er, fs, fr, ts, tr, tl, sa, ra, sv, zf):
    at = Place(planes, experts)
    z, i, core = at.z, at.i, at.core
    rows, width = tokens.shape
    chips = at.chips
    per_plane = experts // 2
    share = dstage.shape[1]
    quarter = share // 4
    half = width // 2
    fhalf = istage.shape[2] // 2
    oshare = ostage.shape[1]
    ohalf = oshare // 2
    pairs = width // 128
    spot = lax.rem(i, 8)
    base = i - spot
    loads = [pltpu.make_async_copy(w, dstage.at[m], ld.at[m]) for m, w in enumerate((wq, wk, wv, wo))]
    loads += [
        pltpu.make_async_copy(fi.at[0], istage.at[0], ld.at[4]),
        pltpu.make_async_copy(ni.at[0], istage.at[1], ld.at[5]),
        pltpu.make_async_copy(fo.at[0], ostage.at[0], ld.at[6]),
        pltpu.make_async_copy(no.at[0], ostage.at[1], ld.at[7]),
    ]
    for load in loads:
        load.start()
    met = greet(at)
    zrow = pl.multiple_of(z * share, share)
    for m in range(4):
        loads[m].wait()
        wd[m, pl.ds(zrow, share), :] = dstage[m].astype(BF)
    packs[z, 0:nrouter, :] = router[...].astype(BF)
    norm_row = lax.broadcasted_iota(jnp.int32, (16, share), 0)
    norms = jnp.zeros((16, share), F32)
    for n, values in enumerate((g1, b1, g2, b2)):
        norms = jnp.where(norm_row == n, values[...], norms)
    packs[z, nrouter:nrouter + 16, :] = norms.astype(BF)
    met()

    def block(plane, row_quarter, column_half):
        return wd.at[
            :,
            pl.ds(pl.multiple_of(plane * share + row_quarter * quarter, 16), quarter),
            pl.ds(pl.multiple_of(column_half * half, 128), half),
        ]

    rq = 2 * at.yb + core
    rqy = 2 * (1 - at.yb) + core
    rqs = 2 * at.yb + 1 - core
    rqys = 2 * (1 - at.yb) + 1 - core
    xb, xo = at.xb, 1 - at.xb
    started, remote_sends = [], []
    for j in range(1, planes):
        zt = lax.rem(z + j, planes)
        mine = block(z, rq, xb)
        copy = send_to(mine, mine, zs.at[j - 1], zr.at[j - 1], zt, i)
        direct = jnp.logical_or(lax.div(zt, 2) == lax.div(z, 2), jnp.logical_and(zt >= 1, zt <= 2))
        pl.when(direct)(copy.start)
        remote_sends.append((direct, copy))
        copy = send_to(packs.at[z], packs.at[z], ps.at[j - 1], pr.at[j - 1], zt, i)
        copy.start()
        started.append(copy)

    def cast(source, target, kind, chunk):
        def step(n, carry):
            part = pl.ds(pl.multiple_of(n * chunk, chunk), chunk)
            target[kind, part, :] = source[kind, part, :].astype(BF)
            return carry

        lax.fori_loop(0, source.shape[1] // chunk, step, 0)

    def in_block(plane, h):
        return win.at[
            pl.ds(pl.multiple_of(plane * share, 16), share),
            pl.ds(pl.multiple_of(h * fhalf, 128), fhalf),
        ]

    def out_block(plane, h):
        return wout.at[pl.ds(pl.multiple_of(plane * oshare + h * ohalf, 16), ohalf), :]


    def ship(kind, h, which):
        zh = 3 * core if kind == 0 else 1 + core
        remote = jnp.logical_or(zh != z, core != h)
        src = (
            ibf.at[kind, :, pl.ds(h * fhalf, fhalf)]
            if which == 0
            else obf.at[kind, pl.ds(h * ohalf, ohalf), :]
        )
        dst = in_block(z, h) if which == 0 else out_block(z, h)
        far = send_to(src, dst, es.at[kind, h, which], er.at[z, which], zh, 2 * at.chip + h)
        near = pltpu.make_async_copy(src, dst, er.at[z, which])
        pl.when(remote)(far.start)
        pl.when(jnp.logical_not(remote))(near.start)
        remote_sends.append((remote, far))

    def ship_in(kind):
        loads[4 + kind].wait()
        cast(istage, ibf, kind, 16)
        for h in range(2):
            ship(kind, h, 0)

    ship_in(1)
    end = 3 * (z - 1)
    handed = []
    for j in range(1, planes):
        zz = lax.rem(z + planes - j, planes)
        hand = jnp.logical_and(lax.div(zz, 2) != lax.div(z, 2), jnp.logical_and(z >= 1, z <= 2))
        mine = block(zz, rq, xb)
        there = lax.rem(end + planes - zz, planes)
        copy = send_to(mine, mine, zf.at[j - 1], zr.at[jnp.maximum(there, 1) - 1], jnp.clip(end, 0, planes - 1), i)

        @pl.when(hand)
        def _():
            send_to(mine, mine, zs.at[j - 1], zr.at[j - 1], z, i).wait_recv()
            copy.start()

        handed.append(hand)
        remote_sends.append((hand, copy))
    ship_in(0)

    shift = experts.bit_length() - 1
    above = lax.broadcasted_iota(jnp.int32, (rows, rows), 0)
    across = lax.broadcasted_iota(jnp.int32, (rows, rows), 1)
    segment = segs[...].astype(F32)
    fact_row = lax.broadcasted_iota(jnp.int32, (8, rows), 0)
    facts = jnp.zeros((8, rows), F32)
    for n, values in enumerate((routes[0:1, :].astype(F32), routes[1:2, :].astype(F32), segment)):
        facts = jnp.where(fact_row == n, values, facts)
    fact_columns = dot((above == across).astype(F32).astype(BF), facts.astype(BF), NT)
    route_columns = [fact_columns[:, n:n + 1] for n in range(2)]
    route = fact_columns.astype(jnp.int32)
    expert = jnp.bitwise_and(route, experts - 1)
    kind = jnp.right_shift(route, shift)
    host_plane = jnp.where(jnp.bitwise_and(expert, 1) == 0, kind, 3 - kind)
    host = host_plane * per_plane + jnp.right_shift(expert, 1)
    chip_iota = lax.broadcasted_iota(jnp.int32, (rows, chips), 1)
    chosen = [(chip_iota == host[:, n:n + 1]).astype(F32) for n in range(2)]
    earlier = (across < above).astype(F32).astype(BF)
    before = dot(earlier, (chosen[0] + chosen[1]).astype(BF), NN)
    position = [jnp.sum(one * before, axis=1, keepdims=True) for one in chosen]
    slot = [
        jnp.where(position[n] < capacity, host[:, n:n + 1].astype(F32) * padded + position[n], -1.0)
        for n in range(2)
    ]
    place = slot_places(slot, chips * padded)
    both = place[0] + place[1]

    def fill(target, values):
        sent = dot(both, values, TN)
        for n in range(chips):
            target[n] = sent[n * padded:(n + 1) * padded].astype(BF)

    def token_copy(src, dst, which, step):
        target = lax.rem(at.me + step, chips)
        zt, it = lax.div(target, per_plane), 2 * lax.rem(target, per_plane) + core
        return send_to(src.at[target], dst.at[at.me], ts.at[which, step], tr.at[which, step], zt, it)

    def token_start(src, dst, which):
        pltpu.make_async_copy(src.at[at.me], dst.at[at.me], tl.at[which]).start()

        def step(n, carry):
            token_copy(src, dst, which, n).start()
            return carry

        lax.fori_loop(1, chips, step, 0)

    def token_finish(src, dst, which):
        def step(n, carry):
            source = lax.rem(at.me + chips - n, chips)
            send_to(
                src.at[source], dst.at[source], ts.at[which, n], tr.at[which, n], z, i
            ).wait_recv()
            token_copy(src, dst, which, n).wait_send()
            return carry

        lax.fori_loop(1, chips, step, 0)
        pltpu.make_async_copy(src.at[at.me], dst.at[at.me], tl.at[which]).wait()

    fill(esend, cot[...])
    token_start(esend, dland, 0)
    for n, kind in ((6, 0), (7, 1)):
        loads[n].wait()
        cast(ostage, obf, kind, 32)
        for h in range(2):
            ship(kind, h, 1)
    same = jnp.logical_and(fact_columns[:, 2:3] == segment, across <= above)
    allow[...] = same.astype(F32)

    def pass_on(src, j, step, target):
        copy = send_to(src, src, gs.at[j - 1, step], gr.at[j - 1, step], z, target)
        copy.start()
        started.append(copy)

    def landed(dst, j, step):
        send_to(dst, dst, gs.at[j - 1, step], gr.at[j - 1, step], z, i).wait_recv()

    for j in range(1, planes):
        zz = lax.rem(z + planes - j, planes)
        mine = block(zz, rq, xb)
        arrival = send_to(mine, mine, zs.at[j - 1], zr.at[j - 1], z, i)
        pl.when(jnp.logical_not(handed[j - 1]))(arrival.wait_recv)
        pass_on(mine, j, 0, at.xn)
        pass_on(mine, j, 1, at.yn)
        pass_on(mine, j, 2, at.sib)
        send_to(packs.at[zz], packs.at[zz], ps.at[j - 1], pr.at[j - 1], z, i).wait_recv()
    pk[...] = jnp.concatenate([packs[p] for p in range(planes)], axis=1)

    x = tokens[...].astype(F32)
    gain = pk[nrouter:nrouter + 1, :].astype(F32)
    bias = pk[nrouter + 1:nrouter + 2, :].astype(F32)
    act_one[...] = (norm_parts(x)[0] * gain + bias).astype(BF)

    for j in range(1, planes):
        zz = lax.rem(z + planes - j, planes)
        bx, by = block(zz, rq, xo), block(zz, rqy, xb)
        landed(bx, j, 0)
        landed(by, j, 1)
        onward = block(zz, rq + core * (rqy - rq), xo + core * (xb - xo))
        pass_on(onward, j, 3, at.yn + core * (at.xn - at.yn))
        pass_on(bx, j, 4, at.sib)
        pass_on(by, j, 5, at.sib)
    for j in range(1, planes):
        zz = lax.rem(z + planes - j, planes)
        bd = block(zz, rqy, xo)
        landed(bd, j, 3)
        pass_on(bd, j, 6, at.sib)
    for j in range(1, planes):
        zz = lax.rem(z + planes - j, planes)
        landed(block(zz, rqs, xb), j, 2)
        landed(block(zz, rqs, xo), j, 4)
        landed(block(zz, rqys, xb), j, 5)
        landed(block(zz, rqys, xo), j, 6)

    def act_copy(step, whole):
        target = lax.rem(spot + step, 8)
        src = act_one if whole else att
        return target, send_to(src, ga.at[spot], sa.at[step], ra.at[step], z, base + target)

    def act_near(whole):
        return pltpu.make_async_copy(act_one if whole else att, ga.at[spot], tl.at[3])

    for step in range(1, 8):
        target, copy = act_copy(step, True)
        pl.when(target < pairs)(copy.start)
    pl.when(spot < pairs)(act_near(True).start)

    one = act_one[...]
    q[...] = dot(one, wd[0], NN, BF)
    k[...] = dot(one, wd[1], NN, BF)
    v[...] = dot(one, wd[2], NN, BF)
    lane = lax.broadcasted_iota(jnp.int32, (rows, 128), 1)
    masks = [(lane < HEAD).astype(F32).astype(BF), (lane >= HEAD).astype(F32).astype(BF)]
    score_scale = HEAD ** (-0.5)

    def head_pair(n, carry):
        cols = pl.ds(pl.multiple_of(n * 128, 128), 128)
        q2, k2, v2 = q[:, cols], k[:, cols], v[:, cols]
        total = jnp.zeros((rows, 128), F32)
        for side in range(2):
            scores = dot(q2 * masks[side], k2, NT) * score_scale
            scores = jnp.where(allow[...] > 0.5, scores, MASKED)
            expo = jnp.exp(scores - jnp.max(scores, axis=-1, keepdims=True))
            p = expo / jnp.sum(expo, axis=-1, keepdims=True)
            probs[2 * n + side] = p
            total += dot(p.astype(BF), v2 * masks[side], NN)
        att[:, cols] = total.astype(BF)
        return carry

    lax.fori_loop(0, pairs, head_pair, 0)
    residual = x + dot(att[...], wd[3], NN)
    resid[...] = residual
    gain = pk[nrouter + 2:nrouter + 3, :].astype(F32)
    bias = pk[nrouter + 3:nrouter + 4, :].astype(F32)
    two = (norm_parts(residual)[0] * gain + bias).astype(BF)
    act_two[...] = two
    fill(xsend, two)
    token_start(xsend, xland, 1)
    for step in range(1, 8):
        target, copy = act_copy(step, False)
        pl.when(target >= pairs)(copy.start)
    pl.when(spot >= pairs)(act_near(False).start)

    logits = dot(two, pk[0:nrouter, :], NT)
    route_iota = lax.broadcasted_iota(jnp.int32, (rows, nrouter), 1)
    picked = [
        jnp.sum(jnp.where(route_iota == route[:, n:n + 1], logits, 0.0), axis=1, keepdims=True)
        for n in range(2)
    ]
    top = jnp.maximum(picked[0], picked[1])
    lifted = [jnp.exp(one_pick - top) for one_pick in picked]
    gates = [one_lift / (lifted[0] + lifted[1]) for one_lift in lifted]
    values = jnp.zeros((rows, 128), F32)
    for n, column in enumerate(gates + slot + route_columns):
        values = jnp.where(lane == n, column, values)
    aux[...] = values
    lanes = lane.astype(F32)
    table = jnp.zeros((chips, 128), F32)
    for n in range(2):
        kept = jnp.logical_and(lanes == position[n], position[n] < capacity)
        table += exact_dot(chosen[n], jnp.where(kept, gates[n], 0.0), TN)
    for n in range(chips):
        gsend[n] = table[n:n + 1]
    token_start(gsend, gland, 2)
    kept_arrays = ((wd, owd), (act_two, oact), (q, oq), (k, ok), (v, ov), (resid, oresid), (probs, oprobs))
    saves = [pltpu.make_async_copy(src, dst, sv.at[n]) for n, (src, dst) in enumerate(kept_arrays)]
    for copy in saves:
        copy.start()

    def hand_on(plane, which):
        blk = in_block(plane, core) if which == 0 else out_block(plane, core)
        send_to(blk, blk, es.at[0, 0, which], er.at[plane, which], z, i).wait_recv()
        copy = send_to(blk, blk, fs.at[plane, which], fr.at[plane, which], z, at.sib)
        copy.start()
        started.append(copy)

    for which in range(2):
        for plane in range(planes):
            hand_on(plane, which)
    for src, dst, which in ((esend, dland, 0), (xsend, xland, 1), (gsend, gland, 2)):
        token_finish(src, dst, which)
    for step in range(1, 8):
        source = lax.rem(spot + 8 - step, 8)
        send_to(act_one, ga.at[source], sa.at[step], ra.at[step], z, i).wait_recv()
        act_copy(step, True)[1].wait_send()
    act_near(True).wait()
    for which in range(2):
        for plane in range(planes):
            blk = in_block(plane, 1 - core) if which == 0 else out_block(plane, 1 - core)
            send_to(blk, blk, fs.at[plane, which], fr.at[plane, which], z, i).wait_recv()
    for copy in started:
        copy.wait_send()
    for remote, far in remote_sends:
        pl.when(remote)(far.wait_send)
    for copy in saves:
        copy.wait()


def front(planes, experts, capacity, padded, nrouter, tokens, cot, segment_ids, routes, router, norms,
          wq, wk, wv, wo, fi, fo, ni, no):
    rows, width = tokens.shape
    share = wq.shape[0]
    ff = fi.shape[2]
    oshare = fo.shape[1]
    chips = planes * experts // 2
    dma = pltpu.SemaphoreType.DMA
    vm = pltpu.VMEM
    sds = jax.ShapeDtypeStruct
    flat = sds((rows, width), BF)
    slab = sds((chips, padded, width), BF)
    return pl.pallas_call(
        functools.partial(front_kernel, planes, experts, capacity, padded, nrouter),
        out_shape=(
            sds((4, width, width), BF),
            sds((nrouter + 16, width), BF),
            sds((width, ff), BF),
            sds((ff, width), BF),
            flat, flat, flat, flat,
            sds((rows, width), F32),
            sds((HEADS, rows, rows), F32),
            sds((rows, 128), F32),
            sds((8, rows, width), BF),
            slab,
            slab,
            sds((chips, 1, 128), F32),
        ),
        in_specs=[vmem_spec()] * 9 + [any_spec()] * 8,
        out_specs=(any_spec(), vmem_spec()) + (any_spec(),) * 8 + (vmem_spec(),) + (any_spec(),) * 4,
        scratch_shapes=[
            vm((4, width, width), BF),
        ] + [vm((rows, width), BF)] * 6 + [
            vm((rows, width), F32),
            vm((HEADS, rows, rows), F32),
            vm((planes, nrouter + 16, share), BF),
            vm((rows, rows), F32),
            vm((chips, padded, width), BF),
            vm((chips, padded, width), BF),
            vm((chips, 1, 128), F32),
            vm((4, share, width), F32),
            vm((2, share, ff), F32),
            vm((2, oshare, width), F32),
            vm((2, share, ff), BF),
            vm((2, oshare, width), BF),
            dma((8,)),
            dma((planes - 1,)), dma((planes - 1,)), dma((planes - 1,)), dma((planes - 1,)),
            dma((planes - 1, 7)), dma((planes - 1, 7)),
            dma((2, 2, 2)), dma((planes, 2)), dma((planes, 2)), dma((planes, 2)),
            dma((3, chips)), dma((3, chips)), dma((4,)), dma((8,)), dma((8,)), dma((7,)), dma((planes - 1,)),
        ],
        compiler_params=pltpu.CompilerParams(
            collective_id=0, has_side_effects=True, vmem_limit_bytes=VMEM_LIMIT
        ),
        name="front",
    )(tokens, cot, segment_ids, routes.T, router.T, *[norm.reshape(1, share) for norm in norms],
      wq, wk, wv, wo, fi, fo, ni, no)


GELU_SCALE = 0.7978845608028654
GELU_CUBE = 0.044715


def rear_kernel(planes, experts, padded, pieces, blocks, ga_groups, nrouter,
                far_x, far_do, gate, *refs):
    back_in, refs = refs[:11], refs[11:]
    (win, wout, ga,
                block_out, grad_tokens, fb, osmall, wi, wo, yland, dxland,
                x, do, tokens, cot, aux, act_two, q, k, v, resid, probs, wd, pk,
                hwi, hwo, dy, hid, dpre, dxsend, dgsend, dgland, ysend, landed_rows,
                gd, dsend, dres, gsum, szb, rzb, rup,
                sms, smr, small, ri, ro,
                ls, ts, tr, tl, gl,
                es, er, hs, hr, ys, yr, yl, sd, rd, us, ur, zs, zr, gs, gr, ms, mr, lb) = refs
    back_held = (tokens, cot, aux, act_two, q, k, v, resid, probs, wd, pk)
    back_loads = [
        pltpu.make_async_copy(src, dst, lb.at[n]) for n, (src, dst) in enumerate(zip(back_in, back_held))
    ]
    at = Place(planes, experts)
    z, i, core = at.z, at.i, at.core
    chips = at.chips
    per_plane = experts // 2
    rows, width = tokens.shape
    pairs = width // 128
    spot = lax.rem(i, 8)
    base = i - spot
    upper = rup.shape[0] if experts > 8 else 0
    ga_rows = 8 * rows // ga_groups
    datt, dq, dk, dv = [dpre.at[pl.ds(0, rows), pl.ds(n * width, width)] for n in range(4)]
    chunk = per_plane * padded // pieces
    batch = per_plane // pieces
    ff = hwi.shape[1]
    wide = ff // blocks
    load_i = pltpu.make_async_copy(win, hwi, ls.at[0])
    load_o = pltpu.make_async_copy(wout, hwo, ls.at[1])
    load_x = [pltpu.make_async_copy(far_x, x, ls.at[2]), pltpu.make_async_copy(far_do, do, ls.at[3])]
    for copy in load_x + [load_i, load_o]:
        copy.start()
    met = greet(at)
    diagonal = lax.broadcasted_iota(jnp.int32, (padded, 128), 1) == lax.broadcasted_iota(jnp.int32, (padded, 128), 0)
    for copy in load_x + [load_i]:
        copy.wait()

    def copies(plane, n):
        target = plane * per_plane + n
        there = 2 * n + core
        rows_in = dxland.at[pl.ds(pl.multiple_of(at.me * padded, 8), padded), :]
        return [
            send_to(dxsend.at[target], rows_in, ts.at[0, target], tr.at[0, at.me], plane, there),
            send_to(dgsend.at[target], dgland.at[at.me], ts.at[1, target], tr.at[1, at.me], plane, there),
        ]

    def own_copies():
        rows_in = dxland.at[pl.ds(pl.multiple_of(at.me * padded, 8), padded), :]
        return [
            pltpu.make_async_copy(dxsend.at[at.me], rows_in, tl.at[0]),
            pltpu.make_async_copy(dgsend.at[at.me], dgland.at[at.me], tl.at[1]),
        ]

    def work(plane, piece, opening=None):
        first = plane * per_plane + piece * batch
        span = pl.ds(pl.multiple_of((plane * pieces + piece) * chunk, 16), chunk)
        x_c = x[span, :]
        do_c = do[span, :].astype(F32)
        column = jnp.concatenate(
            [
                jnp.sum(jnp.where(diagonal, gate[first + n], 0.0), axis=1, keepdims=True)
                for n in range(batch)
            ],
            axis=0,
        )
        dy_c = (do_c * column).astype(BF)
        dy[span, :] = dy_c
        y_sum = jnp.zeros((chunk, width), F32)
        dx_sum = jnp.zeros((chunk, width), F32)
        for b in range(blocks):
            cols = slice(b * wide, (b + 1) * wide)
            u = dot(x_c, hwi[:, cols], NN)
            if b == 0 and opening is not None:
                @pl.when(opening)
                def _():
                    load_o.wait()
                    for copy in back_loads:
                        copy.start()
            dz = dot(dy_c, hwo[cols, :], NT)
            square = u * u
            bent = jnp.tanh(GELU_SCALE * (u + GELU_CUBE * (square * u)))
            cdf = 0.5 * (1.0 + bent)
            slope = cdf + (0.5 * GELU_SCALE) * u * (1.0 - bent * bent) * (1.0 + 3.0 * GELU_CUBE * square)
            hidden = (u * cdf).astype(BF)
            d_pre = (dz * slope).astype(BF)
            hid[span, cols] = hidden
            dpre[span, cols] = d_pre
            y_sum += dot(hidden, hwo[cols, :], NN)
            dx_sum += dot(d_pre, hwi[:, cols], NT)
        y_low = y_sum.astype(BF)
        d_gate = jnp.sum(y_low.astype(F32) * do_c, axis=1, keepdims=True)
        for n in range(batch):
            part = slice(n * padded, (n + 1) * padded)
            source = first + n
            ysend[source] = y_sum[part].astype(BF)
            dxsend[source] = dx_sum[part].astype(BF)
            dgsend[source] = jnp.sum(jnp.where(diagonal, d_gate[part], 0.0), axis=0, keepdims=True)

    def far_plane(turn):
        half = 1 - 2 * lax.rem(z, 2)
        other = lax.rem(z + 2, planes)
        return jnp.where(turn == 0, other, jnp.where(turn == 1, planes - 1 - z, z + half))

    def remote_turn(turn, carry):
        plane = far_plane(lax.div(turn, pieces))
        piece = lax.rem(turn, pieces)
        work(plane, piece, turn == 0)
        pl.when(turn == 0)(met)
        for n in range(batch):
            for copy in copies(plane, piece * batch + n):
                copy.start()
        return carry

    lax.fori_loop(0, (planes - 1) * pieces, remote_turn, 0)
    for piece in range(pieces):
        work(z, piece)
    for copy in own_copies():
        copy.start()
    for n in range(per_plane):
        for copy in copies(z, n):
            pl.when(at.chip != n)(copy.start)

    def landing(source):
        return yland.at[pl.ds(pl.multiple_of(source * padded, 8), padded), :]

    def y_copy(step):
        target = lax.rem(at.me + step, chips)
        zt, it = lax.div(target, per_plane), 2 * lax.rem(target, per_plane) + core
        return send_to(ysend.at[target], landing(at.me), ys.at[step], yr.at[step], zt, it)

    def y_start(step, carry):
        y_copy(step).start()
        return carry

    y_own = pltpu.make_async_copy(ysend.at[at.me], landing(at.me), yl.at[0])
    y_own.start()
    lax.fori_loop(1, chips, y_start, 0)

    ce = z - 1
    host = jnp.logical_and(z >= 1, z <= 2)
    half_i, half_o = width // planes // 2, ff // planes // 2

    def part(source, size, p, c):
        return source.at[pl.ds(pl.multiple_of((2 * p + c) * size, 16), size), :]

    pair = [
        [
            send_to(part(src, size, p, 1 - core), land.at[p], es.at[which, p], er.at[which, p], z, at.sib)
            for p in range(planes)
        ]
        for which, (src, land, size) in enumerate(((hwi, ri, half_i), (hwo, ro, half_o)))
    ]
    fetch_ga = [
        pltpu.make_async_copy(
            ga.at[pl.ds(g * ga_rows, ga_rows), :],
            hid.at[pl.ds(0, ga_rows), pl.ds(g * width, width)],
            gl.at[g],
        )
        for g in range(ga_groups)
    ]

    @pl.when(host)
    def _():
        turned = x[...].T
        for b in range(blocks):
            cols = slice(b * wide, (b + 1) * wide)
            hwi[:, cols] = dot(turned, dpre[:, cols], NN, BF)
        for copy in pair[0]:
            copy.start()
        for b in range(blocks):
            cols = slice(b * wide, (b + 1) * wide)
            hwo[cols, :] = dot(hid[:, cols], dy[...], TN, BF)
        for copy in pair[1]:
            copy.start()

    for copy in fetch_ga:
        copy.start()

    owner = 2 * at.chip + ce
    shipments = []

    def ship(p, which):
        src, dst = (part(hwi, half_i, p, core), wi.at[core]) if which == 0 else (part(hwo, half_o, p, core), wo.at[core])
        near = jnp.logical_and(z == p, core == ce)
        far_copy = send_to(src, dst, hs.at[p, which], hr.at[core, which], p, owner)
        near_copy = pltpu.make_async_copy(src, dst, hr.at[core, which])
        is_far = jnp.logical_and(host, jnp.logical_not(near))
        pl.when(is_far)(far_copy.start)
        pl.when(jnp.logical_and(host, near))(near_copy.start)
        shipments.append((is_far, far_copy))

    def add_pair(which, mine, theirs, size, chunk):
        @pl.when(host)
        def _():
            for copy in pair[which]:
                copy.wait_recv()

            def add(n, carry):
                low = pl.ds(pl.multiple_of(n * chunk, chunk), chunk)
                for p in range(planes):
                    here = pl.ds(pl.multiple_of((2 * p + core) * size + n * chunk, 16), chunk)
                    mine[here, :] = (
                        mine[here, :].astype(F32) + theirs[p, low, :].astype(F32)
                    ).astype(BF)
                return carry

            lax.fori_loop(0, size // chunk, add, 0)

    add_pair(0, hwi, ri, half_i, 16)
    for p in range(planes):
        ship(p, 0)
    add_pair(1, hwo, ro, half_o, 64)
    for p in (0, 3):
        ship(p, 1)

    def dx_wait(step, carry):
        source = lax.rem(at.me + step, at.chips)
        rows_in = dxland.at[pl.ds(pl.multiple_of(source * padded, 8), padded), :]
        send_to(dxsend.at[source], rows_in, ts.at[0, source], tr.at[0, source], z, i).wait_recv()
        send_to(dgsend.at[source], dgland.at[source], ts.at[1, source], tr.at[1, source], z, i).wait_recv()
        return carry

    for copy in own_copies():
        copy.wait()
    lax.fori_loop(1, at.chips, dx_wait, 0)
    fetch_dx = pltpu.make_async_copy(dxland, landed_rows, yl.at[1])
    fetch_dx.start()
    fetch_dx.wait()

    for copy in back_loads:
        copy.wait()

    aux_v = aux[...]
    gates = [aux_v[:, 0:1], aux_v[:, 1:2]]
    place = slot_places([aux_v[:, 2:3], aux_v[:, 3:4]], chips * padded)
    d_out = cot[...].astype(F32)
    d_act = dot(place[0] + place[1], landed_rows[...], NN)
    table = dgland[:, 0, :]
    d_gate = slot_values(aux_v, table, padded, chips)
    mean_gate = gates[0] * d_gate[0] + gates[1] * d_gate[1]
    route_iota = lax.broadcasted_iota(jnp.int32, (rows, nrouter), 1).astype(F32)
    d_logits = jnp.zeros((rows, nrouter), F32)
    for n in range(2):
        chosen = route_iota == aux_v[:, 4 + n:5 + n]
        d_logits = d_logits + jnp.where(chosen, gates[n] * (d_gate[n] - mean_gate), 0.0)
    d_logits = d_logits.astype(BF)
    small[0:nrouter, :] = dot(d_logits, act_two[...], TN)
    d_act = d_act + dot(d_logits, pk[0:nrouter, :], NN)
    gain_one = pk[nrouter:nrouter + 1, :].astype(F32)
    gain_two = pk[nrouter + 2:nrouter + 3, :].astype(F32)
    d_norm, g_gain, g_bias = norm_back(resid[...], gain_two, d_act)
    small[nrouter:nrouter + 16, :] = jnp.zeros((16, width), F32)
    small[nrouter + 2:nrouter + 3, :] = g_gain
    small[nrouter + 3:nrouter + 4, :] = g_bias
    d_res = d_out + d_norm
    dres[...] = d_res
    d_branch = d_res.astype(BF)
    half = width // 2
    for n in range(2):
        dsend[pairs + n] = d_branch[:, n * half:(n + 1) * half]
    datt[...] = dot(d_branch, wd[3], NT, BF)

    def d_copy(target):
        return send_to(dsend.at[target], gd.at[spot], sd.at[target], rd.at[spot], z, base + target)

    def d_near(target):
        return pltpu.make_async_copy(dsend.at[target], gd.at[spot], rd.at[spot])

    def d_start(target):
        far = spot != target
        pl.when(far)(d_copy(target).start)
        pl.when(jnp.logical_not(far))(d_near(target).start)

    for n in range(2):
        d_start(pairs + n)

    lane = lax.broadcasted_iota(jnp.int32, (rows, 128), 1)
    masks = [(lane < HEAD).astype(F32).astype(BF), (lane >= HEAD).astype(F32).astype(BF)]
    score_scale = HEAD ** (-0.5)

    def head_pair(n, carry):
        cols = pl.ds(pl.multiple_of(n * 128, 128), 128)
        q2, k2, v2, da2 = q[:, cols], k[:, cols], v[:, cols], datt[:, cols]
        sums = [jnp.zeros((rows, 128), F32) for _ in range(3)]
        for side in range(2):
            mask = masks[side]
            da = da2 * mask
            p = probs[2 * n + side]
            dpb = dot(da, v2, NT)
            delta = jnp.sum(p * dpb, axis=-1, keepdims=True)
            ds = (p * (dpb - delta)).astype(BF)
            sums[0] += dot(ds, k2 * mask, NN)
            sums[1] += dot(ds, q2 * mask, TN)
            sums[2] += dot(p.astype(BF), da, TN)
        low = [(sums[0] * score_scale).astype(BF), (sums[1] * score_scale).astype(BF), sums[2].astype(BF)]
        for m, (value, full) in enumerate(zip(low, (dq, dk, dv))):
            dsend[n, :, m * 128:(m + 1) * 128] = value
            full[:, cols] = value
        d_start(n)
        return carry

    lax.fori_loop(0, pairs, head_pair, 0)

    d_one = dot(dq[...], wd[0], NT) + dot(dk[...], wd[1], NT) + dot(dv[...], wd[2], NT)
    d_norm, g_gain, g_bias = norm_back(tokens[...].astype(F32), gain_one, d_one)
    grad_tokens[...] = (dres[...] + d_norm).astype(BF)
    small[nrouter:nrouter + 1, :] = g_gain
    small[nrouter + 1:nrouter + 2, :] = g_bias

    hops = [at.sib, at.xn, at.yn]
    for n in range(upper):
        bit = 8 << n
        hops.append(i + bit - 2 * bit * lax.rem(lax.div(i, bit), 2))
    moves = [(z, t) for t in hops]
    for n in range(planes.bit_length() - 1):
        bit = 1 << n
        moves.append((z + bit - 2 * bit * lax.rem(lax.div(z, bit), 2), i))
    small_copies = []

    def small_start(n):
        if n >= 2:
            small_copies[n - 2].wait_send()
        sms[n % 2] = small[...]
        copy = send_to(sms.at[n % 2], smr.at[n], ms.at[n], mr.at[n], moves[n][0], moves[n][1])
        copy.start()
        small_copies.append(copy)

    def small_step(n):
        small_copies[n].wait_recv()
        small[...] = small[...] + smr[n]
        if n + 1 < len(moves):
            small_start(n + 1)

    small_start(0)

    small_step(0)

    def d_wait(source, carry):
        send_to(gd.at[source], gd.at[source], sd.at[source], rd.at[source], z, i).wait_recv()
        return carry

    lax.fori_loop(0, 8, d_wait, 0)
    columns = gd.shape[2]
    total = jnp.zeros((width, columns), F32)
    sources = ga_rows // rows
    for g in range(ga_groups):
        fetch_ga[g].wait()
        total += dot(
            hid[0:ga_rows, g * width:(g + 1) * width],
            gd[g * sources:(g + 1) * sources].reshape(ga_rows, columns), TN,
        )
    gsum[...] = total.reshape(planes, width // planes, columns)
    small_step(1)
    tail = []
    for n in range(upper):
        szb[...] = gsum[...].astype(BF)
        copy = send_to(szb, rup.at[n], us.at[n], ur.at[n], z, hops[3 + n])
        copy.start()
        copy.wait_recv()
        gsum[...] = szb[...].astype(F32) + rup[n].astype(F32)
        copy.wait_send()
    szb[...] = gsum[...].astype(BF)
    partner = z + 1 - 2 * lax.rem(z, 2)
    others = 2 - 2 * lax.div(z, 2)
    outer = jnp.logical_not(host)
    copy = send_to(szb.at[partner], rzb.at[0], zs.at[0], zr.at[0], partner, i)
    copy.start()
    tail.append(copy)
    inward = [
        send_to(szb.at[others + n], rzb.at[2 + n], zs.at[1 + n], zr.at[2 + n], partner, i) for n in range(2)
    ]
    across = [
        send_to(szb.at[others + n], rzb.at[1], zs.at[1 + n], zr.at[1], others + n, i) for n in range(2)
    ]

    @pl.when(outer)
    def _():
        for copy in inward:
            copy.start()

    @pl.when(host)
    def _():
        for n in range(2):
            inward[n].wait_recv()
            szb[others + n] = (gsum[others + n] + rzb[2 + n].astype(F32)).astype(BF)
            across[n].start()

    shipments += [(outer, copy) for copy in inward] + [(host, copy) for copy in across]
    for p in (1, 2):
        ship(p, 1)
    small_step(2)

    def y_finish(step, carry):
        source = lax.rem(at.me + chips - step, chips)
        send_to(landing(source), landing(source), ys.at[step], yr.at[step], z, i).wait_recv()
        y_copy(step).wait_send()
        return carry

    y_own.wait()
    lax.fori_loop(1, chips, y_finish, 0)
    fetch = pltpu.make_async_copy(yland, landed_rows, yl.at[1])
    fetch.start()
    fetch.wait()
    y_all = landed_rows[...]
    mixed = gates[0] * dot(place[0], y_all, NN) + gates[1] * dot(place[1], y_all, NN)
    block_out[...] = (resid[...] + mixed).astype(BF)

    fin = gsum[z]
    for n in range(2):
        send_to(rzb.at[n], rzb.at[n], zs.at[n], zr.at[n], z, i).wait_recv()
        fin = fin + rzb[n].astype(F32)
    fb[spot] = fin.astype(BF)
    px, py = spot + 2 - 4 * at.xb, spot + 4 - 8 * at.yb
    pd = px + 4 - 8 * at.yb
    flip = 1 - 2 * core

    def pass_on(where, step, target):
        copy = send_to(fb.at[where], fb.at[where], gs.at[step], gr.at[step], z, target)
        copy.start()
        tail.append(copy)

    def landed(where, step):
        send_to(fb.at[where], fb.at[where], gs.at[step], gr.at[step], z, i).wait_recv()

    pass_on(spot, 0, at.xn)
    pass_on(spot, 1, at.yn)
    pass_on(spot, 2, at.sib)
    small_step(3)
    landed(px, 0)
    landed(py, 1)
    pass_on(px + core * (py - px), 3, at.yn + core * (at.xn - at.yn))
    pass_on(px, 4, at.sib)
    pass_on(py, 5, at.sib)
    for n in range(4, len(moves)):
        small_step(n)
    osmall[...] = small[...]
    landed(pd, 3)
    pass_on(pd, 6, at.sib)
    for h in range(2):
        send_to(wi.at[h], wi.at[h], hs.at[0, 0], hr.at[h, 0], z, i).wait_recv()
        send_to(wo.at[h], wo.at[h], hs.at[0, 1], hr.at[h, 1], z, i).wait_recv()
    landed(spot + flip, 2)
    landed(px + flip, 4)
    landed(py + flip, 5)
    landed(pd + flip, 6)
    for copy in tail + small_copies[-2:]:
        copy.wait_send()
    def d_sent(target, carry):
        pl.when(spot != target)(d_copy(target).wait_send)
        return carry

    lax.fori_loop(0, 8, d_sent, 0)

    @pl.when(host)
    def _():
        for copy in pair[0] + pair[1]:
            copy.wait_send()

    for is_far, copy in shipments:
        pl.when(is_far)(copy.wait_send)

    def dx_sent(step, carry):
        target = lax.rem(at.me + step, at.chips)
        for copy in copies(lax.div(target, per_plane), lax.rem(target, per_plane)):
            copy.wait_send()
        return carry

    lax.fori_loop(1, at.chips, dx_sent, 0)


def rear(planes, experts, nrouter, x, do, gate, back_in, win, wout, ga):
    rows, width = back_in[0].shape
    chips, padded, _ = x.shape
    slots = chips * padded
    ff = win.shape[1]
    pieces, blocks = (1, 4) if experts <= 8 else (2, 8)
    ga_groups = ff // width
    share, fshare, half = width // planes, ff // planes, width // 2
    upper = max(experts.bit_length() - 4, 1)
    nbits = experts.bit_length() - 1 + planes.bit_length() - 1
    dma = pltpu.SemaphoreType.DMA
    vm = pltpu.VMEM
    sds = jax.ShapeDtypeStruct
    return pl.pallas_call(
        functools.partial(rear_kernel, planes, experts, padded, pieces, blocks, ga_groups, nrouter),
        out_shape=(
            sds((rows, width), BF),
            sds((rows, width), BF),
            sds((8, share, half), BF),
            sds((nrouter + 16, width), F32),
            sds((2, share // 2, ff), BF),
            sds((2, fshare // 2, width), BF),
            sds((slots, width), BF),
            sds((slots, width), BF),
        ),
        in_specs=[any_spec()] * 2 + [vmem_spec()] + [any_spec()] * 14,
        out_specs=(vmem_spec(),) * 4 + (any_spec(),) * 4,
        scratch_shapes=[vm((slots, width), BF)] * 2 + [vm(a.shape, a.dtype) for a in back_in] + [
            vm((width, ff), BF),
            vm((ff, width), BF),
            vm((slots, width), BF),
            vm((slots, ff), BF),
            vm((slots, ff), BF),
            vm((chips, padded, width), BF),
            vm((chips, 1, 128), F32),
            vm((chips, 1, 128), F32),
            vm((chips, padded, width), BF),
            vm((slots, width), BF),
            vm((8, rows, half), BF),
            vm((8, rows, half), BF),
            vm((rows, width), F32),
            vm((planes, share, half), F32),
            vm((planes, share, half), BF),
            vm((4, share, half), BF),
            vm((upper, planes, share, half) if experts > 8 else (1, 8, 128), BF),
            vm((2, nrouter + 16, width), F32),
            vm((nbits, nrouter + 16, width), F32),
            vm((nrouter + 16, width), F32),
            vm((planes, share // 2, ff), BF),
            vm((planes, fshare // 2, width), BF),
            dma((4,)), dma((2, chips)), dma((2, chips)), dma((2,)), dma((ga_groups,)),
            dma((2, planes)), dma((2, planes)),
            dma((planes, 2)), dma((2, 2)),
            dma((chips,)), dma((chips,)), dma((2,)),
            dma((8,)), dma((8,)),
            dma((upper,)), dma((upper,)),
            dma((3,)), dma((4,)),
            dma((7,)), dma((7,)), dma((nbits,)), dma((nbits,)), dma((11,)),
        ],
        compiler_params=pltpu.CompilerParams(
            collective_id=2, has_side_effects=True, vmem_limit_bytes=REAR_LIMIT
        ),
        name="rear",
    )(x.reshape(slots, width), do.reshape(slots, width), gate, *back_in, win, wout, ga.reshape(8 * rows, width))


def finish_kernel(planes, nrouter, *refs):
    given, refs = refs[:6], refs[6:]
    (ob, ot, o0, o1, o2, o3, og, v0, v1, v2, v3, ogi, ogo,
     s0, s1, s2, s3, sg, sv, si, so, block_out, grad_tokens, fb, small, wi, wo, sem, lsem) = refs
    held = (block_out, grad_tokens, fb, small, wi, wo)
    loads = [pltpu.make_async_copy(src, dst, lsem.at[n]) for n, (src, dst) in enumerate(zip(given, held))]
    for n in (4, 5, 2, 0, 1, 3):
        loads[n].start()
    z = lax.axis_index("dp")
    share = s0.shape[0]
    pairs = s0.shape[1] // 128
    half = s0.shape[1] // 2
    copies = []

    def write(source, target):
        copy = pltpu.make_async_copy(source, target, sem.at[len(copies)])
        copy.start()
        copies.append(copy)

    for n, (wide, low, out) in ((4, (si, wi, ogi)), (5, (so, wo, ogo))):
        loads[n].wait()
        chunk = low.shape[1]
        for h in range(2):
            wide[h * chunk:(h + 1) * chunk, :] = low[h].astype(F32)
            write(wide.at[pl.ds(h * chunk, chunk), :], out.at[pl.ds(h * chunk, chunk), :])
    for n, source, out in ((0, block_out, ob), (1, grad_tokens, ot)):
        loads[n].wait()
        write(source, out)
    loads[2].wait()
    for m, (stage, out) in enumerate(((s0, o0), (s1, o1), (s2, o2))):
        for n in range(pairs):
            stage[:, n * 128:(n + 1) * 128] = fb[n, :, m * 128:(m + 1) * 128].astype(F32)
        write(stage, out)
    for n in range(2):
        s3[:, n * half:(n + 1) * half] = fb[pairs + n].astype(F32)
    write(s3, o3)
    loads[3].wait()
    mine = small[:, 0:share]
    for p in range(1, planes):
        mine = jnp.where(z == p, small[:, p * share:(p + 1) * share], mine)
    sg[...] = mine[0:nrouter]
    write(sg, og)
    for n, out in enumerate((v0, v1, v2, v3)):
        sv[n] = mine[nrouter + n:nrouter + n + 1]
        write(sv.at[n], out)
    for copy in copies:
        copy.wait()


def finish(planes, nrouter, block_out, grad_tokens, fb, small, wi, wo):
    rows, width = block_out.shape
    _, share, half = fb.shape
    ff = wi.shape[2]
    fshare = 2 * wo.shape[1]
    vm = pltpu.VMEM
    sds = jax.ShapeDtypeStruct
    dense = ((share, width),) * 4 + ((nrouter, share),)
    wide = ((share, ff), (fshare, width))
    results = dense + ((1, share),) * 4 + wide
    stages = dense + ((4, 1, share),) + wide
    return pl.pallas_call(
        functools.partial(finish_kernel, planes, nrouter),
        out_shape=(sds((rows, width), BF),) * 2 + tuple(sds(shape, F32) for shape in results),
        in_specs=[any_spec()] * 6,
        out_specs=(any_spec(),) * 13,
        scratch_shapes=[vm(shape, F32) for shape in stages]
        + [vm(a.shape, a.dtype) for a in (block_out, grad_tokens, fb, small, wi, wo)]
        + [pltpu.SemaphoreType.DMA((16,)), pltpu.SemaphoreType.DMA((6,))],
        compiler_params=pltpu.CompilerParams(vmem_limit_bytes=VMEM_LIMIT),
        name="finish",
    )(block_out, grad_tokens, fb, small, wi, wo)


def shards(planes, experts, tokens, segment_ids, routes, ln1_gain, ln1_bias, ln2_gain, ln2_bias,
           w_query, w_key, w_value, w_output, w_router, frozen_in, frozen_out, new_in, new_out,
           cotangent):
    rows, width = tokens.shape
    expert_count = w_router.shape[1]
    capacity = 5 * rows // (2 * expert_count)
    padded = -(-capacity // 8) * 8
    (wd, pk, win, wout, act_two, q, k, v, resid, probs, aux, ga, x_recv, do_recv, g_recv) = front(
        planes, experts, capacity, padded, expert_count, tokens, cotangent, segment_ids, routes,
        w_router, (ln1_gain, ln1_bias, ln2_gain, ln2_bias),
        w_query, w_key, w_value, w_output, frozen_in, frozen_out, new_in, new_out,
    )
    block_out, grad_tokens, dense, small, low_in, low_out, _, _ = rear(
        planes, experts, expert_count, x_recv, do_recv, g_recv,
        (tokens, cotangent, aux, act_two, q, k, v, resid, probs, wd, pk), win, wout, ga,
    )
    block_out, grad_tokens, oq, ok, ov, ow, router, *norms, ogi, ogo = finish(
        planes, expert_count, block_out, grad_tokens, dense, small, low_in, low_out
    )
    norms = [norm.reshape(width // planes) for norm in norms]
    return (
        block_out, grad_tokens, oq, ok, ov, ow, router.T,
        norms[0], norms[1], norms[2], norms[3], ogi[None], ogo[None],
    )


def solution(mesh):
    rows = P(("dp", "expert"), None)
    in_specs = (rows, rows, rows) + (P("dp"),) * 4 + (P("dp", None),) * 5
    in_specs += (P("expert", "dp", None),) * 4 + (rows,)
    out_specs = (rows, rows) + (P("dp", None),) * 5 + (P("dp"),) * 4
    out_specs += (P("expert", "dp", None),) * 2
    body = functools.partial(shards, mesh.shape["dp"], mesh.shape["expert"])
    return jax.shard_map(body, mesh=mesh, in_specs=in_specs, out_specs=out_specs, check_vma=False)
```
